32 devices in a mesh: grp: 2 (over y), pan: 4 (over z), en: 4 (over x, core).
Axes of the slice: x: 2, y: 2, z: 4, core: 2. Of those that a mesh axis runs over, the one named last changes fastest.
Arguments:
- retarded: float32 [2, 8, 2048, 2048], P(None, ('grp', 'en'), 'pan'), parts along dimension 1, may hold values from -0.75 to 0.75
- contact: float32 [2, 8, 2048, 128], P(None, ('grp', 'en'), 'pan'), parts along dimension 1, may hold values from -6 to 6
- atom_kind: int32 [256], replicated, may hold values from 0 to 3
- coupling: float32 [4, 3], replicated, may hold values from 0.2 to 1
- shifts: int32 [3], replicated, may hold values from 1 to 3, as said below
Outputs:
- lesser_diag: float32 [2, 8, 2048, 128], P(None, ('grp', 'en'), 'pan'), parts along dimension 1
- lesser_upper: float32 [2, 8, 2048, 128], P(None, ('grp', 'en'), 'pan'), parts along dimension 1
- sigma_next: float32 [2, 8, 2048, 128], P(None, ('grp', 'en'), 'pan'), parts along dimension 1
The draws below stay inside these ranges and needn't reach their ends.
There are 2 independent parts, one for each index of `grp`. The reference program is written for one: setup_inputs(seed, part) draws one part's arguments, and reference() takes and returns one part's arrays. A program takes and returns all parts, laid end to end along the dimension named above; an argument that names none is the same for every part. Nothing has to cross between parts.
Inputs may be any that keep to these rules, and one draw needn't show every extreme that they name: `shifts`: the three entries are distinct: one is 1, one is 3, and one lies strictly between them.
All inputs are finite; a program needn't handle non-finite values.
Results may differ from the reference program's by a relative error of at most 0.0001.
Values sent between devices are 32-bit elements; how exact they have to be, the bound alone decides.
No kernel may reach another device: no remote copies, remote signals or barrier semaphores. Data moves between devices by JAX's collectives and lax.ppermute only.
A program may use at most 128 MiB of HBM per device.

```python
import math
import jax
import jax.numpy as jnp
from jax import lax

N = 2048
B = 128
ORB = 8
KINDS = 4
MODES = 3
ITERS = 2
ENERGIES = 4
ATOMS = 256


def draw_shifts(key, part):
    order_key = jax.random.fold_in(key, 71)
    middle_key = jax.random.fold_in(key, 72)
    middle = jax.random.randint(middle_key, (), 2, ENERGIES - 1, dtype=jnp.int32)
    values = jnp.stack([jnp.array(1, jnp.int32), middle, jnp.array(ENERGIES - 1, jnp.int32)])
    order = jax.random.permutation(order_key, 3)
    return values[order].astype(jnp.int32)


def place_ends(result, own_key, smallest, largest):
    spot = [jax.random.randint(jax.random.fold_in(own_key, axis), (), 0, length) for axis, length in enumerate(result.shape)]
    main_axis = result.shape.index(max(result.shape))
    next_to = spot[:main_axis] + [(spot[main_axis] + 1) % result.shape[main_axis]] + spot[main_axis + 1:]
    return result.at[tuple(spot)].set(smallest).at[tuple(next_to)].set(largest)


def steps_of(own_key, shape, cuts, low, high):
    gain, own = 1.0, jax.random.fold_in(own_key, 6)
    for position, blocks in cuts:
        draws = jnp.exp(jax.random.uniform(jax.random.fold_in(own, position), (blocks,), jnp.float32, low / len(cuts), high / len(cuts)))
        gain = gain * jnp.repeat(draws, shape[position] // blocks).reshape([-1 if axis == position else 1 for axis in range(len(shape))])
    return gain


def normal_values(rng, shape, width, limit, shards=(), kind=jnp.bfloat16):
    result = width * jax.random.normal(rng, shape, jnp.float32)
    if shards:
        result = result * steps_of(rng, shape, shards, -0.22, 0.18)
    return jnp.clip(result, -limit, limit).astype(kind)


def setup_inputs(seed: int = 0, part: int = 0) -> dict:
    seeds = jax.random.split(jax.random.key(seed), 6)
    part_keys = jax.random.split(jax.random.fold_in(seeds[5], part), 6)
    return {
        "retarded": normal_values(part_keys[0], (2, ENERGIES, N, N), 0.125, 0.75, ((1, 4), (2, 4)), jnp.float32),
        "contact": normal_values(part_keys[1], (2, ENERGIES, N, B), 1.0, 6.0, ((1, 4), (2, 4)), jnp.float32),
        "atom_kind": place_ends(jax.random.randint(seeds[2], (ATOMS,), 0, KINDS), jax.random.fold_in(seeds[2], 1), 0, KINDS - 1).astype(jnp.int32),
        "coupling": jnp.clip(jnp.exp(jax.random.uniform(seeds[3], (KINDS, MODES), jnp.float32, math.log(0.2), math.log(1.0))), 0.2, 1.0),
        "shifts": draw_shifts(jax.random.fold_in(seeds[5], 71), part),
    }


precise = lax.Precision.HIGHEST

def mix_plain(blocks):
    return jnp.stack([jnp.stack([blocks[0], blocks[1]]), jnp.stack([-blocks[1], blocks[0]])])

def mix_conj(blocks):
    return jnp.stack([jnp.stack([blocks[0], -blocks[1]]), jnp.stack([blocks[1], blocks[0]])])

def blocked(green_cols, blocks):
    return jnp.einsum('a...rkq,ac...kqj->c...rkj', green_cols, mix_plain(blocks), precision=precise)

def adjoint_product(left_side, right_mixed):
    return jnp.einsum('a...rn,ac...sn->c...rs', left_side, right_mixed, precision=precise)

def coupling_factor(atom_kind, coupling):
    onehot = (atom_kind[:, None] == jnp.arange(coupling.shape[0], dtype=jnp.int32)[None, :]).astype(jnp.float32)
    per_atom = jnp.dot(onehot, coupling, precision=precise, preferred_element_type=jnp.float32)
    per_orbital = jnp.repeat(per_atom, ORB, axis=0)
    per_column = jnp.repeat(per_orbital.reshape(N // B, B, coupling.shape[1]), B, axis=0)
    return per_orbital[:, None, :] * per_column

def energy_table(shifts, levels):
    energy = jnp.arange(levels, dtype=jnp.int32)
    target = energy[None, :, None]
    source = energy[None, None, :]
    offsets = shifts[:, None, None]
    return ((source == target + offsets) | (source == target - offsets)).astype(jnp.float32)

def phonon(lesser_diag, shift_table, factor):
    shifted = jnp.einsum('mef,cfrb->mcerb', shift_table, lesser_diag, precision=precise)
    return jnp.einsum('mcerb,rbm->cerb', shifted, factor, precision=precise)

def lesser(energy_pair):
    retard_one, sigma_one = energy_pair
    blocks = N // B
    block_scale = 1.0 / math.sqrt(B)
    product = blocked(retard_one.reshape(2, N, blocks, B), sigma_one.reshape(2, blocks, B, B)).reshape(2, N, N)
    prod_rows = product.reshape(2, blocks, B, N)
    retard_mixed = mix_conj(retard_one.reshape(2, blocks, B, N))
    diagonal = adjoint_product(prod_rows, retard_mixed) * block_scale
    upper_part = adjoint_product(prod_rows[:, :-1], retard_mixed[:, :, 1:]) * block_scale
    upper_part = jnp.concatenate([upper_part, jnp.zeros((2, 1, B, B), jnp.float32)], axis=1)
    return (diagonal.reshape(2, N, B), upper_part.reshape(2, N, B))

def reference(retarded, contact, atom_kind, coupling, shifts):
    factor = coupling_factor(atom_kind, coupling)
    shift_table = energy_table(shifts, ENERGIES)
    moved_green = jnp.moveaxis(retarded, 1, 0)
    self_energy = contact
    for rounds in range(ITERS):
        diag_all, upper_all = lax.map(lesser, (moved_green, jnp.moveaxis(self_energy, 1, 0)))
        lesser_diag = jnp.moveaxis(diag_all, 0, 1)
        lesser_upper = jnp.moveaxis(upper_all, 0, 1)
        self_energy = contact + phonon(lesser_diag, shift_table, factor)
    return (lesser_diag, lesser_upper, self_energy)
```

```python
import functools
import math

import jax
import jax.numpy as jnp
from jax import lax
from jax.experimental import pallas as pl
from jax.experimental.pallas import tpu as pltpu
from jax.sharding import PartitionSpec as P

B = 128
ORB = 8
ITERS = 2

F32 = jnp.float32
BF16 = jnp.bfloat16


def shifted(x, axis, by):
    devices = lax.axis_size(axis)
    pairs = [(i, i + by) for i in range(devices) if 0 <= i + by < devices]
    return lax.ppermute(x, axis, pairs)


def swapped(x, axis, bit):
    return lax.ppermute(x, axis, [(i, i ^ bit) for i in range(lax.axis_size(axis))])


def spread(x, axis):
    pieces = [(0, x)]
    bit = lax.axis_size(axis) // 2
    while bit:
        pieces += [(far ^ bit, swapped(piece, axis, bit)) for far, piece in pieces]
        bit //= 2
    return pieces


def split(x):
    high = x.astype(BF16)
    return high, (x - high.astype(F32)).astype(BF16)


def dot(a, b):
    return jnp.dot(a, b, preferred_element_type=F32)


def dot_t(a, b):
    return lax.dot_general(a, b, (((1,), (1,)), ((), ())), preferred_element_type=F32)


def times(a, b):
    return dot(a[0], b[0]) + (dot(a[1], b[0]) + dot(a[0], b[1]))


def times_t(a, b):
    return dot_t(a[0], b[0]) + (dot_t(a[1], b[0]) + dot_t(a[0], b[1]))


def pair_rows(x):
    return tuple(
        jnp.concatenate([v, jnp.concatenate([v[:, B:], -v[:, :B]], axis=1)], axis=0) for v in x
    )


def rows_of(x, start, size):
    return tuple(v[start : start + size] for v in x)


def panel_kernel(local, steps, half, first, final, last, scale, *refs):
    refs = list(refs)
    k_ref = refs.pop(0)
    g_ref = refs.pop(0)
    s_ref = refs.pop(0)
    x_ref, y_ref = (refs.pop(0), refs.pop(0)) if final else (None, None)
    in_ref = None if first else refs.pop(0)
    if last:
        acc_ref = refs.pop()
        out_refs = refs
    else:
        (acc_ref,) = refs
    step = pl.program_id(0)
    k = k_ref[step]

    @pl.when(step == 0)
    def _():
        acc_ref[...] = jnp.zeros_like(acc_ref) if first else in_ref[...]

    green = split(jnp.concatenate([g_ref[0, 0], g_ref[1, 0]], axis=1))
    sr, si = s_ref[0, 0], s_ref[1, 0]
    sigma = split(
        jnp.concatenate(
            [jnp.concatenate([sr, si], axis=1), jnp.concatenate([-si, sr], axis=1)], axis=0
        )
    )
    product = split(times(green, sigma))
    for i in range(local):
        right = pair_rows(rows_of(product, i * B, B))
        if final and i < local - 1:
            both = times_t(rows_of(green, i * B, 2 * B), right)
            acc_ref[i] += both[:B]
            acc_ref[local + i] += both[B:]
        else:
            acc_ref[i] += times_t(rows_of(green, i * B, B), right)
    if final:

        @pl.when(k < half)
        def _():
            over = split(jnp.concatenate([x_ref[0, 0], x_ref[1, 0]], axis=1))
            right = pair_rows(rows_of(product, (local - 1) * B, B))
            acc_ref[2 * local - 1] += times_t(over, right)

        @pl.when(k >= half)
        def _():
            under = split(jnp.concatenate([y_ref[0, 0], y_ref[1, 0]], axis=1))
            right = pair_rows(split(times(under, sigma)))
            acc_ref[2 * local] += times_t(rows_of(green, 0, B), right)

    if last:

        @pl.when(step == steps - 1)
        def _():
            def put(ref, row, where):
                ref[0, 0, row * B : (row + 1) * B] = acc_ref[where, :, :B].T * scale
                ref[1, 0, row * B : (row + 1) * B] = acc_ref[where, :, B:].T * scale

            for i in range(local):
                put(out_refs[0], i, i)
                if final:
                    put(out_refs[1], i, local + i)
            if final:
                put(out_refs[2], 0, 2 * local)


def panel(green, source, piece, carry, edges, final, last, name):
    rows, columns = green.shape[2:]
    local = rows // B
    half = columns // B // 2
    ks = source * local + jnp.arange(local, dtype=jnp.int32)
    specs = [
        pl.BlockSpec((2, 1, rows, B), lambda j, k: (0, 0, 0, k[j])),
        pl.BlockSpec((2, 1, B, B), lambda j, k: (0, 0, j, 0)),
    ]
    operands = [green, piece]
    if final:
        specs += [
            pl.BlockSpec((2, 1, B, B), lambda j, k: (0, 0, 0, jnp.minimum(k[j], half - 1))),
            pl.BlockSpec((2, 1, B, B), lambda j, k: (0, 0, 0, jnp.maximum(k[j] - half, 0))),
        ]
        operands += edges
    count = 2 * local + 1 if final else local
    whole = pl.BlockSpec((count, B, 2 * B), lambda j, k: (0, 0, 0))
    if carry is not None:
        specs.append(whole)
        operands.append(carry)
    if last:
        tall = jax.ShapeDtypeStruct((2, 1, rows, B), F32)
        shapes = [tall] + ([tall, jax.ShapeDtypeStruct((2, 1, B, B), F32)] if final else [])
        out_specs = [pl.BlockSpec(s.shape, lambda j, k: (0, 0, 0, 0)) for s in shapes]
        scratch = [pltpu.VMEM((count, B, 2 * B), F32)]
    else:
        shapes = [jax.ShapeDtypeStruct((count, B, 2 * B), F32)]
        out_specs = [whole]
        scratch = []
    work = 3 * 2 * (2 * B) * (2 * B) * (rows + (2 * rows if final else rows)) * local
    out = pl.pallas_call(
        functools.partial(
            panel_kernel, local, local, half, carry is None, final, last, 1.0 / math.sqrt(B)
        ),
        grid_spec=pltpu.PrefetchScalarGridSpec(
            num_scalar_prefetch=1,
            grid=(local,),
            in_specs=specs,
            out_specs=out_specs,
            scratch_shapes=scratch,
        ),
        out_shape=shapes,
        cost_estimate=pl.CostEstimate(
            flops=work, bytes_accessed=8 * rows * B * local, transcendentals=0
        ),
        name=name,
    )(ks, *operands)
    return out if last else out[0]


def phonon_kernel(fars, modes, shift_ref, en_ref, contact_ref, col_ref, row_ref, *refs):
    out_ref = refs[-1]
    energy = en_ref[0]
    outer = [col_ref[:, m : m + 1] * row_ref[m : m + 1, :] for m in range(modes)]
    re, im = contact_ref[0, 0], contact_ref[1, 0]
    for far, ref in zip(fars, refs[:-1]):
        apart = jnp.abs((energy ^ far) - energy)
        weight = sum(
            jnp.where(apart == shift_ref[m], 1.0, 0.0).astype(F32) * outer[m] for m in range(modes)
        )
        re += weight * ref[0, 0]
        im += weight * ref[1, 0]
    out_ref[0, 0] = re
    out_ref[1, 0] = im


def phonon(shifts, energy, contact, columns, lines, pieces):
    rows = contact.shape[2]
    modes = shifts.shape[0]
    block = pl.BlockSpec((2, 1, B, B), lambda i, *_: (0, 0, i, 0))
    return pl.pallas_call(
        functools.partial(phonon_kernel, [far for far, _ in pieces], modes),
        grid_spec=pltpu.PrefetchScalarGridSpec(
            num_scalar_prefetch=2,
            grid=(rows // B,),
            in_specs=[
                block,
                pl.BlockSpec((B, modes), lambda i, *_: (i, 0)),
                pl.BlockSpec((modes, B), lambda i, *_: (0, i)),
            ]
            + [block] * len(pieces),
            out_specs=block,
        ),
        out_shape=jax.ShapeDtypeStruct(contact.shape, F32),
        cost_estimate=pl.CostEstimate(
            flops=rows * B * 20, bytes_accessed=8 * rows * B * 5, transcendentals=0
        ),
        name="phonon",
    )(shifts, energy, contact, columns, lines, *[piece for _, piece in pieces])


def body(retarded, contact, atom_kind, coupling, shifts):
    rows, columns = retarded.shape[2:]
    pan = lax.axis_index("pan")
    energy = lax.axis_index("en").astype(jnp.int32).reshape(1)
    atoms = rows // ORB
    kinds = lax.dynamic_slice_in_dim(atom_kind, pan * atoms, atoms, 0)
    per_atom = sum(
        jnp.where(kinds[:, None] == kind, coupling[kind][None, :], 0.0)
        for kind in range(coupling.shape[0])
    )
    per_row = jnp.repeat(per_atom, ORB, axis=0)
    per_line = jnp.repeat(per_atom.T, ORB, axis=1)
    edges = None
    sigma = contact
    for rounds in range(ITERS):
        final = rounds == ITERS - 1
        pieces = spread(sigma, "pan")
        if final:
            edges = [
                shifted(retarded[:, :, :B, : columns // 2], "pan", -1),
                shifted(retarded[:, :, -B:, columns // 2 :], "pan", 1),
            ]
        carry = None
        for number, (far, piece) in enumerate(pieces):
            last = number == len(pieces) - 1
            carry = panel(
                retarded, pan ^ far, piece, carry, edges, final, last, f"panel{rounds}{number}"
            )
        lesser_diag = carry[0]
        if final:
            upper, above = carry[1:]
            lesser_upper = upper.at[:, :, -B:].add(shifted(above, "pan", -1))
        found = spread(lesser_diag, "en")[1:]
        sigma = phonon(shifts, energy, contact, per_row, per_line, found)
    return (lesser_diag, lesser_upper, sigma)


def solution(mesh):
    spread_spec = P(None, ("grp", "en"), "pan", None)
    return jax.shard_map(
        body,
        mesh=mesh,
        in_specs=(spread_spec, spread_spec, P(), P(), P()),
        out_specs=(spread_spec, spread_spec, spread_spec),
        check_vma=False,
    )
```

```python
import functools
import math

import jax
import jax.numpy as jnp
from jax import lax
from jax.experimental import pallas as pl
from jax.experimental.pallas import tpu as pltpu
from jax.sharding import PartitionSpec as P


B = 128
ORB = 8
ITERS = 2
VMEM_BYTES = 28 * 2**20

F32 = jnp.float32
BF16 = jnp.bfloat16


def swapped(x, axis, bit):
    return lax.ppermute(x, axis, [(i, i ^ bit) for i in range(lax.axis_size(axis))])


def spread(x, axis):
    pieces = [(0, x)]
    bit = lax.axis_size(axis) // 2
    while bit:
        found = []
        for far, piece in pieces:
            found.append((far ^ bit, swapped(piece, axis, bit)))
        pieces += found
        bit //= 2
    return pieces


def split(x):
    high = x.astype(BF16)
    return high, (x - high.astype(F32)).astype(BF16)


def dot(a, b):
    return jnp.dot(a, b, preferred_element_type=F32)


def dot_t(a, b):
    return lax.dot_general(a, b, (((1,), (1,)), ((), ())), preferred_element_type=F32)


def times(a, b):
    return dot(a[0], b[0]) + (dot(a[1], b[0]) + dot(a[0], b[1]))


def times_t(a, b):
    return dot_t(a[0], b[0]) + (dot_t(a[1], b[0]) + dot_t(a[0], b[1]))


def total(terms):
    return functools.reduce(lambda a, b: a + b, terms)


def pair_rows(x):
    return tuple(
        jnp.concatenate([v, jnp.concatenate([v[:, B:], -v[:, :B]], axis=1)], axis=0) for v in x
    )


def rows_of(x, start, size):
    return tuple(v[start : start + size] for v in x)


def panel_kernel(local, many, far, half, diag, upper, first, last, scale, *refs):
    refs = list(refs)
    at_ref, g_ref, s_ref = refs[:3]
    refs = refs[3:]
    if upper:
        even_ref, odd_ref = refs[:2]
        refs = refs[2:]
    kinds = ([local] if diag else []) + ([local + 1] if upper else [])
    ins = []
    if not first:
        ins, refs = refs[: len(kinds)], refs[len(kinds) :]
    if last:
        outs, accs = refs[: len(refs) - len(kinds)], refs[len(refs) - len(kinds) :]
    else:
        accs = refs
    step = pl.program_id(0)

    @pl.when(step == 0)
    def _():
        for i, acc in enumerate(accs):
            acc[...] = jnp.zeros_like(acc) if first else ins[i][...]

    greens, sigmas, products = [], [], []
    for u in range(many):
        cut = slice(u * B, (u + 1) * B)
        green = split(jnp.concatenate([g_ref[0, 0, :, cut], g_ref[1, 0, :, cut]], axis=1))
        sr, si = s_ref[0, 0, cut], s_ref[1, 0, cut]
        sigma = split(
            jnp.concatenate(
                [jnp.concatenate([sr, si], axis=1), jnp.concatenate([-si, sr], axis=1)], axis=0
            )
        )
        greens.append(green)
        sigmas.append(sigma)
        products.append(split(times(green, sigma)))
    acc_diag = accs[0] if diag else None
    acc_upper = accs[-1] if upper else None
    for i in range(local):
        start = 0 if diag else 1
        size = (1 if diag else 0) + (1 if upper and i < local - 1 else 0)
        if not size:
            continue
        terms = total(
            times_t(rows_of(green, (i + start) * B, size * B), pair_rows(rows_of(product, i * B, B)))
            for green, product in zip(greens, products)
        )
        if diag:
            acc_diag[i] += terms[:B]
        if upper and i < local - 1:
            acc_upper[i] += terms[-B:]
    if upper:
        pan = at_ref[0]
        below = ((pan ^ far) * (local // many) + step) * many < half
        own = (pan % 2 == 0) == below

        def extra(u):
            cut = slice(u * B, (u + 1) * B)
            return split(
                jnp.concatenate(
                    [
                        jnp.where(own, even_ref[j, 0, :, cut], odd_ref[j, 0, :, cut])
                        for j in range(2)
                    ],
                    axis=1,
                )
            )

        @pl.when(below)
        def _():
            acc_upper[local - 1] += total(
                times_t(extra(u), pair_rows(rows_of(products[u], (local - 1) * B, B)))
                for u in range(many)
            )

        @pl.when(jnp.logical_not(below))
        def _():
            acc_upper[local] += total(
                times_t(rows_of(greens[u], 0, B), pair_rows(split(times(extra(u), sigmas[u]))))
                for u in range(many)
            )

    if last:

        @pl.when(step == local // many - 1)
        def _():
            def put(ref, row, acc, where):
                ref[0, 0, row * B : (row + 1) * B] = acc[where, :, :B].T * scale
                ref[1, 0, row * B : (row + 1) * B] = acc[where, :, B:].T * scale

            free = list(outs)
            if diag:
                ref = free.pop(0)
                for i in range(local):
                    put(ref, i, acc_diag, i)
            if upper:
                for i in range(local):
                    put(free[0], i, acc_upper, i)
                put(free[1], 0, acc_upper, local)


def panel(at, green, far, piece, carry, edges, diag, upper, last):
    rows, columns = green.shape[2:]
    local = rows // B
    many = 2 if local % 2 == 0 else 1
    steps = local // many
    half = columns // B // 2
    specs = [
        pl.BlockSpec((2, 1, rows, many * B), lambda j, at: (0, 0, 0, (at[0] ^ far) * steps + j)),
        pl.BlockSpec((2, 1, many * B, B), lambda j, at: (0, 0, j, 0)),
    ]
    operands = [green, piece]
    if upper:
        parts = half // many
        edge = pl.BlockSpec(
            (2, 1, B, many * B), lambda j, at: (0, 0, 0, ((at[0] ^ far) * steps + j) % parts)
        )
        specs += [edge, edge]
        operands += edges
    counts = ([local] if diag else []) + ([local + 1] if upper else [])
    sums = [jax.ShapeDtypeStruct((count, B, 2 * B), F32) for count in counts]
    sum_specs = [pl.BlockSpec(s.shape, lambda j, at: (0, 0, 0)) for s in sums]
    if carry is not None:
        specs += sum_specs
        operands += carry
    if last:
        tall = jax.ShapeDtypeStruct((2, 1, rows, B), F32)
        small = jax.ShapeDtypeStruct((2, 1, B, B), F32)
        shapes = ([tall] if diag else []) + ([tall, small] if upper else [])
        out_specs = [pl.BlockSpec(s.shape, lambda j, at: (0, 0, 0, 0)) for s in shapes]
        scratch = [pltpu.VMEM(s.shape, F32) for s in sums]
    else:
        shapes, out_specs, scratch = sums, sum_specs, []
    work = 3 * 2 * (2 * B) * (2 * B) * rows * local * (1 + len(counts))
    return pl.pallas_call(
        functools.partial(
            panel_kernel,
            local,
            many,
            far,
            half,
            diag,
            upper,
            carry is None,
            last,
            1.0 / math.sqrt(B),
        ),
        grid_spec=pltpu.PrefetchScalarGridSpec(
            num_scalar_prefetch=1,
            grid=(steps,),
            in_specs=specs,
            out_specs=out_specs,
            scratch_shapes=scratch,
        ),
        out_shape=shapes,
        compiler_params=pltpu.CompilerParams(vmem_limit_bytes=VMEM_BYTES),
        cost_estimate=pl.CostEstimate(
            flops=work, bytes_accessed=8 * rows * B * local, transcendentals=0
        ),
    )(at, *operands)


def phonon_kernel(fars, modes, shift_ref, at_ref, contact_ref, col_ref, row_ref, *refs):
    out_ref = refs[-1]
    energy = at_ref[1]
    chosen = []
    for far in fars:
        apart = jnp.abs((energy ^ far) - energy)
        chosen.append([jnp.where(apart == shift_ref[m], 1.0, 0.0).astype(F32) for m in range(modes)])
    for start in range(0, contact_ref.shape[2], B):
        rows = slice(start, start + B)
        outer = [col_ref[rows, m : m + 1] * row_ref[m : m + 1, rows] for m in range(modes)]
        re, im = contact_ref[0, 0, rows], contact_ref[1, 0, rows]
        for weights, ref in zip(chosen, refs[:-1]):
            weight = total(w * o for w, o in zip(weights, outer))
            re += weight * ref[0, 0, rows]
            im += weight * ref[1, 0, rows]
        out_ref[0, 0, rows] = re
        out_ref[1, 0, rows] = im


def phonon(shifts, at, contact, columns, lines, pieces):
    rows = contact.shape[2]
    modes = shifts.shape[0]
    whole = pl.BlockSpec(contact.shape, lambda i, *_: (0, 0, 0, 0))
    return pl.pallas_call(
        functools.partial(phonon_kernel, [far for far, _ in pieces], modes),
        grid_spec=pltpu.PrefetchScalarGridSpec(
            num_scalar_prefetch=2,
            grid=(1,),
            in_specs=[
                whole,
                pl.BlockSpec((rows, modes), lambda i, *_: (0, 0)),
                pl.BlockSpec((modes, rows), lambda i, *_: (0, 0)),
            ]
            + [whole] * len(pieces),
            out_specs=whole,
        ),
        out_shape=jax.ShapeDtypeStruct(contact.shape, F32),
        compiler_params=pltpu.CompilerParams(vmem_limit_bytes=VMEM_BYTES),
        cost_estimate=pl.CostEstimate(
            flops=rows * B * 20, bytes_accessed=8 * rows * B * 5, transcendentals=0
        ),
    )(shifts, at, contact, columns, lines, *[piece for _, piece in pieces])


def add_kernel(upper_ref, above_ref, out_ref):
    out_ref[...] = upper_ref[...] + above_ref[...]


def with_above(upper, above):
    rows = upper.shape[2]
    tail = pl.BlockSpec((2, 1, B, B), lambda i: (0, 0, rows // B - 1, 0))
    return pl.pallas_call(
        add_kernel,
        grid=(1,),
        in_specs=[tail, pl.BlockSpec((2, 1, B, B), lambda i: (0, 0, 0, 0))],
        out_specs=tail,
        out_shape=jax.ShapeDtypeStruct(upper.shape, F32),
        input_output_aliases={0: 0},
        compiler_params=pltpu.CompilerParams(vmem_limit_bytes=VMEM_BYTES),
        cost_estimate=pl.CostEstimate(flops=2 * B * B, bytes_accessed=24 * B * B, transcendentals=0),
        name="above",
    )(upper, above)


def edge_rows(retarded, pan):
    rows, columns = retarded.shape[2:]
    devices = lax.axis_size("pan")
    found, cuts = [], []
    for odd in (0, 1):
        up = (pan % 2 == odd).astype(jnp.int32)
        part = lax.dynamic_slice(
            retarded,
            (0, 0, up * (rows - B), up * (columns // 2)),
            (2, 1, B, columns // 2),
        )
        pairs = []
        for i in range(odd, devices - 1, 2):
            pairs += [(i, i + 1), (i + 1, i)]
        cuts.append(part)
        found.append(lax.ppermute(part, "pan", pairs))
    return found, cuts


def body(retarded, contact, atom_kind, coupling, shifts):
    rows = retarded.shape[2]
    pan = lax.axis_index("pan").astype(jnp.int32)
    energy = lax.axis_index("en").astype(jnp.int32)
    at = jnp.where(jnp.arange(2, dtype=jnp.int32) == 0, pan, energy)
    atoms = rows // ORB
    kinds = lax.dynamic_slice_in_dim(atom_kind, pan * atoms, atoms, 0)
    per_atom = sum(
        jnp.where(kinds[:, None] == kind, coupling[kind][None, :], 0.0)
        for kind in range(coupling.shape[0])
    )
    per_row = jnp.repeat(per_atom, ORB, axis=0)
    per_line = jnp.repeat(per_atom.T, ORB, axis=1)
    edges, cuts = edge_rows(retarded, pan)
    sigma = contact
    for rounds in range(ITERS):
        final = rounds == ITERS - 1
        pieces = spread(sigma, "pan")
        if rounds == 0:
            ready = lax.optimization_barrier((contact, per_row, per_line, *cuts))
            pieces[0] = (0, ready[0])
            per_row, per_line = ready[1:3]
        carry = None
        for far, piece in pieces[:-1]:
            carry = panel(at, retarded, far, piece, carry, edges, True, final, False)
        far, piece = pieces[-1]
        (lesser_diag,) = panel(at, retarded, far, piece, carry[:1], edges, True, False, True)
        found = spread(lesser_diag, "en")[1:]
        if final:
            upper, above = panel(at, retarded, far, piece, carry[1:], edges, False, True, True)
            devices = lax.axis_size("pan")
            above = lax.ppermute(above, "pan", [(i + 1, i) for i in range(devices - 1)])
            lesser_upper = with_above(upper, above)
        sigma = phonon(shifts, at, contact, per_row, per_line, found)
    return (lesser_diag, lesser_upper, sigma)


def solution(mesh):
    spread_spec = P(None, ("grp", "en"), "pan", None)
    return jax.shard_map(
        body,
        mesh=mesh,
        in_specs=(spread_spec, spread_spec, P(), P(), P()),
        out_specs=(spread_spec, spread_spec, spread_spec),
        check_vma=False,
    )
```

```python
import functools
import math

import jax
import jax.numpy as jnp
from jax import lax
from jax.experimental import pallas as pl
from jax.experimental.pallas import tpu as pltpu
from jax.sharding import PartitionSpec as P


B = 128
ORB = 8
ITERS = 2
VMEM_BYTES = 28 * 2**20

F32 = jnp.float32
BF16 = jnp.bfloat16


def swapped(x, axis, bit):
    return lax.ppermute(x, axis, [(i, i ^ bit) for i in range(lax.axis_size(axis))])


def spread(x, axis):
    pieces = [(0, x)]
    bit = lax.axis_size(axis) // 2
    while bit:
        found = []
        for far, piece in pieces:
            found.append((far ^ bit, swapped(piece, axis, bit)))
        pieces += found
        bit //= 2
    return pieces


def split(x):
    high = x.astype(BF16)
    return high, (x - high.astype(F32)).astype(BF16)


def dot(a, b):
    return jnp.dot(a, b, preferred_element_type=F32)


def dot_t(a, b):
    return lax.dot_general(a, b, (((1,), (1,)), ((), ())), preferred_element_type=F32)


def times(a, b):
    return dot(a[0], b[0]) + (dot(a[1], b[0]) + dot(a[0], b[1]))


def times_t(a, b):
    return dot_t(a[0], b[0]) + (dot_t(a[1], b[0]) + dot_t(a[0], b[1]))


def total(terms):
    return functools.reduce(lambda a, b: a + b, terms)


def pair_rows(x):
    return tuple(
        jnp.concatenate([v, jnp.concatenate([v[:, B:], -v[:, :B]], axis=1)], axis=0) for v in x
    )


def rows_of(x, start, size):
    return tuple(v[start : start + size] for v in x)


def panel_kernel(local, far, starts, diag, upper, back, first, last, devices, scale, *refs):
    refs = list(refs)
    at_ref, g_ref = refs[:2]
    piece_refs, refs = refs[2 : 2 + len(starts)], refs[2 + len(starts) :]
    if upper:
        even_ref, odd_ref = refs[:2]
        refs = refs[2:]
    count = int(diag) + int(upper) + int(back)
    ins = []
    if not first:
        ins, refs = refs[:count], refs[count:]
    if last and upper:
        above_ref, refs = refs[0], refs[1:]
    outs = refs
    pan = at_ref[0]
    source = pan ^ far
    middle = devices // 2
    half = devices * local // 2

    greens, sigmas, products, columns = [], [], [], []
    for start, s_ref in zip(starts, piece_refs):
        for u in range(s_ref.shape[2] // B):
            k = source * local + start + u
            columns.append(pl.ds(pl.multiple_of((k % half) * B, B), B))
            cut = pl.ds(pl.multiple_of(k * B, B), B)
            green = split(jnp.concatenate([g_ref[0, 0, :, cut], g_ref[1, 0, :, cut]], axis=1))
            rows = slice(u * B, (u + 1) * B)
            sr, si = s_ref[0, 0, rows], s_ref[1, 0, rows]
            sigma = split(
                jnp.concatenate(
                    [jnp.concatenate([sr, si], axis=1), jnp.concatenate([-si, sr], axis=1)], axis=0
                )
            )
            greens.append(green)
            sigmas.append(sigma)
            products.append(split(times(green, sigma)))

    def old(which, i):
        return 0.0 if first else ins[which][i]

    def put(ref, row, value):
        ref[0, 0, row * B : (row + 1) * B] = value[:, :B].T * scale
        ref[1, 0, row * B : (row + 1) * B] = value[:, B:].T * scale

    at_upper = int(diag)
    for i in range(local):
        start = 0 if diag else 1
        size = int(diag) + int(upper and i < local - 1)
        if not size:
            continue
        terms = total(
            times_t(rows_of(green, (i + start) * B, size * B), pair_rows(rows_of(product, i * B, B)))
            for green, product in zip(greens, products)
        )
        if diag:
            value = old(0, i) + terms[:B]
            if last:
                put(outs[0], i, value)
            else:
                outs[0][i] = value
        if upper and i < local - 1:
            value = old(at_upper, i) + terms[-B:]
            if last:
                put(outs[at_upper], i, value)
            else:
                outs[at_upper][i] = value
    if upper:
        source_high = source >= middle
        ours = (source_high == (pan >= middle)) if back else None
        theirs = source_high != (pan + 1 >= middle)
        even = pan % 2 == 0

        def edge(near, column):
            return split(
                jnp.concatenate(
                    [
                        jnp.where(near, even_ref[j, 0, :, column], odd_ref[j, 0, :, column])
                        for j in range(2)
                    ],
                    axis=1,
                )
            )

        if first:
            outs[at_upper][local - 1] = jnp.zeros((B, 2 * B), F32)
            outs[at_upper + 1][0] = jnp.zeros((B, 2 * B), F32)
        if last:
            edge_sum = ins[at_upper]
        else:
            edge_sum = outs[at_upper]

        @pl.when(theirs)
        def _():
            terms = total(
                times_t(edge(even, column), pair_rows(rows_of(product, (local - 1) * B, B)))
                for product, column in zip(products, columns)
            )
            if last:
                put(outs[at_upper], local - 1, edge_sum[local - 1] + terms + above_ref[0])
            else:
                edge_sum[local - 1] += terms

        if last:

            @pl.when(jnp.logical_not(theirs))
            def _():
                put(outs[at_upper], local - 1, edge_sum[local - 1] + above_ref[0])

        if back:

            @pl.when(ours)
            def _():
                outs[at_upper + 1][0] += total(
                    times_t(
                        rows_of(green, 0, B),
                        pair_rows(split(times(edge(jnp.logical_not(even), column), sigma))),
                    )
                    for green, sigma, column in zip(greens, sigmas, columns)
                )


def panel(at, green, far, pieces, carry, edges, kinds, last, above=None):
    rows = green.shape[2]
    local = rows // B
    devices = lax.axis_size("pan")
    counts = {"diag": local, "upper": local, "back": 1}
    vmem = pl.BlockSpec(memory_space=pltpu.VMEM)
    starts, many = [], 0
    for start, piece in pieces:
        starts.append(start)
        many += piece.shape[2] // B
    operands = [at, green] + [piece for _, piece in pieces]
    if "upper" in kinds:
        operands += edges
    shapes = {kind: jax.ShapeDtypeStruct((counts[kind], B, 2 * B), F32) for kind in kinds}
    aliases = {}
    if carry is not None:
        for number, kind in enumerate(kinds):
            if not last:
                aliases[len(operands)] = number
            operands.append(carry[kind])
    if last:
        shapes = {kind: jax.ShapeDtypeStruct((2, 1, rows, B), F32) for kind in kinds}
        if above is not None:
            operands.append(above)
    work = 3 * 2 * (2 * B) * (2 * B) * rows * many * (1 + len(kinds))
    out = pl.pallas_call(
        functools.partial(
            panel_kernel,
            local,
            far,
            starts,
            "diag" in kinds,
            "upper" in kinds,
            "back" in kinds,
            carry is None,
            last,
            devices,
            1.0 / math.sqrt(B),
        ),
        in_specs=[pl.BlockSpec(memory_space=pltpu.SMEM)] + [vmem] * (len(operands) - 1),
        out_specs=[vmem] * len(shapes),
        out_shape=list(shapes.values()),
        input_output_aliases=aliases,
        compiler_params=pltpu.CompilerParams(vmem_limit_bytes=VMEM_BYTES),
        cost_estimate=pl.CostEstimate(
            flops=work, bytes_accessed=8 * rows * B * many, transcendentals=0
        ),
    )(*operands)
    return dict(zip(kinds, out))


def phonon_kernel(fars, modes, shift_ref, at_ref, contact_ref, col_ref, row_ref, *refs):
    out_refs = refs[len(fars) :]
    energy = at_ref[1]
    chosen = []
    for far in fars:
        apart = jnp.abs((energy ^ far) - energy)
        chosen.append([jnp.where(apart == shift_ref[m], 1.0, 0.0).astype(F32) for m in range(modes)])
    for start in range(0, contact_ref.shape[2], B):
        rows = slice(start, start + B)
        outer = [col_ref[rows, m : m + 1] * row_ref[m : m + 1, rows] for m in range(modes)]
        values = [contact_ref[0, 0, rows], contact_ref[1, 0, rows]]
        for weights, ref in zip(chosen, refs):
            weight = total(w * o for w, o in zip(weights, outer))
            values = [value + weight * ref[j, 0, rows] for j, value in enumerate(values)]
        first = 0
        for number, ref in enumerate(out_refs):
            at = start if number == 0 else start - first
            if 0 <= at < ref.shape[2]:
                for j in range(2):
                    ref[j, 0, at : at + B] = values[j]
            if number > 0:
                first += ref.shape[2]


def phonon(shifts, at, contact, columns, lines, pieces, chunks):
    parts, energies, rows = contact.shape[:3]
    modes = shifts.shape[0]
    vmem = pl.BlockSpec(memory_space=pltpu.VMEM)
    smem = pl.BlockSpec(memory_space=pltpu.SMEM)
    shapes = [jax.ShapeDtypeStruct(contact.shape, F32)]
    if chunks > 1:
        shapes += [jax.ShapeDtypeStruct((parts, energies, rows // chunks, B), F32)] * chunks
    return pl.pallas_call(
        functools.partial(phonon_kernel, [far for far, _ in pieces], modes),
        in_specs=[smem, smem] + [vmem] * (3 + len(pieces)),
        out_specs=[vmem] * len(shapes),
        out_shape=shapes,
        compiler_params=pltpu.CompilerParams(vmem_limit_bytes=VMEM_BYTES),
        cost_estimate=pl.CostEstimate(
            flops=rows * B * 20, bytes_accessed=8 * rows * B * 5, transcendentals=0
        ),
    )(shifts, at, contact, columns, lines, *[piece for _, piece in pieces])


def edge_rows(retarded, pan):
    rows, columns = retarded.shape[2:]
    devices = lax.axis_size("pan")
    middle = devices // 2
    up_start = (pan + 1 >= middle).astype(jnp.int32)
    down_start = (pan < middle).astype(jnp.int32)
    found, cuts = [], []
    for odd in (0, 1):
        up = pan % 2 == odd
        row = jnp.where(up, rows - B, 0)
        column = jnp.where(up, up_start, down_start) * (columns // 2)
        part = lax.dynamic_slice(retarded, (0, 0, row, column), (2, 1, B, columns // 2))
        pairs = []
        for i in range(odd, devices - 1, 2):
            pairs += [(i, i + 1), (i + 1, i)]
        cuts.append(part)
        found.append(lax.ppermute(part, "pan", pairs))
    return found, cuts


def gathered(whole, chunks):
    size = whole.shape[2] // B // len(chunks)
    parts = [(i * size, chunk) for i, chunk in enumerate(chunks)]
    first = lax.axis_size("pan") // 2
    pieces = [(0, [(0, whole)])]
    bit = first
    while bit:
        found = []
        for far, piece in pieces:
            if bit == first:
                piece = parts
            sent = []
            for start, block in piece:
                sent.append((start, swapped(block, "pan", bit)))
            found.append((far ^ bit, sent))
        pieces += found
        bit //= 2
    return pieces


def body(retarded, contact, atom_kind, coupling, shifts):
    rows = retarded.shape[2]
    local = rows // B
    chunks = 2 if local % 2 == 0 else 1
    pan = lax.axis_index("pan").astype(jnp.int32)
    energy = lax.axis_index("en").astype(jnp.int32)
    at = jnp.where(jnp.arange(2, dtype=jnp.int32) == 0, pan, energy)
    atoms = rows // ORB
    kinds = lax.dynamic_slice_in_dim(atom_kind, pan * atoms, atoms, 0)
    per_atom = sum(
        jnp.where(kinds[:, None] == kind, coupling[kind][None, :], 0.0)
        for kind in range(coupling.shape[0])
    )
    per_row = jnp.repeat(per_atom, ORB, axis=0)
    per_line = jnp.repeat(per_atom.T, ORB, axis=1)
    edges, cuts = edge_rows(retarded, pan)
    sigma = contact
    parts = [contact]
    if chunks > 1:
        size = rows // chunks
        parts = [contact[:, :, i * size : (i + 1) * size] for i in range(chunks)]
    for rounds in range(ITERS):
        final = rounds == ITERS - 1
        pieces = gathered(sigma, parts)
        if rounds == 0:
            ready = lax.optimization_barrier((contact, per_row, per_line, *cuts))
            pieces[0] = (0, [(0, ready[0])])
            per_row, per_line = ready[1:3]
        work = ("diag", "upper", "back") if final else ("diag",)
        sums = None
        order = sorted(pieces[:-1], key=lambda piece: (piece[0] != 0, piece[0] >= lax.axis_size("pan") // 2))
        for far, blocks in order:
            kinds_here = work
            if final and far >= lax.axis_size("pan") // 2:
                kinds_here = work[:2]
            new = panel(at, retarded, far, blocks, sums, edges, kinds_here, False)
            sums = dict(sums or {}, **new)
        far, blocks = pieces[-1]
        for number, block in enumerate(blocks):
            last = number == len(blocks) - 1
            new = panel(at, retarded, far, [block], sums, edges, ("diag",), last)
            sums = dict(sums, **new)
        lesser_diag = sums["diag"]
        found = spread(lesser_diag, "en")[1:]
        if final:
            devices = lax.axis_size("pan")
            above = lax.ppermute(sums["back"], "pan", [(i + 1, i) for i in range(devices - 1)])
            lesser_upper = panel(
                at, retarded, far, blocks, sums, edges, ("upper",), True, above
            )["upper"]
        out = phonon(shifts, at, contact, per_row, per_line, found, 1 if final else chunks)
        sigma, parts = out[0], (out[1:] if len(out) > 1 else out)
    return (lesser_diag, lesser_upper, sigma)


def solution(mesh):
    def step(retarded, *args):
        spread_spec = P(None, ("grp", "en"), "pan", None)
        inner = jax.shard_map(
            body,
            mesh=mesh,
            in_specs=(spread_spec, spread_spec, P(), P(), P()),
            out_specs=(spread_spec, spread_spec, spread_spec),
            check_vma=False,
        )
        return inner(retarded, *args)

    return step
```

```python
import functools
import math

import jax
import jax.numpy as jnp
from jax import lax
from jax.experimental import pallas as pl
from jax.experimental.pallas import tpu as pltpu
from jax.sharding import PartitionSpec as P


B = 128
ORB = 8
ITERS = 2
VMEM_BYTES = 28 * 2**20

F32 = jnp.float32
BF16 = jnp.bfloat16


def swapped(x, axis, bit):
    return lax.ppermute(x, axis, [(i, i ^ bit) for i in range(lax.axis_size(axis))])


def spread(chunks, axis):
    pieces = [[(0, chunk)] for chunk in chunks]
    bit = lax.axis_size(axis) // 2
    while bit:
        for own in pieces:
            found = []
            for far, piece in own:
                found.append((far ^ bit, swapped(piece, axis, bit)))
            own += found
        bit //= 2
    return pieces


def split(x):
    high = x.astype(BF16)
    return high, (x - high.astype(F32)).astype(BF16)


def dot(a, b):
    return jnp.dot(a, b, preferred_element_type=F32)


def dot_t(a, b):
    return lax.dot_general(a, b, (((1,), (1,)), ((), ())), preferred_element_type=F32)


def times(a, b):
    return dot(a[0], b[0]) + (dot(a[1], b[0]) + dot(a[0], b[1]))


def times_t(a, b):
    return dot_t(a[0], b[0]) + (dot_t(a[1], b[0]) + dot_t(a[0], b[1]))


def total(terms):
    return functools.reduce(lambda a, b: a + b, terms)


def pair_rows(x):
    return tuple(
        jnp.concatenate([v, jnp.concatenate([v[:, B:], -v[:, :B]], axis=1)], axis=0) for v in x
    )


def rows_of(x, start, size):
    return tuple(v[start : start + size] for v in x)


def panel_kernel(local, far, starts, diag, upper, back, first, last, chunks, devices, scale, *refs):
    refs = list(refs)
    at_ref, g_ref = refs[:2]
    piece_refs, refs = refs[2 : 2 + len(starts)], refs[2 + len(starts) :]
    if upper:
        even_ref, odd_ref = refs[:2]
        refs = refs[2:]
    count = int(diag) + int(upper) + int(back)
    ins = []
    if not first:
        ins, refs = refs[:count], refs[count:]
    outs = refs
    pan = at_ref[0]
    source = pan ^ far
    middle = devices // 2
    half = devices * local // 2

    greens, sigmas, products, columns = [], [], [], []
    for start, s_ref in zip(starts, piece_refs):
        for u in range(s_ref.shape[2] // B):
            k = source * local + start + u
            columns.append(pl.ds(pl.multiple_of((k % half) * B, B), B))
            cut = pl.ds(pl.multiple_of(k * B, B), B)
            green = split(jnp.concatenate([g_ref[0, 0, :, cut], g_ref[1, 0, :, cut]], axis=1))
            rows = slice(u * B, (u + 1) * B)
            sr, si = s_ref[0, 0, rows], s_ref[1, 0, rows]
            sigma = split(
                jnp.concatenate(
                    [jnp.concatenate([sr, si], axis=1), jnp.concatenate([-si, sr], axis=1)], axis=0
                )
            )
            greens.append(green)
            sigmas.append(sigma)
            products.append(split(times(green, sigma)))

    def old(which, i):
        return 0.0 if first else ins[which][i]

    def put(ref, row, value):
        ref[0, 0, row * B : (row + 1) * B] = value[:, :B].T * scale
        ref[1, 0, row * B : (row + 1) * B] = value[:, B:].T * scale

    at_upper = int(diag)
    for i in range(local):
        start = 0 if diag else 1
        size = int(diag) + int(upper and i < local - 1)
        if not size:
            continue
        terms = total(
            times_t(rows_of(green, (i + start) * B, size * B), pair_rows(rows_of(product, i * B, B)))
            for green, product in zip(greens, products)
        )
        if diag:
            value = old(0, i) + terms[:B]
            if last:
                for ref in outs[chunks:]:
                    put(ref, i, value)
                put(outs[i * chunks // local], i % (local // chunks), value)
            else:
                outs[0][i] = value
        if upper and i < local - 1:
            value = old(at_upper, i) + terms[-B:]
            if last:
                put(outs[at_upper], i, value)
            else:
                outs[at_upper][i] = value
    if upper:
        source_high = source >= middle
        ours = (source_high == (pan >= middle)) if back else None
        theirs = source_high != (pan + 1 >= middle)
        even = pan % 2 == 0

        def edge(near, column):
            return split(
                jnp.concatenate(
                    [
                        jnp.where(near, even_ref[j, 0, :, column], odd_ref[j, 0, :, column])
                        for j in range(2)
                    ],
                    axis=1,
                )
            )

        if first:
            outs[at_upper][local - 1] = jnp.zeros((B, 2 * B), F32)
            outs[at_upper + 1][0] = jnp.zeros((B, 2 * B), F32)
        if last:
            edge_sum = ins[at_upper]
        else:
            edge_sum = outs[at_upper]

        @pl.when(theirs)
        def _():
            terms = total(
                times_t(edge(even, column), pair_rows(rows_of(product, (local - 1) * B, B)))
                for product, column in zip(products, columns)
            )
            if last:
                put(outs[at_upper], local - 1, edge_sum[local - 1] + terms)
            else:
                edge_sum[local - 1] += terms

        if last:

            @pl.when(jnp.logical_not(theirs))
            def _():
                put(outs[at_upper], local - 1, edge_sum[local - 1])

        if back:

            @pl.when(ours)
            def _():
                outs[at_upper + 1][0] += total(
                    times_t(
                        rows_of(green, 0, B),
                        pair_rows(split(times(edge(jnp.logical_not(even), column), sigma))),
                    )
                    for green, sigma, column in zip(greens, sigmas, columns)
                )


def panel(at, green, far, pieces, carry, edges, kinds, last, chunks=1, whole=False):
    rows = green.shape[2]
    local = rows // B
    devices = lax.axis_size("pan")
    counts = {"diag": local, "upper": local, "back": 1}
    vmem = pl.BlockSpec(memory_space=pltpu.VMEM)
    starts, many = [], 0
    for start, piece in pieces:
        starts.append(start)
        many += piece.shape[2] // B
    operands = [at, green] + [piece for _, piece in pieces]
    if "upper" in kinds:
        operands += edges
    shapes = {kind: jax.ShapeDtypeStruct((counts[kind], B, 2 * B), F32) for kind in kinds}
    aliases = {}
    if carry is not None:
        for number, kind in enumerate(kinds):
            if not last:
                aliases[len(operands)] = number
            operands.append(carry[kind])
    if last:
        shapes = {kind: jax.ShapeDtypeStruct((2, 1, rows, B), F32) for kind in kinds}
        if "diag" in kinds:
            part = jax.ShapeDtypeStruct((2, 1, rows // chunks, B), F32)
            shapes = {number: part for number in range(chunks)}
            if whole:
                shapes["whole"] = jax.ShapeDtypeStruct((2, 1, rows, B), F32)
    work = 3 * 2 * (2 * B) * (2 * B) * rows * many * (1 + len(kinds))
    out = pl.pallas_call(
        functools.partial(
            panel_kernel,
            local,
            far,
            starts,
            "diag" in kinds,
            "upper" in kinds,
            "back" in kinds,
            carry is None,
            last,
            chunks,
            devices,
            1.0 / math.sqrt(B),
        ),
        in_specs=[pl.BlockSpec(memory_space=pltpu.SMEM)] + [vmem] * (len(operands) - 1),
        out_specs=[vmem] * len(shapes),
        out_shape=list(shapes.values()),
        input_output_aliases=aliases,
        compiler_params=pltpu.CompilerParams(vmem_limit_bytes=VMEM_BYTES),
        cost_estimate=pl.CostEstimate(
            flops=work, bytes_accessed=8 * rows * B * many, transcendentals=0
        ),
    )(*operands)
    if last and "diag" in kinds:
        return {"diag": out}
    return dict(zip(kinds, out))


def phonon_kernel(fars, modes, row, size, final, scale, shift_ref, at_ref, contact_ref, *refs):
    col_ref, row_ref = refs[:2]
    piece_refs, refs = refs[2 : 2 + len(fars)], refs[2 + len(fars) :]
    energy = at_ref[1]
    chosen = []
    for far in fars:
        apart = jnp.abs((energy ^ far) - energy)
        chosen.append([jnp.where(apart == shift_ref[m], 1.0, 0.0).astype(F32) for m in range(modes)])
    out_ref = refs[-2] if final and len(refs) > 2 else refs[-1]
    for start in range(0, size, B):
        rows = slice(row + start, row + start + B)
        here = slice(start, start + B)
        outer = [col_ref[rows, m : m + 1] * row_ref[m : m + 1, rows] for m in range(modes)]
        values = [contact_ref[0, 0, rows], contact_ref[1, 0, rows]]
        for weights, ref in zip(chosen, piece_refs):
            weight = total(w * o for w, o in zip(weights, outer))
            values = [value + weight * ref[j, 0, here] for j, value in enumerate(values)]
        for j in range(2):
            out_ref[j, 0, here] = values[j]
    if final and len(refs) > 2:
        upper_ref, above_ref = refs[:2]
        for j in range(2):
            more = above_ref[0, :, j * B : (j + 1) * B].T * scale
            refs[-1][j, 0] = upper_ref[j, 0] + more


def phonon(shifts, at, contact, columns, lines, pieces, number, chunks):
    parts, energies, rows = contact.shape[:3]
    size = rows // chunks
    vmem = pl.BlockSpec(memory_space=pltpu.VMEM)
    smem = pl.BlockSpec(memory_space=pltpu.SMEM)
    return pl.pallas_call(
        functools.partial(
            phonon_kernel,
            [far for far, _ in pieces],
            shifts.shape[0],
            number * size,
            size,
            False,
            1.0,
        ),
        in_specs=[smem, smem] + [vmem] * (3 + len(pieces)),
        out_specs=vmem,
        out_shape=jax.ShapeDtypeStruct((parts, energies, size, B), F32),
        compiler_params=pltpu.CompilerParams(vmem_limit_bytes=VMEM_BYTES),
        cost_estimate=pl.CostEstimate(
            flops=size * B * 20, bytes_accessed=8 * size * B * 5, transcendentals=0
        ),
    )(shifts, at, contact, columns, lines, *[piece for _, piece in pieces])


def skip_kernel(count, kernel, *refs):
    kernel(*refs[:count], *refs[count + 1 :])


def phonon_final(shifts, at, contact, columns, lines, pieces, number, chunks, so_far, ends):
    rows = contact.shape[2]
    size = rows // chunks
    vmem = pl.BlockSpec(memory_space=pltpu.VMEM)
    smem = pl.BlockSpec(memory_space=pltpu.SMEM)
    kernel = functools.partial(
        phonon_kernel,
        [far for far, _ in pieces],
        shifts.shape[0],
        number * size,
        size,
        True,
        1.0 / math.sqrt(B),
    )
    operands = [shifts, at, contact, columns, lines, *[piece for _, piece in pieces]]
    specs = [smem, smem] + [vmem] * (3 + len(pieces))
    shapes = [jax.ShapeDtypeStruct(contact.shape, F32)]
    out_specs = [pl.BlockSpec((2, 1, size, B), lambda i: (0, 0, number, 0))]
    aliases = {}
    if so_far is not None:
        kernel = functools.partial(skip_kernel, len(operands), kernel)
        aliases[len(operands)] = 0
        operands.append(so_far)
        specs.append(pl.BlockSpec(memory_space=pl.ANY))
    if ends is not None:
        upper, above = ends
        tail = pl.BlockSpec((2, 1, B, B), lambda i: (0, 0, rows // B - 1, 0))
        aliases[len(operands)] = 1
        operands += [upper, above]
        specs += [tail, vmem]
        shapes.append(jax.ShapeDtypeStruct(upper.shape, F32))
        out_specs.append(tail)
    return pl.pallas_call(
        kernel,
        grid=(1,),
        in_specs=specs,
        out_specs=out_specs,
        out_shape=shapes,
        input_output_aliases=aliases,
        compiler_params=pltpu.CompilerParams(vmem_limit_bytes=VMEM_BYTES),
        cost_estimate=pl.CostEstimate(
            flops=size * B * 20, bytes_accessed=8 * size * B * 5, transcendentals=0
        ),
    )(*operands)


def cut_kernel(contact_ref, *refs):
    outs, sems = refs[:-1], refs[-1]
    copies = []
    start = 0
    for number, ref in enumerate(outs):
        size = ref.shape[2]
        at = 0 if number == len(outs) - 1 else start
        start += size
        copies.append(
            pltpu.make_async_copy(contact_ref.at[:, :, pl.ds(at, size)], ref, sems.at[number])
        )
    for copy in copies:
        copy.start()
    for copy in copies:
        copy.wait()


def cut(contact, chunks):
    parts, energies, rows = contact.shape[:3]
    part = jax.ShapeDtypeStruct((parts, energies, rows // chunks, B), F32)
    vmem = pl.BlockSpec(memory_space=pltpu.VMEM)
    return pl.pallas_call(
        cut_kernel,
        in_specs=[pl.BlockSpec(memory_space=pltpu.HBM)],
        out_specs=[vmem] * (chunks + 1),
        out_shape=[part] * chunks + [jax.ShapeDtypeStruct(contact.shape, F32)],
        scratch_shapes=[pltpu.SemaphoreType.DMA((chunks + 1,))],
        compiler_params=pltpu.CompilerParams(vmem_limit_bytes=VMEM_BYTES),
        cost_estimate=pl.CostEstimate(
            flops=0, bytes_accessed=32 * rows * B, transcendentals=0
        ),
        name="cut",
    )(contact)


def edge_rows(retarded, pan):
    rows, columns = retarded.shape[2:]
    devices = lax.axis_size("pan")
    middle = devices // 2
    up_start = (pan + 1 >= middle).astype(jnp.int32)
    down_start = (pan < middle).astype(jnp.int32)
    found, cuts = [], []
    for odd in (0, 1):
        up = pan % 2 == odd
        row = jnp.where(up, rows - B, 0)
        column = jnp.where(up, up_start, down_start) * (columns // 2)
        part = lax.dynamic_slice(retarded, (0, 0, row, column), (2, 1, B, columns // 2))
        pairs = []
        for i in range(odd, devices - 1, 2):
            pairs += [(i, i + 1), (i + 1, i)]
        cuts.append(part)
        found.append(lax.ppermute(part, "pan", pairs))
    return found, cuts


def gathered(near, chunks):
    size = chunks[0].shape[2] // B
    parts = [(i * size, chunk) for i, chunk in enumerate(chunks)]
    first = lax.axis_size("pan") // 2
    pieces = [(0, near)]
    bit = first
    while bit:
        found = []
        for far, piece in pieces:
            if bit == first:
                piece = parts
            sent = []
            for start, block in piece:
                sent.append((start, swapped(block, "pan", bit)))
            found.append((far ^ bit, sent))
        pieces += found
        bit //= 2
    return pieces


def body(retarded, contact, atom_kind, coupling, shifts):
    rows = retarded.shape[2]
    local = rows // B
    chunks = 2 if local % 2 == 0 else 1
    high = lax.axis_size("pan") // 2
    pan = lax.axis_index("pan").astype(jnp.int32)
    energy = lax.axis_index("en").astype(jnp.int32)
    at = jnp.where(jnp.arange(2, dtype=jnp.int32) == 0, pan, energy)
    atoms = rows // ORB
    kinds = lax.dynamic_slice_in_dim(atom_kind, pan * atoms, atoms, 0)
    per_atom = sum(
        jnp.where(kinds[:, None] == kind, coupling[kind][None, :], 0.0)
        for kind in range(coupling.shape[0])
    )
    per_row = jnp.repeat(per_atom, ORB, axis=0)
    per_line = jnp.repeat(per_atom.T, ORB, axis=1)
    edges, cuts = edge_rows(retarded, pan)
    *parts, copied = cut(contact, chunks)
    near = [(0, contact)]
    for rounds in range(ITERS):
        final = rounds == ITERS - 1
        pieces = gathered(near, parts)
        if rounds == 0:
            ready = lax.optimization_barrier((copied, per_row, per_line, *cuts))
            pieces[0] = (0, [(0, ready[0])])
            copied, per_row, per_line = ready[:3]
        work = ("diag", "upper", "back") if final else ("diag",)
        sums = None
        groups = [(far, 0, blocks) for far, blocks in pieces[:-1]]
        groups.sort(key=lambda group: (group[0] != 0, group[0] >= high))
        if final and chunks > 1 and 1 < high:
            far, _, blocks = groups.pop([far for far, _, _ in groups].index(high))
            groups.insert(1, (far, 0, blocks[:1]))
            groups.append((far, 1, blocks[1:]))
        for far, number, blocks in groups:
            kinds_here = work[:2] if final and far >= high else work
            new = panel(at, retarded, far, blocks, sums, edges, kinds_here, False)
            sums = dict(sums or {}, **new)
        far, blocks = pieces[-1]
        for number, block in enumerate(blocks):
            last = number == len(blocks) - 1
            new = panel(
                at, retarded, far, [block], sums, edges, ("diag",), last, chunks, final and last
            )
            sums = dict(sums, **new)
        found = spread(sums["diag"][:chunks], "en")
        settings = (shifts, at, copied, per_row, per_line)
        if not final:
            parts = [phonon(*settings, own[1:], number, chunks) for number, own in enumerate(found)]
            near = [(i * (local // chunks), part) for i, part in enumerate(parts)]
    devices = lax.axis_size("pan")
    above = lax.ppermute(sums["back"], "pan", [(i + 1, i) for i in range(devices - 1)])
    upper = panel(at, retarded, far, blocks, sums, edges, ("upper",), True)["upper"]
    sigma = None
    for number, own in enumerate(found):
        ends = (upper, above) if number == chunks - 1 else None
        sigma, *rest = phonon_final(*settings, own[1:], number, chunks, sigma, ends)
    return (sums["diag"][chunks], rest[0], sigma)


def solution(mesh):
    def step(retarded, *args):
        spread_spec = P(None, ("grp", "en"), "pan", None)
        inner = jax.shard_map(
            body,
            mesh=mesh,
            in_specs=(spread_spec, spread_spec, P(), P(), P()),
            out_specs=(spread_spec, spread_spec, spread_spec),
            check_vma=False,
        )
        return inner(retarded, *args)

    return step
```

```python
import functools
import math

import jax
import jax.numpy as jnp
from jax import lax
from jax.experimental import pallas as pl
from jax.experimental.pallas import tpu as pltpu
from jax.sharding import PartitionSpec as P


B = 128
ORB = 8
ITERS = 2
VMEM_BYTES = 28 * 2**20

F32 = jnp.float32
BF16 = jnp.bfloat16


def swapped(x, axis, bit):
    return lax.ppermute(x, axis, [(i, i ^ bit) for i in range(lax.axis_size(axis))])


def spread(chunks, axis):
    pieces = [[(0, chunk)] for chunk in chunks]
    bit = lax.axis_size(axis) // 2
    while bit:
        for own in pieces:
            found = []
            for far, piece in own:
                found.append((far ^ bit, swapped(piece, axis, bit)))
            own += found
        bit //= 2
    return pieces


def split(x):
    high = x.astype(BF16)
    return high, (x - high.astype(F32)).astype(BF16)


def dot(a, b):
    return jnp.dot(a, b, preferred_element_type=F32)


def dot_t(a, b):
    return lax.dot_general(a, b, (((1,), (1,)), ((), ())), preferred_element_type=F32)


def times(a, b):
    return dot(a[0], b[0]) + (dot(a[1], b[0]) + dot(a[0], b[1]))


def times_t(a, b):
    return dot_t(a[0], b[0]) + (dot_t(a[1], b[0]) + dot_t(a[0], b[1]))


def total(terms):
    return functools.reduce(lambda a, b: a + b, terms)


def pair_rows(x):
    return tuple(
        jnp.concatenate([v, jnp.concatenate([v[:, B:], -v[:, :B]], axis=1)], axis=0) for v in x
    )


def rows_of(x, start, size):
    return tuple(v[start : start + size] for v in x)


def panel_kernel(local, far, starts, kinds, first, last, chunks, devices, scale, *refs):
    refs = list(refs)
    at_ref, g_ref = refs[:2]
    piece_refs, refs = refs[2 : 2 + len(starts)], refs[2 + len(starts) :]
    edges = "over" in kinds or "back" in kinds
    if edges:
        even_ref, odd_ref = refs[:2]
        refs = refs[2:]
    ins = {}
    for kind in kinds:
        if kind not in first:
            ins[kind] = refs.pop(0)
    outs = refs if last else dict(zip(kinds, refs))
    pan = at_ref[0]
    source = pan ^ far
    middle = devices // 2
    half = devices * local // 2
    whole = "diag" in kinds or "upper" in kinds
    low = 0 if whole else (local - 1) * B

    greens, sigmas, products, columns = [], [], [], []
    for start, s_ref in zip(starts, piece_refs):
        for u in range(s_ref.shape[2] // B):
            k = source * local + start + u
            columns.append(pl.ds(pl.multiple_of((k % half) * B, B), B))
            cut = pl.ds(pl.multiple_of(k * B, B), B)
            rows = slice(u * B, (u + 1) * B)
            sr, si = s_ref[0, 0, rows], s_ref[1, 0, rows]
            sigmas.append(
                split(
                    jnp.concatenate(
                        [jnp.concatenate([sr, si], axis=1), jnp.concatenate([-si, sr], axis=1)],
                        axis=0,
                    )
                )
            )
            greens.append(lambda low, high, cut=cut: split(
                jnp.concatenate([g_ref[0, 0, low:high, cut], g_ref[1, 0, low:high, cut]], axis=1)
            ))
            if whole:
                greens[-1] = functools.partial(
                    lambda whole, low, high: rows_of(whole, low, high - low),
                    greens[-1](0, local * B),
                )
                products.append(split(times(greens[-1](0, local * B), sigmas[-1])))

    def old(kind, i):
        return ins[kind][i] if kind in ins else 0.0

    def put(ref, row, value):
        ref[0, 0, row * B : (row + 1) * B] = value[:, :B].T * scale
        ref[1, 0, row * B : (row + 1) * B] = value[:, B:].T * scale

    diag, upper = "diag" in kinds, "upper" in kinds
    for i in range(local):
        start = 0 if diag else 1
        size = int(diag) + int(upper and i < local - 1)
        if not size:
            continue
        terms = total(
            times_t(green((i + start) * B, (i + start + size) * B), pair_rows(rows_of(product, i * B, B)))
            for green, product in zip(greens, products)
        )
        if diag:
            value = old("diag", i) + terms[:B]
            if last:
                for ref in outs[chunks:]:
                    put(ref, i, value)
                put(outs[i * chunks // local], i % (local // chunks), value)
            else:
                outs["diag"][i] = value
        if upper and i < local - 1:
            value = old("upper", i) + terms[-B:]
            if last:
                put(outs[0], i, value)
            else:
                outs["upper"][i] = value
    if edges:
        source_high = source >= middle
        even = pan % 2 == 0

        def edge(near, column):
            return split(
                jnp.concatenate(
                    [
                        jnp.where(near, even_ref[j, 0, :, column], odd_ref[j, 0, :, column])
                        for j in range(2)
                    ],
                    axis=1,
                )
            )

        def over_terms():
            terms = []
            for number, column in enumerate(columns):
                if whole:
                    product = rows_of(products[number], (local - 1) * B, B)
                else:
                    product = split(times(greens[number](low, local * B), sigmas[number]))
                terms.append(times_t(edge(even, column), pair_rows(product)))
            return total(terms)

        def back_terms():
            return total(
                times_t(green(0, B), pair_rows(split(times(edge(jnp.logical_not(even), column), sigma))))
                for green, sigma, column in zip(greens, sigmas, columns)
            )

        if "over" in kinds:
            theirs = source_high != (pan + 1 >= middle)
            if last:
                end = outs[0]

                @pl.when(theirs)
                def _():
                    put(end, local - 1, old("over", 0) + over_terms())

                @pl.when(jnp.logical_not(theirs))
                def _():
                    put(end, local - 1, jnp.zeros((B, 2 * B), F32) + old("over", 0))

            else:
                if "over" not in ins:
                    outs["over"][0] = jnp.zeros((B, 2 * B), F32)

                @pl.when(theirs)
                def _():
                    outs["over"][0] += over_terms()

        if "back" in kinds:
            if "back" not in ins:
                outs["back"][0] = jnp.zeros((B, 2 * B), F32)

            @pl.when(source_high == (pan >= middle))
            def _():
                outs["back"][0] += back_terms()


def panel(at, green, far, pieces, carry, edges, kinds, last, chunks=1, whole=False):
    rows = green.shape[2]
    local = rows // B
    devices = lax.axis_size("pan")
    counts = {"diag": local, "upper": local - 1, "over": 1, "back": 1}
    kinds = tuple(kind for kind in kinds if counts[kind])
    vmem = pl.BlockSpec(memory_space=pltpu.VMEM)
    starts, many = [], 0
    for start, piece in pieces:
        starts.append(start)
        many += piece.shape[2] // B
    operands = [at, green] + [piece for _, piece in pieces]
    if "over" in kinds or "back" in kinds:
        operands += edges
    shapes = {kind: jax.ShapeDtypeStruct((counts[kind], B, 2 * B), F32) for kind in kinds}
    aliases = {}
    first = []
    for number, kind in enumerate(kinds):
        if kind not in carry:
            first.append(kind)
            continue
        if not last:
            aliases[len(operands)] = number
        operands.append(carry[kind])
    if last:
        tall = jax.ShapeDtypeStruct((2, 1, rows, B), F32)
        shapes = {"upper": tall}
        if "diag" in kinds:
            part = jax.ShapeDtypeStruct((2, 1, rows // chunks, B), F32)
            shapes = {number: part for number in range(chunks)}
            if whole:
                shapes["whole"] = tall
    full = "diag" in kinds or "upper" in kinds
    work = 3 * 2 * (2 * B) * (2 * B) * many * (rows if full else B) * (1 + len(kinds))
    out = pl.pallas_call(
        functools.partial(
            panel_kernel,
            local,
            far,
            starts,
            kinds,
            first,
            last,
            chunks,
            devices,
            1.0 / math.sqrt(B),
        ),
        in_specs=[pl.BlockSpec(memory_space=pltpu.SMEM)] + [vmem] * (len(operands) - 1),
        out_specs=[vmem] * len(shapes),
        out_shape=list(shapes.values()),
        input_output_aliases=aliases,
        compiler_params=pltpu.CompilerParams(vmem_limit_bytes=VMEM_BYTES),
        cost_estimate=pl.CostEstimate(
            flops=work, bytes_accessed=8 * rows * B * many, transcendentals=0
        ),
    )(*operands)
    if last:
        return {"diag": out} if "diag" in kinds else {"upper": out[0]}
    return dict(carry, **dict(zip(kinds, out)))


def phonon_kernel(fars, modes, row, size, final, scale, shift_ref, at_ref, contact_ref, *refs):
    col_ref, row_ref = refs[:2]
    piece_refs, refs = refs[2 : 2 + len(fars)], refs[2 + len(fars) :]
    energy = at_ref[1]
    chosen = []
    for far in fars:
        apart = jnp.abs((energy ^ far) - energy)
        chosen.append([jnp.where(apart == shift_ref[m], 1.0, 0.0).astype(F32) for m in range(modes)])
    out_ref = refs[-2] if final and len(refs) > 2 else refs[-1]
    for start in range(0, size, B):
        rows = slice(row + start, row + start + B)
        here = slice(start, start + B)
        outer = [col_ref[rows, m : m + 1] * row_ref[m : m + 1, rows] for m in range(modes)]
        values = [contact_ref[0, 0, rows], contact_ref[1, 0, rows]]
        for weights, ref in zip(chosen, piece_refs):
            weight = total(w * o for w, o in zip(weights, outer))
            values = [value + weight * ref[j, 0, here] for j, value in enumerate(values)]
        for j in range(2):
            out_ref[j, 0, here] = values[j]
    if final and len(refs) > 2:
        upper_ref, above_ref = refs[:2]
        for j in range(2):
            more = above_ref[0, :, j * B : (j + 1) * B].T * scale
            refs[-1][j, 0] = upper_ref[j, 0] + more


def phonon(shifts, at, contact, columns, lines, pieces, number, chunks):
    parts, energies, rows = contact.shape[:3]
    size = rows // chunks
    vmem = pl.BlockSpec(memory_space=pltpu.VMEM)
    smem = pl.BlockSpec(memory_space=pltpu.SMEM)
    return pl.pallas_call(
        functools.partial(
            phonon_kernel,
            [far for far, _ in pieces],
            shifts.shape[0],
            number * size,
            size,
            False,
            1.0,
        ),
        in_specs=[smem, smem] + [vmem] * (3 + len(pieces)),
        out_specs=vmem,
        out_shape=jax.ShapeDtypeStruct((parts, energies, size, B), F32),
        compiler_params=pltpu.CompilerParams(vmem_limit_bytes=VMEM_BYTES),
        cost_estimate=pl.CostEstimate(
            flops=size * B * 20, bytes_accessed=8 * size * B * 5, transcendentals=0
        ),
    )(shifts, at, contact, columns, lines, *[piece for _, piece in pieces])


def skip_kernel(count, kernel, *refs):
    kernel(*refs[:count], *refs[count + 1 :])


def phonon_final(shifts, at, contact, columns, lines, pieces, number, chunks, so_far, ends):
    rows = contact.shape[2]
    size = rows // chunks
    vmem = pl.BlockSpec(memory_space=pltpu.VMEM)
    smem = pl.BlockSpec(memory_space=pltpu.SMEM)
    kernel = functools.partial(
        phonon_kernel,
        [far for far, _ in pieces],
        shifts.shape[0],
        number * size,
        size,
        True,
        1.0 / math.sqrt(B),
    )
    operands = [shifts, at, contact, columns, lines, *[piece for _, piece in pieces]]
    specs = [smem, smem] + [vmem] * (3 + len(pieces))
    shapes = [jax.ShapeDtypeStruct(contact.shape, F32)]
    out_specs = [pl.BlockSpec((2, 1, size, B), lambda i: (0, 0, number, 0))]
    aliases = {}
    if so_far is not None:
        kernel = functools.partial(skip_kernel, len(operands), kernel)
        aliases[len(operands)] = 0
        operands.append(so_far)
        specs.append(pl.BlockSpec(memory_space=pl.ANY))
    if ends is not None:
        upper, above = ends
        tail = pl.BlockSpec((2, 1, B, B), lambda i: (0, 0, rows // B - 1, 0))
        aliases[len(operands)] = 1
        operands += [upper, above]
        specs += [tail, vmem]
        shapes.append(jax.ShapeDtypeStruct(upper.shape, F32))
        out_specs.append(tail)
    return pl.pallas_call(
        kernel,
        grid=(1,),
        in_specs=specs,
        out_specs=out_specs,
        out_shape=shapes,
        input_output_aliases=aliases,
        compiler_params=pltpu.CompilerParams(vmem_limit_bytes=VMEM_BYTES),
        cost_estimate=pl.CostEstimate(
            flops=size * B * 20, bytes_accessed=8 * size * B * 5, transcendentals=0
        ),
    )(*operands)


def cut_kernel(contact_ref, *refs):
    outs, sems = refs[:-1], refs[-1]
    copies = []
    start = 0
    for number, ref in enumerate(outs):
        size = ref.shape[2]
        at = 0 if number == len(outs) - 1 else start
        start += size
        copies.append(
            pltpu.make_async_copy(contact_ref.at[:, :, pl.ds(at, size)], ref, sems.at[number])
        )
    for copy in copies:
        copy.start()
    for copy in copies:
        copy.wait()


def cut(contact, chunks):
    parts, energies, rows = contact.shape[:3]
    part = jax.ShapeDtypeStruct((parts, energies, rows // chunks, B), F32)
    vmem = pl.BlockSpec(memory_space=pltpu.VMEM)
    return pl.pallas_call(
        cut_kernel,
        in_specs=[pl.BlockSpec(memory_space=pltpu.HBM)],
        out_specs=[vmem] * (chunks + 1),
        out_shape=[part] * chunks + [jax.ShapeDtypeStruct(contact.shape, F32)],
        scratch_shapes=[pltpu.SemaphoreType.DMA((chunks + 1,))],
        compiler_params=pltpu.CompilerParams(vmem_limit_bytes=VMEM_BYTES),
        cost_estimate=pl.CostEstimate(
            flops=0, bytes_accessed=32 * rows * B, transcendentals=0
        ),
        name="cut",
    )(contact)


def edge_rows(retarded, pan):
    rows, columns = retarded.shape[2:]
    devices = lax.axis_size("pan")
    middle = devices // 2
    up_start = (pan + 1 >= middle).astype(jnp.int32)
    down_start = (pan < middle).astype(jnp.int32)
    found, cuts = [], []
    for odd in (0, 1):
        up = pan % 2 == odd
        row = jnp.where(up, rows - B, 0)
        column = jnp.where(up, up_start, down_start) * (columns // 2)
        part = lax.dynamic_slice(retarded, (0, 0, row, column), (2, 1, B, columns // 2))
        pairs = []
        for i in range(odd, devices - 1, 2):
            pairs += [(i, i + 1), (i + 1, i)]
        cuts.append(part)
        found.append(lax.ppermute(part, "pan", pairs))
    return found, cuts


def gathered(near, chunks):
    size = chunks[0].shape[2] // B
    parts = [(i * size, chunk) for i, chunk in enumerate(chunks)]
    first = lax.axis_size("pan") // 2
    pieces = [(0, near)]
    bit = first
    while bit:
        found = []
        for far, piece in pieces:
            if bit == first:
                piece = parts
            sent = []
            for start, block in piece:
                sent.append((start, swapped(block, "pan", bit)))
            found.append((far ^ bit, sent))
        pieces += found
        bit //= 2
    return pieces


def body(retarded, contact, atom_kind, coupling, shifts):
    rows = retarded.shape[2]
    local = rows // B
    chunks = 2 if local % 2 == 0 else 1
    high = lax.axis_size("pan") // 2
    pan = lax.axis_index("pan").astype(jnp.int32)
    energy = lax.axis_index("en").astype(jnp.int32)
    at = jnp.where(jnp.arange(2, dtype=jnp.int32) == 0, pan, energy)
    atoms = rows // ORB
    kinds = lax.dynamic_slice_in_dim(atom_kind, pan * atoms, atoms, 0)
    per_atom = sum(
        jnp.where(kinds[:, None] == kind, coupling[kind][None, :], 0.0)
        for kind in range(coupling.shape[0])
    )
    per_row = jnp.repeat(per_atom, ORB, axis=0)
    per_line = jnp.repeat(per_atom.T, ORB, axis=1)
    edges, cuts = edge_rows(retarded, pan)
    *parts, copied = cut(contact, chunks)
    near = [(0, contact)]
    for rounds in range(ITERS):
        final = rounds == ITERS - 1
        pieces = gathered(near, parts)
        if rounds == 0:
            ready = lax.optimization_barrier((copied, per_row, per_line, *cuts))
            pieces[0] = (0, [(0, ready[0])])
            copied, per_row, per_line = ready[:3]
        groups = [(far, 0, blocks) for far, blocks in pieces[:-1]]
        groups.sort(key=lambda group: (group[0] != 0, group[0] >= high))
        if chunks > 1 and high > 1:
            far, _, blocks = groups.pop([far for far, _, _ in groups].index(high))
            groups.insert(1, (far, 0, blocks[:1]))
            groups.append((far, 1, blocks[1:]))
        sums = {}
        for far, number, blocks in groups:
            work = ("diag", "upper") if final else ("diag",)
            if final and 0 < far < high:
                work += ("over", "back")
            sums = panel(at, retarded, far, blocks, sums, edges, work, False)
            if final and far == 0:
                held = blocks
        if final:
            sums = panel(at, retarded, 0, held, sums, edges, ("over", "back"), False)
        far, blocks = pieces[-1]
        for number, block in enumerate(blocks):
            last = number == len(blocks) - 1
            new = panel(
                at, retarded, far, [block], sums, edges, ("diag",), last, chunks, final and last
            )
            sums = dict(sums, **new)
        found = spread(sums["diag"][:chunks], "en")
        settings = (shifts, at, copied, per_row, per_line)
        if not final:
            parts = [phonon(*settings, own[1:], number, chunks) for number, own in enumerate(found)]
            near = [(i * (local // chunks), part) for i, part in enumerate(parts)]
    devices = lax.axis_size("pan")
    above = lax.ppermute(sums["back"], "pan", [(i + 1, i) for i in range(devices - 1)])
    for far, blocks in pieces[1:-1]:
        if far >= high:
            sums = panel(at, retarded, far, blocks, sums, edges, ("over",), False)
    far, blocks = pieces[-1]
    upper = panel(at, retarded, far, blocks, sums, edges, ("upper", "over"), True)["upper"]
    sigma = None
    for number, own in enumerate(found):
        ends = (upper, above) if number == 0 else None
        sigma, *more = phonon_final(*settings, own[1:], number, chunks, sigma, ends)
        if more:
            (lesser_upper,) = more
    return (sums["diag"][chunks], lesser_upper, sigma)


def solution(mesh):
    def step(retarded, *args):
        spread_spec = P(None, ("grp", "en"), "pan", None)
        inner = jax.shard_map(
            body,
            mesh=mesh,
            in_specs=(spread_spec, spread_spec, P(), P(), P()),
            out_specs=(spread_spec, spread_spec, spread_spec),
            check_vma=False,
        )
        return inner(retarded, *args)

    return step
```

```python
import functools
import math

import jax
import jax.numpy as jnp
from jax import lax
from jax.experimental import pallas as pl
from jax.experimental.pallas import tpu as pltpu
from jax.sharding import PartitionSpec as P


B = 128
ORB = 8
ITERS = 2
VMEM_BYTES = 28 * 2**20

F32 = jnp.float32
BF16 = jnp.bfloat16


def swapped(x, axis, bit):
    return lax.ppermute(x, axis, [(i, i ^ bit) for i in range(lax.axis_size(axis))])


def spread(chunks, axis):
    pieces = [[(0, chunk)] for chunk in chunks]
    bit = lax.axis_size(axis) // 2
    while bit:
        for own in pieces:
            found = []
            for far, piece in own:
                found.append((far ^ bit, swapped(piece, axis, bit)))
            own += found
        bit //= 2
    return pieces


def split(x):
    high = x.astype(BF16)
    return high, (x - high.astype(F32)).astype(BF16)


def dot(a, b):
    return jnp.dot(a, b, preferred_element_type=F32)


def dot_t(a, b):
    return lax.dot_general(a, b, (((1,), (1,)), ((), ())), preferred_element_type=F32)


def times(a, b):
    return dot(a[0], b[0]) + (dot(a[1], b[0]) + dot(a[0], b[1]))


def total(terms):
    return functools.reduce(lambda a, b: a + b, terms)


def rows_of(x, start, size):
    return tuple(v[start : start + size] for v in x)


def halves(x):
    return tuple(v[:, :B] for v in x), tuple(v[:, B:] for v in x)


def stacked(blocks):
    blocks = [halves(block) for block in blocks]
    return tuple(
        jnp.concatenate(
            [jnp.concatenate([block[j][part] for block in blocks], axis=1) for j in range(2)], axis=0
        )
        for part in range(2)
    )


def against(lefts, rights):
    terms = []
    for i in range(0, len(lefts), 2):
        left, right = stacked(lefts[i : i + 2]), stacked(rights[i : i + 2])
        terms += [dot_t(left[0], right[0]), dot_t(left[1], right[0]), dot_t(left[0], right[1])]
    both = total(terms)
    rows = both.shape[0] // 2
    re, im = both[:rows], both[rows:]
    return jnp.concatenate([re[:, :B] + im[:, B:], re[:, B:] - im[:, :B]], axis=1)


def panel_kernel(local, far, starts, kinds, first, last, chunks, devices, scale, *refs):
    refs = list(refs)
    at_ref, g_ref = refs[:2]
    piece_refs, refs = refs[2 : 2 + len(starts)], refs[2 + len(starts) :]
    edges = "over" in kinds or "back" in kinds
    if edges:
        even_ref, odd_ref = refs[:2]
        refs = refs[2:]
    ins = {}
    for kind in kinds:
        if kind not in first:
            ins[kind] = refs.pop(0)
    outs = refs if last else dict(zip(kinds, refs))
    pan = at_ref[0]
    source = pan ^ far
    middle = devices // 2
    half = devices * local // 2
    whole = "diag" in kinds or "upper" in kinds
    low = 0 if whole else (local - 1) * B

    greens, sigmas, products, columns = [], [], [], []
    for start, s_ref in zip(starts, piece_refs):
        for u in range(s_ref.shape[2] // B):
            k = source * local + start + u
            columns.append(pl.ds(pl.multiple_of((k % half) * B, B), B))
            cut = pl.ds(pl.multiple_of(k * B, B), B)
            rows = slice(u * B, (u + 1) * B)
            sr, si = s_ref[0, 0, rows], s_ref[1, 0, rows]
            sigmas.append(
                split(
                    jnp.concatenate(
                        [jnp.concatenate([sr, si], axis=1), jnp.concatenate([-si, sr], axis=1)],
                        axis=0,
                    )
                )
            )
            greens.append(lambda low, high, cut=cut: split(
                jnp.concatenate([g_ref[0, 0, low:high, cut], g_ref[1, 0, low:high, cut]], axis=1)
            ))
            if whole:
                greens[-1] = functools.partial(
                    lambda whole, low, high: rows_of(whole, low, high - low),
                    greens[-1](0, local * B),
                )
                products.append(split(times(greens[-1](0, local * B), sigmas[-1])))

    def old(kind, i):
        return ins[kind][i] if kind in ins else 0.0

    def put(ref, row, value):
        ref[0, 0, row * B : (row + 1) * B] = value[:, :B].T * scale
        ref[1, 0, row * B : (row + 1) * B] = value[:, B:].T * scale

    diag, upper = "diag" in kinds, "upper" in kinds
    for i in range(local):
        start = 0 if diag else 1
        size = int(diag) + int(upper and i < local - 1)
        if not size:
            continue
        terms = against(
            [green((i + start) * B, (i + start + size) * B) for green in greens],
            [rows_of(product, i * B, B) for product in products],
        )
        if diag:
            value = old("diag", i) + terms[:B]
            if last:
                for ref in outs[chunks:]:
                    put(ref, i, value)
                put(outs[i * chunks // local], i % (local // chunks), value)
            else:
                outs["diag"][i] = value
        if upper and i < local - 1:
            value = old("upper", i) + terms[-B:]
            if last:
                put(outs[0], i, value)
            else:
                outs["upper"][i] = value
    if edges:
        source_high = source >= middle
        even = pan % 2 == 0

        def edge(near, column):
            return split(
                jnp.concatenate(
                    [
                        jnp.where(near, even_ref[j, 0, :, column], odd_ref[j, 0, :, column])
                        for j in range(2)
                    ],
                    axis=1,
                )
            )

        def over_terms():
            rights = []
            for number in range(len(columns)):
                if whole:
                    rights.append(rows_of(products[number], (local - 1) * B, B))
                else:
                    rights.append(split(times(greens[number](low, local * B), sigmas[number])))
            return against([edge(even, column) for column in columns], rights)

        def back_terms():
            return against(
                [green(0, B) for green in greens],
                [
                    split(times(edge(jnp.logical_not(even), column), sigma))
                    for sigma, column in zip(sigmas, columns)
                ],
            )

        if "over" in kinds:
            theirs = source_high != (pan + 1 >= middle)
            if last:
                end = outs[0]

                @pl.when(theirs)
                def _():
                    put(end, local - 1, old("over", 0) + over_terms())

                @pl.when(jnp.logical_not(theirs))
                def _():
                    put(end, local - 1, jnp.zeros((B, 2 * B), F32) + old("over", 0))

            else:
                if "over" not in ins:
                    outs["over"][0] = jnp.zeros((B, 2 * B), F32)

                @pl.when(theirs)
                def _():
                    outs["over"][0] += over_terms()

        if "back" in kinds:
            if "back" not in ins:
                outs["back"][0] = jnp.zeros((B, 2 * B), F32)

            @pl.when(source_high == (pan >= middle))
            def _():
                outs["back"][0] += back_terms()


def panel(at, green, far, pieces, carry, edges, kinds, last, chunks=1, whole=False):
    rows = green.shape[2]
    local = rows // B
    devices = lax.axis_size("pan")
    counts = {"diag": local, "upper": local - 1, "over": 1, "back": 1}
    kinds = tuple(kind for kind in kinds if counts[kind])
    vmem = pl.BlockSpec(memory_space=pltpu.VMEM)
    starts, many = [], 0
    for start, piece in pieces:
        starts.append(start)
        many += piece.shape[2] // B
    operands = [at, green] + [piece for _, piece in pieces]
    if "over" in kinds or "back" in kinds:
        operands += edges
    shapes = {kind: jax.ShapeDtypeStruct((counts[kind], B, 2 * B), F32) for kind in kinds}
    aliases = {}
    first = []
    for number, kind in enumerate(kinds):
        if kind not in carry:
            first.append(kind)
            continue
        if not last:
            aliases[len(operands)] = number
        operands.append(carry[kind])
    if last:
        tall = jax.ShapeDtypeStruct((2, 1, rows, B), F32)
        shapes = {"upper": tall}
        if "diag" in kinds:
            part = jax.ShapeDtypeStruct((2, 1, rows // chunks, B), F32)
            shapes = {number: part for number in range(chunks)}
            if whole:
                shapes["whole"] = tall
    full = "diag" in kinds or "upper" in kinds
    work = 3 * 2 * (2 * B) * (2 * B) * many * (rows if full else B) * (1 + len(kinds))
    out = pl.pallas_call(
        functools.partial(
            panel_kernel,
            local,
            far,
            starts,
            kinds,
            first,
            last,
            chunks,
            devices,
            1.0 / math.sqrt(B),
        ),
        in_specs=[pl.BlockSpec(memory_space=pltpu.SMEM)] + [vmem] * (len(operands) - 1),
        out_specs=[vmem] * len(shapes),
        out_shape=list(shapes.values()),
        input_output_aliases=aliases,
        compiler_params=pltpu.CompilerParams(vmem_limit_bytes=VMEM_BYTES),
        cost_estimate=pl.CostEstimate(
            flops=work, bytes_accessed=8 * rows * B * many, transcendentals=0
        ),
    )(*operands)
    if last:
        return {"diag": out} if "diag" in kinds else {"upper": out[0]}
    return dict(carry, **dict(zip(kinds, out)))


def phonon_kernel(fars, modes, row, size, final, scale, shift_ref, at_ref, contact_ref, *refs):
    col_ref, row_ref = refs[:2]
    piece_refs, refs = refs[2 : 2 + len(fars)], refs[2 + len(fars) :]
    energy = at_ref[1]
    chosen = []
    for far in fars:
        apart = jnp.abs((energy ^ far) - energy)
        chosen.append([jnp.where(apart == shift_ref[m], 1.0, 0.0).astype(F32) for m in range(modes)])
    out_ref = refs[-2] if final and len(refs) > 2 else refs[-1]
    for start in range(0, size, B):
        rows = slice(row + start, row + start + B)
        here = slice(start, start + B)
        outer = [col_ref[rows, m : m + 1] * row_ref[m : m + 1, rows] for m in range(modes)]
        values = [contact_ref[0, 0, rows], contact_ref[1, 0, rows]]
        for weights, ref in zip(chosen, piece_refs):
            weight = total(w * o for w, o in zip(weights, outer))
            values = [value + weight * ref[j, 0, here] for j, value in enumerate(values)]
        for j in range(2):
            out_ref[j, 0, here] = values[j]
    if final and len(refs) > 2:
        upper_ref, above_ref = refs[:2]
        for j in range(2):
            more = above_ref[0, :, j * B : (j + 1) * B].T * scale
            refs[-1][j, 0] = upper_ref[j, 0] + more


def phonon(shifts, at, contact, columns, lines, pieces, number, chunks):
    parts, energies, rows = contact.shape[:3]
    size = rows // chunks
    vmem = pl.BlockSpec(memory_space=pltpu.VMEM)
    smem = pl.BlockSpec(memory_space=pltpu.SMEM)
    return pl.pallas_call(
        functools.partial(
            phonon_kernel,
            [far for far, _ in pieces],
            shifts.shape[0],
            number * size,
            size,
            False,
            1.0,
        ),
        in_specs=[smem, smem] + [vmem] * (3 + len(pieces)),
        out_specs=vmem,
        out_shape=jax.ShapeDtypeStruct((parts, energies, size, B), F32),
        compiler_params=pltpu.CompilerParams(vmem_limit_bytes=VMEM_BYTES),
        cost_estimate=pl.CostEstimate(
            flops=size * B * 20, bytes_accessed=8 * size * B * 5, transcendentals=0
        ),
    )(shifts, at, contact, columns, lines, *[piece for _, piece in pieces])


def skip_kernel(count, kernel, *refs):
    kernel(*refs[:count], *refs[count + 1 :])


def phonon_final(shifts, at, contact, columns, lines, pieces, number, chunks, so_far, ends):
    rows = contact.shape[2]
    size = rows // chunks
    vmem = pl.BlockSpec(memory_space=pltpu.VMEM)
    smem = pl.BlockSpec(memory_space=pltpu.SMEM)
    kernel = functools.partial(
        phonon_kernel,
        [far for far, _ in pieces],
        shifts.shape[0],
        number * size,
        size,
        True,
        1.0 / math.sqrt(B),
    )
    operands = [shifts, at, contact, columns, lines, *[piece for _, piece in pieces]]
    specs = [smem, smem] + [vmem] * (3 + len(pieces))
    shapes = [jax.ShapeDtypeStruct(contact.shape, F32)]
    out_specs = [pl.BlockSpec((2, 1, size, B), lambda i: (0, 0, number, 0))]
    aliases = {}
    if so_far is not None:
        kernel = functools.partial(skip_kernel, len(operands), kernel)
        aliases[len(operands)] = 0
        operands.append(so_far)
        specs.append(pl.BlockSpec(memory_space=pl.ANY))
    if ends is not None:
        upper, above = ends
        tail = pl.BlockSpec((2, 1, B, B), lambda i: (0, 0, rows // B - 1, 0))
        aliases[len(operands)] = 1
        operands += [upper, above]
        specs += [tail, vmem]
        shapes.append(jax.ShapeDtypeStruct(upper.shape, F32))
        out_specs.append(tail)
    return pl.pallas_call(
        kernel,
        grid=(1,),
        in_specs=specs,
        out_specs=out_specs,
        out_shape=shapes,
        input_output_aliases=aliases,
        compiler_params=pltpu.CompilerParams(vmem_limit_bytes=VMEM_BYTES),
        cost_estimate=pl.CostEstimate(
            flops=size * B * 20, bytes_accessed=8 * size * B * 5, transcendentals=0
        ),
    )(*operands)


def cut_kernel(contact_ref, *refs):
    outs, sems = refs[:-1], refs[-1]
    copies = []
    start = 0
    for number, ref in enumerate(outs):
        size = ref.shape[2]
        at = 0 if number == len(outs) - 1 else start
        start += size
        copies.append(
            pltpu.make_async_copy(contact_ref.at[:, :, pl.ds(at, size)], ref, sems.at[number])
        )
    for copy in copies:
        copy.start()
    for copy in copies:
        copy.wait()


def cut(contact, chunks):
    parts, energies, rows = contact.shape[:3]
    part = jax.ShapeDtypeStruct((parts, energies, rows // chunks, B), F32)
    vmem = pl.BlockSpec(memory_space=pltpu.VMEM)
    return pl.pallas_call(
        cut_kernel,
        in_specs=[pl.BlockSpec(memory_space=pltpu.HBM)],
        out_specs=[vmem] * (chunks + 1),
        out_shape=[part] * chunks + [jax.ShapeDtypeStruct(contact.shape, F32)],
        scratch_shapes=[pltpu.SemaphoreType.DMA((chunks + 1,))],
        compiler_params=pltpu.CompilerParams(vmem_limit_bytes=VMEM_BYTES),
        cost_estimate=pl.CostEstimate(
            flops=0, bytes_accessed=32 * rows * B, transcendentals=0
        ),
        name="cut",
    )(contact)


def edge_rows(retarded, pan):
    rows, columns = retarded.shape[2:]
    devices = lax.axis_size("pan")
    middle = devices // 2
    up_start = (pan + 1 >= middle).astype(jnp.int32)
    down_start = (pan < middle).astype(jnp.int32)
    found, cuts = [], []
    for odd in (0, 1):
        up = pan % 2 == odd
        row = jnp.where(up, rows - B, 0)
        column = jnp.where(up, up_start, down_start) * (columns // 2)
        part = lax.dynamic_slice(retarded, (0, 0, row, column), (2, 1, B, columns // 2))
        pairs = []
        for i in range(odd, devices - 1, 2):
            pairs += [(i, i + 1), (i + 1, i)]
        cuts.append(part)
        found.append(lax.ppermute(part, "pan", pairs))
    return found, cuts


def gathered(near, chunks):
    size = chunks[0].shape[2] // B
    parts = [(i * size, chunk) for i, chunk in enumerate(chunks)]
    first = lax.axis_size("pan") // 2
    pieces = [(0, near)]
    bit = first
    while bit:
        found = []
        for far, piece in pieces:
            if bit == first:
                piece = parts
            sent = []
            for start, block in piece:
                sent.append((start, swapped(block, "pan", bit)))
            found.append((far ^ bit, sent))
        pieces += found
        bit //= 2
    return pieces


def body(retarded, contact, atom_kind, coupling, shifts):
    rows = retarded.shape[2]
    local = rows // B
    chunks = 2 if local % 2 == 0 else 1
    high = lax.axis_size("pan") // 2
    pan = lax.axis_index("pan").astype(jnp.int32)
    energy = lax.axis_index("en").astype(jnp.int32)
    at = jnp.where(jnp.arange(2, dtype=jnp.int32) == 0, pan, energy)
    atoms = rows // ORB
    kinds = lax.dynamic_slice_in_dim(atom_kind, pan * atoms, atoms, 0)
    per_atom = sum(
        jnp.where(kinds[:, None] == kind, coupling[kind][None, :], 0.0)
        for kind in range(coupling.shape[0])
    )
    per_row = jnp.repeat(per_atom, ORB, axis=0)
    per_line = jnp.repeat(per_atom.T, ORB, axis=1)
    edges, cuts = edge_rows(retarded, pan)
    *parts, copied = cut(contact, chunks)
    near = [(0, contact)]
    for rounds in range(ITERS):
        final = rounds == ITERS - 1
        pieces = gathered(near, parts)
        if rounds == 0:
            ready = lax.optimization_barrier((copied, per_row, per_line, *cuts))
            pieces[0] = (0, [(0, ready[0])])
            copied, per_row, per_line = ready[:3]
        groups = [(far, 0, blocks) for far, blocks in pieces[:-1]]
        groups.sort(key=lambda group: (group[0] != 0, group[0] >= high))
        if chunks > 1 and high > 1:
            far, _, blocks = groups.pop([far for far, _, _ in groups].index(high))
            groups.insert(1, (far, 0, blocks[:1]))
            groups.append((far, 1, blocks[1:]))
        sums = {}
        for far, number, blocks in groups:
            work = ("diag", "upper") if final else ("diag",)
            if final and 0 < far < high:
                work += ("over", "back")
            sums = panel(at, retarded, far, blocks, sums, edges, work, False)
            if final and far == 0:
                held = blocks
        if final:
            sums = panel(at, retarded, 0, held, sums, edges, ("over", "back"), False)
        far, blocks = pieces[-1]
        for number, block in enumerate(blocks):
            last = number == len(blocks) - 1
            new = panel(
                at, retarded, far, [block], sums, edges, ("diag",), last, chunks, final and last
            )
            sums = dict(sums, **new)
        found = spread(sums["diag"][:chunks], "en")
        settings = (shifts, at, copied, per_row, per_line)
        if not final:
            parts = [phonon(*settings, own[1:], number, chunks) for number, own in enumerate(found)]
            near = [(i * (local // chunks), part) for i, part in enumerate(parts)]
    devices = lax.axis_size("pan")
    above = lax.ppermute(sums["back"], "pan", [(i + 1, i) for i in range(devices - 1)])
    for far, blocks in pieces[1:-1]:
        if far >= high:
            sums = panel(at, retarded, far, blocks, sums, edges, ("over",), False)
    far, blocks = pieces[-1]
    upper = panel(at, retarded, far, blocks, sums, edges, ("upper", "over"), True)["upper"]
    sigma = None
    for number, own in enumerate(found):
        ends = (upper, above) if number == 0 else None
        sigma, *more = phonon_final(*settings, own[1:], number, chunks, sigma, ends)
        if more:
            (lesser_upper,) = more
    return (sums["diag"][chunks], lesser_upper, sigma)


def solution(mesh):
    def step(retarded, *args):
        spread_spec = P(None, ("grp", "en"), "pan", None)
        inner = jax.shard_map(
            body,
            mesh=mesh,
            in_specs=(spread_spec, spread_spec, P(), P(), P()),
            out_specs=(spread_spec, spread_spec, spread_spec),
            check_vma=False,
        )
        return inner(retarded, *args)

    return step
```

```python
import functools
import math

import jax
import jax.numpy as jnp
from jax import lax
from jax.experimental import pallas as pl
from jax.experimental.pallas import tpu as pltpu
from jax.sharding import PartitionSpec as P


B = 128
ORB = 8
ITERS = 2
VMEM_BYTES = 28 * 2**20

F32 = jnp.float32
BF16 = jnp.bfloat16


def swapped(x, axis, bit):
    return lax.ppermute(x, axis, [(i, i ^ bit) for i in range(lax.axis_size(axis))])


def spread(chunks, axis):
    pieces = [[(0, chunk)] for chunk in chunks]
    bit = lax.axis_size(axis) // 2
    while bit:
        for own in pieces:
            found = []
            for far, piece in own:
                found.append((far ^ bit, swapped(piece, axis, bit)))
            own += found
        bit //= 2
    return pieces


def split(x):
    high = x.astype(BF16)
    return high, (x - high.astype(F32)).astype(BF16)


def dot(a, b):
    return jnp.dot(a, b, preferred_element_type=F32)


def dot_t(a, b):
    return lax.dot_general(a, b, (((1,), (1,)), ((), ())), preferred_element_type=F32)


def times(a, b):
    return dot(a[0], b[0]) + (dot(a[1], b[0]) + dot(a[0], b[1]))


def total(terms):
    return functools.reduce(lambda a, b: a + b, terms)


def rows_of(x, start, size):
    return tuple(v[start : start + size] for v in x)


def halves(x):
    return tuple(v[:, :B] for v in x), tuple(v[:, B:] for v in x)


def stacked(blocks):
    blocks = [halves(block) for block in blocks]
    return tuple(
        jnp.concatenate(
            [jnp.concatenate([block[j][part] for block in blocks], axis=1) for j in range(2)], axis=0
        )
        for part in range(2)
    )


def against(lefts, rights):
    terms = []
    for i in range(0, len(lefts), 2):
        left, right = stacked(lefts[i : i + 2]), stacked(rights[i : i + 2])
        terms += [dot_t(left[0], right[0]), dot_t(left[1], right[0]), dot_t(left[0], right[1])]
    both = total(terms)
    rows = both.shape[0] // 2
    re, im = both[:rows], both[rows:]
    return jnp.concatenate([re[:, :B] + im[:, B:], re[:, B:] - im[:, :B]], axis=1)


def panel_kernel(local, far, starts, kinds, first, last, chunks, devices, scale, *refs):
    refs = list(refs)
    at_ref, g_ref = refs[:2]
    piece_refs, refs = refs[2 : 2 + len(starts)], refs[2 + len(starts) :]
    edges = "over" in kinds or "back" in kinds
    if edges:
        even_ref, odd_ref = refs[:2]
        refs = refs[2:]
    ins = {}
    for kind in kinds:
        if kind not in first:
            ins[kind] = refs.pop(0)
    outs = refs if last else dict(zip(kinds, refs))
    pan = at_ref[0]
    source = pan ^ far
    middle = devices // 2
    half = devices * local // 2
    whole = "diag" in kinds or "upper" in kinds
    low = 0 if whole else (local - 1) * B

    greens, sigmas, products, columns = [], [], [], []
    for start, s_ref in zip(starts, piece_refs):
        for u in range(s_ref.shape[2] // B):
            k = source * local + start + u
            columns.append(pl.ds(pl.multiple_of((k % half) * B, B), B))
            cut = pl.ds(pl.multiple_of(k * B, B), B)
            rows = slice(u * B, (u + 1) * B)
            sr, si = s_ref[0, 0, rows], s_ref[1, 0, rows]
            sigmas.append(
                split(
                    jnp.concatenate(
                        [jnp.concatenate([sr, si], axis=1), jnp.concatenate([-si, sr], axis=1)],
                        axis=0,
                    )
                )
            )
            greens.append(lambda low, high, cut=cut: split(
                jnp.concatenate([g_ref[0, 0, low:high, cut], g_ref[1, 0, low:high, cut]], axis=1)
            ))
            if whole:
                greens[-1] = functools.partial(
                    lambda whole, low, high: rows_of(whole, low, high - low),
                    greens[-1](0, local * B),
                )
                products.append(split(times(greens[-1](0, local * B), sigmas[-1])))

    def old(kind, i):
        return ins[kind][i] if kind in ins else 0.0

    def put(ref, row, value):
        ref[0, 0, row * B : (row + 1) * B] = value[:, :B].T * scale
        ref[1, 0, row * B : (row + 1) * B] = value[:, B:].T * scale

    diag, upper = "diag" in kinds, "upper" in kinds
    for i in range(local):
        start = 0 if diag else 1
        size = int(diag) + int(upper and i < local - 1)
        if not size:
            continue
        terms = against(
            [green((i + start) * B, (i + start + size) * B) for green in greens],
            [rows_of(product, i * B, B) for product in products],
        )
        if diag:
            value = old("diag", i) + terms[:B]
            if last:
                for ref in outs[chunks:]:
                    put(ref, i, value)
                put(outs[i * chunks // local], i % (local // chunks), value)
            else:
                outs["diag"][i] = value
        if upper and i < local - 1:
            value = old("upper", i) + terms[-B:]
            if last:
                put(outs[0], i, value)
            else:
                outs["upper"][i] = value
    if edges:
        source_high = source >= middle
        even = pan % 2 == 0

        def edge(near, column):
            return split(
                jnp.concatenate(
                    [
                        jnp.where(near, even_ref[j, 0, :, column], odd_ref[j, 0, :, column])
                        for j in range(2)
                    ],
                    axis=1,
                )
            )

        def over_terms():
            rights = []
            for number in range(len(columns)):
                if whole:
                    rights.append(rows_of(products[number], (local - 1) * B, B))
                else:
                    rights.append(split(times(greens[number](low, local * B), sigmas[number])))
            return against([edge(even, column) for column in columns], rights)

        def back_terms():
            return against(
                [green(0, B) for green in greens],
                [
                    split(times(edge(jnp.logical_not(even), column), sigma))
                    for sigma, column in zip(sigmas, columns)
                ],
            )

        if "over" in kinds:
            theirs = source_high != (pan + 1 >= middle)
            if last:
                end = outs[1]

                @pl.when(theirs)
                def _():
                    put(end, 0, old("over", 0) + over_terms())

                @pl.when(jnp.logical_not(theirs))
                def _():
                    put(end, 0, jnp.zeros((B, 2 * B), F32) + old("over", 0))

            else:
                if "over" not in ins:
                    outs["over"][0] = jnp.zeros((B, 2 * B), F32)

                @pl.when(theirs)
                def _():
                    outs["over"][0] += over_terms()

        if "back" in kinds:
            if "back" not in ins:
                outs["back"][0] = jnp.zeros((B, 2 * B), F32)

            @pl.when(source_high == (pan >= middle))
            def _():
                outs["back"][0] += back_terms()


def panel(at, green, far, pieces, carry, edges, kinds, last, chunks=1, whole=False):
    rows = green.shape[2]
    local = rows // B
    devices = lax.axis_size("pan")
    counts = {"diag": local, "upper": local - 1, "over": 1, "back": 1}
    kinds = tuple(kind for kind in kinds if counts[kind])
    vmem = pl.BlockSpec(memory_space=pltpu.VMEM)
    starts, many = [], 0
    for start, piece in pieces:
        starts.append(start)
        many += piece.shape[2] // B
    operands = [at, green] + [piece for _, piece in pieces]
    if "over" in kinds or "back" in kinds:
        operands += edges
    shapes = {kind: jax.ShapeDtypeStruct((counts[kind], B, 2 * B), F32) for kind in kinds}
    aliases = {}
    first = []
    for number, kind in enumerate(kinds):
        if kind not in carry:
            first.append(kind)
            continue
        if not last:
            aliases[len(operands)] = number
        operands.append(carry[kind])
    if last:
        tall = jax.ShapeDtypeStruct((2, 1, rows, B), F32)
        shapes = {"upper": tall, "over": jax.ShapeDtypeStruct((2, 1, B, B), F32)}
        if "diag" in kinds:
            part = jax.ShapeDtypeStruct((2, 1, rows // chunks, B), F32)
            shapes = {number: part for number in range(chunks)}
            if whole:
                shapes["whole"] = tall
    full = "diag" in kinds or "upper" in kinds
    work = 3 * 2 * (2 * B) * (2 * B) * many * (rows if full else B) * (1 + len(kinds))
    out = pl.pallas_call(
        functools.partial(panel_kernel, local, far, starts, kinds, first, last, chunks, devices, 1.0 / math.sqrt(B)),
        in_specs=[pl.BlockSpec(memory_space=pltpu.SMEM)] + [vmem] * (len(operands) - 1),
        out_specs=[vmem] * len(shapes),
        out_shape=list(shapes.values()),
        input_output_aliases=aliases,
        compiler_params=pltpu.CompilerParams(vmem_limit_bytes=VMEM_BYTES),
        cost_estimate=pl.CostEstimate(
            flops=work, bytes_accessed=8 * rows * B * many, transcendentals=0
        ),
    )(*operands)
    if last:
        return {"diag": out} if "diag" in kinds else {"upper": out[0], "over": out[1]}
    return dict(carry, **dict(zip(kinds, out)))


def scattered(fars, modes, row, size, shift_ref, at_ref, contact_ref, col_ref, row_ref, piece_refs):
    energy = at_ref[1]
    chosen = []
    for far in fars:
        apart = jnp.abs((energy ^ far) - energy)
        chosen.append([jnp.where(apart == shift_ref[m], 1.0, 0.0).astype(F32) for m in range(modes)])
    for start in range(0, size, B):
        rows = slice(row + start, row + start + B)
        outer = [col_ref[rows, m : m + 1] * row_ref[m : m + 1, rows] for m in range(modes)]
        values = [contact_ref[0, 0, rows], contact_ref[1, 0, rows]]
        for weights, ref in zip(chosen, piece_refs):
            weight = total(w * o for w, o in zip(weights, outer))
            values = [value + weight * ref[j, 0, start : start + B] for j, value in enumerate(values)]
        yield start, values


def phonon_kernel(fars, modes, row, size, *refs):
    out_ref = refs[-1]
    for start, values in scattered(fars, modes, row, size, *refs[:5], refs[5:-1]):
        for j in range(2):
            out_ref[j, 0, start : start + B] = values[j]


def phonon(shifts, at, contact, columns, lines, pieces, number, chunks):
    parts, energies, rows = contact.shape[:3]
    size = rows // chunks
    vmem = pl.BlockSpec(memory_space=pltpu.VMEM)
    smem = pl.BlockSpec(memory_space=pltpu.SMEM)
    return pl.pallas_call(
        functools.partial(
            phonon_kernel, [far for far, _ in pieces], shifts.shape[0], number * size, size
        ),
        in_specs=[smem, smem] + [vmem] * (3 + len(pieces)),
        out_specs=vmem,
        out_shape=jax.ShapeDtypeStruct((parts, energies, size, B), F32),
        compiler_params=pltpu.CompilerParams(vmem_limit_bytes=VMEM_BYTES),
        cost_estimate=pl.CostEstimate(
            flops=size * B * 20, bytes_accessed=8 * size * B * 5, transcendentals=0
        ),
    )(shifts, at, contact, columns, lines, *[piece for _, piece in pieces])


def ending_kernel(fars, modes, rows, size, scale, *refs):
    settings, refs = refs[:5], refs[5:]
    piece_refs, refs = refs[: len(fars)], refs[len(fars) :]
    row = rows - size
    done_refs, refs = refs[: row // size], refs[row // size :]
    _, over_ref, above_ref, sigma_ref, upper_ref, held, tail, sems = refs
    copies = []

    def send(source, target):
        copies.append(pltpu.make_async_copy(source, target, sems.at[len(copies)]))
        copies[-1].start()

    for number, ref in enumerate(done_refs):
        send(ref, sigma_ref.at[:, :, pl.ds(number * size, size)])
    for j in range(2):
        more = above_ref[0, :, j * B : (j + 1) * B].T * scale
        tail[j, 0] = over_ref[j, 0] + more
    send(tail, upper_ref.at[:, :, pl.ds(rows - B, B)])
    for start, values in scattered(fars, modes, row, size, *settings, piece_refs):
        for j in range(2):
            held[j, 0, start : start + B] = values[j]
        send(held.at[:, :, pl.ds(start, B)], sigma_ref.at[:, :, pl.ds(row + start, B)])
    for copy in copies:
        copy.wait()


def ending(shifts, at, contact, columns, lines, pieces, done, upper, over, above):
    parts, energies, rows = contact.shape[:3]
    size = rows // (len(done) + 1)
    vmem = pl.BlockSpec(memory_space=pltpu.VMEM)
    smem = pl.BlockSpec(memory_space=pltpu.SMEM)
    hbm = pl.BlockSpec(memory_space=pl.ANY)
    operands = [shifts, at, contact, columns, lines, *[piece for _, piece in pieces], *done]
    specs = [smem, smem] + [vmem] * (len(operands) - 2) + [hbm, vmem, vmem]
    return pl.pallas_call(
        functools.partial(ending_kernel, [far for far, _ in pieces], shifts.shape[0], rows, size, 1.0 / math.sqrt(B)),
        in_specs=specs,
        out_specs=[hbm, hbm],
        out_shape=[jax.ShapeDtypeStruct(contact.shape, F32), jax.ShapeDtypeStruct(upper.shape, F32)],
        input_output_aliases={len(operands): 1},
        scratch_shapes=[
            pltpu.VMEM((parts, energies, size, B), F32),
            pltpu.VMEM((parts, energies, B, B), F32),
            pltpu.SemaphoreType.DMA((len(done) + 1 + size // B,)),
        ],
        compiler_params=pltpu.CompilerParams(vmem_limit_bytes=VMEM_BYTES),
        cost_estimate=pl.CostEstimate(
            flops=size * B * 20, bytes_accessed=8 * size * B * 5, transcendentals=0
        ),
    )(*operands, upper, over, above)


def cut_kernel(contact_ref, *refs):
    outs, sems = refs[:-1], refs[-1]
    copies = []
    start = 0
    for number, ref in enumerate(outs):
        size = ref.shape[2]
        at = 0 if number == len(outs) - 1 else start
        start += size
        copies.append(
            pltpu.make_async_copy(contact_ref.at[:, :, pl.ds(at, size)], ref, sems.at[number])
        )
    for copy in copies:
        copy.start()
    for copy in copies:
        copy.wait()


def cut(contact, chunks):
    parts, energies, rows = contact.shape[:3]
    part = jax.ShapeDtypeStruct((parts, energies, rows // chunks, B), F32)
    vmem = pl.BlockSpec(memory_space=pltpu.VMEM)
    return pl.pallas_call(
        cut_kernel,
        in_specs=[pl.BlockSpec(memory_space=pltpu.HBM)],
        out_specs=[vmem] * (chunks + 1),
        out_shape=[part] * chunks + [jax.ShapeDtypeStruct(contact.shape, F32)],
        scratch_shapes=[pltpu.SemaphoreType.DMA((chunks + 1,))],
        compiler_params=pltpu.CompilerParams(vmem_limit_bytes=VMEM_BYTES),
        cost_estimate=pl.CostEstimate(
            flops=0, bytes_accessed=32 * rows * B, transcendentals=0
        ),
        name="cut",
    )(contact)


def edge_rows(retarded, pan):
    rows, columns = retarded.shape[2:]
    devices = lax.axis_size("pan")
    middle = devices // 2
    up_start = (pan + 1 >= middle).astype(jnp.int32)
    down_start = (pan < middle).astype(jnp.int32)
    found, cuts = [], []
    for odd in (0, 1):
        up = pan % 2 == odd
        row = jnp.where(up, rows - B, 0)
        column = jnp.where(up, up_start, down_start) * (columns // 2)
        part = lax.dynamic_slice(retarded, (0, 0, row, column), (2, 1, B, columns // 2))
        pairs = []
        for i in range(odd, devices - 1, 2):
            pairs += [(i, i + 1), (i + 1, i)]
        cuts.append(part)
        found.append(lax.ppermute(part, "pan", pairs))
    return found, cuts


def gathered(near, chunks):
    size = chunks[0].shape[2] // B
    parts = [(i * size, chunk) for i, chunk in enumerate(chunks)]
    first = lax.axis_size("pan") // 2
    pieces = [(0, near)]
    bit = first
    while bit:
        found = []
        for far, piece in pieces:
            if bit == first:
                piece = parts
            sent = []
            for start, block in piece:
                sent.append((start, swapped(block, "pan", bit)))
            found.append((far ^ bit, sent))
        pieces += found
        bit //= 2
    return pieces


def body(retarded, contact, atom_kind, coupling, shifts):
    rows = retarded.shape[2]
    local = rows // B
    chunks = 2 if local % 2 == 0 else 1
    high = lax.axis_size("pan") // 2
    pan = lax.axis_index("pan").astype(jnp.int32)
    energy = lax.axis_index("en").astype(jnp.int32)
    at = jnp.where(jnp.arange(2, dtype=jnp.int32) == 0, pan, energy)
    atoms = rows // ORB
    kinds = lax.dynamic_slice_in_dim(atom_kind, pan * atoms, atoms, 0)
    per_atom = sum(jnp.where(kinds[:, None] == kind, coupling[kind][None, :], 0.0) for kind in range(coupling.shape[0]))
    per_row = jnp.repeat(per_atom, ORB, axis=0)
    per_line = jnp.repeat(per_atom.T, ORB, axis=1)
    edges, cuts = edge_rows(retarded, pan)
    *parts, copied = cut(contact, chunks)
    near = [(0, contact)]
    for rounds in range(ITERS):
        final = rounds == ITERS - 1
        pieces = gathered(near, parts)
        if rounds == 0:
            ready = lax.optimization_barrier((copied, per_row, per_line, *cuts))
            pieces[0] = (0, [(0, ready[0])])
            copied, per_row, per_line = ready[:3]
        groups = [(far, 0, blocks) for far, blocks in pieces[:-1]]
        groups.sort(key=lambda group: (group[0] != 0, group[0] >= high))
        if chunks > 1 and high > 1:
            far, _, blocks = groups.pop([far for far, _, _ in groups].index(high))
            groups.insert(1, (far, 0, blocks[:1]))
            groups.insert(2 if final else len(groups), (far, 1, blocks[1:]))
        sums = {}
        for far, number, blocks in groups:
            work = ("diag", "upper") if final else ("diag",)
            if final and 0 < far < high:
                if "over" not in sums:
                    sums = panel(at, retarded, 0, pieces[0][1], sums, edges, ("over", "back"), False)
                work += ("over", "back")
            sums = panel(at, retarded, far, blocks, sums, edges, work, False)
        far, blocks = pieces[-1]
        for number, block in enumerate(blocks):
            last = number == len(blocks) - 1
            new = panel(at, retarded, far, [block], sums, edges, ("diag",), last, chunks, final and last)
            sums = dict(sums, **new)
        found = spread(sums["diag"][:chunks], "en")
        settings = (shifts, at, copied, per_row, per_line)
        if not final:
            parts = [phonon(*settings, own[1:], number, chunks) for number, own in enumerate(found)]
            near = [(i * (local // chunks), part) for i, part in enumerate(parts)]
    devices = lax.axis_size("pan")
    above = lax.ppermute(sums["back"], "pan", [(i + 1, i) for i in range(devices - 1)])
    for far, blocks in pieces[1:-1]:
        if far >= high:
            sums = panel(at, retarded, far, blocks, sums, edges, ("over",), False)
    far, blocks = pieces[-1]
    ends = panel(at, retarded, far, blocks, sums, edges, ("upper", "over"), True)
    done = [phonon(*settings, own[1:], number, chunks) for number, own in enumerate(found[:-1])]
    sigma, upper = ending(*settings, found[-1][1:], done, ends["upper"], ends["over"], above)
    return (sums["diag"][chunks], upper, sigma)


def solution(mesh):
    def step(retarded, *args):
        spread_spec = P(None, ("grp", "en"), "pan", None)
        inner = jax.shard_map(
            body,
            mesh=mesh,
            in_specs=(spread_spec, spread_spec, P(), P(), P()),
            out_specs=(spread_spec, spread_spec, spread_spec),
            check_vma=False,
        )
        return inner(retarded, *args)

    return step
```

```python
import functools
import math

import jax
import jax.numpy as jnp
from jax import lax
from jax.experimental import pallas as pl
from jax.experimental.pallas import tpu as pltpu
from jax.sharding import PartitionSpec as P


B = 128
ORB = 8
ITERS = 2
VMEM_BYTES = 28 * 2**20

F32 = jnp.float32
BF16 = jnp.bfloat16


def swapped(x, axis, bit):
    return lax.ppermute(x, axis, [(i, i ^ bit) for i in range(lax.axis_size(axis))])


def spread(chunks, axis):
    pieces = [[(0, chunk)] for chunk in chunks]
    bit = lax.axis_size(axis) // 2
    while bit:
        for own in pieces:
            found = []
            for far, piece in own:
                found.append((far ^ bit, swapped(piece, axis, bit)))
            own += found
        bit //= 2
    return pieces


def split(x):
    high = x.astype(BF16)
    return high, (x - high.astype(F32)).astype(BF16)


def dot(a, b):
    return jnp.dot(a, b, preferred_element_type=F32)


def dot_t(a, b):
    return lax.dot_general(a, b, (((1,), (1,)), ((), ())), preferred_element_type=F32)


def times(a, b):
    return dot(a[0], b[0]) + (dot(a[1], b[0]) + dot(a[0], b[1]))


def total(terms):
    return functools.reduce(lambda a, b: a + b, terms)


def rows_of(x, start, size):
    return tuple(v[start : start + size] for v in x)


def halves(x):
    return tuple(v[:, :B] for v in x), tuple(v[:, B:] for v in x)


def stacked(blocks):
    blocks = [halves(block) for block in blocks]
    return tuple(
        jnp.concatenate(
            [jnp.concatenate([block[j][part] for block in blocks], axis=1) for j in range(2)], axis=0
        )
        for part in range(2)
    )


def against(lefts, rights):
    terms = []
    for i in range(0, len(lefts), 2):
        left, right = stacked(lefts[i : i + 2]), stacked(rights[i : i + 2])
        terms += [dot_t(left[0], right[0]), dot_t(left[1], right[0]), dot_t(left[0], right[1])]
    both = total(terms)
    rows = both.shape[0] // 2
    re, im = both[:rows], both[rows:]
    return jnp.concatenate([re[:, :B] + im[:, B:], re[:, B:] - im[:, :B]], axis=1)


def panel_kernel(local, far, starts, kinds, first, last, chunks, devices, scale, *refs):
    refs = list(refs)
    at_ref, g_ref = refs[:2]
    piece_refs, refs = refs[2 : 2 + len(starts)], refs[2 + len(starts) :]
    edges = "over" in kinds or "back" in kinds
    if edges:
        even_ref, odd_ref = refs[:2]
        refs = refs[2:]
    ins = {}
    for kind in kinds:
        if kind not in first:
            ins[kind] = refs.pop(0)
    outs = refs if last else dict(zip(kinds, refs))
    pan = at_ref[0]
    source = pan ^ far
    middle = devices // 2
    half = devices * local // 2
    whole = "diag" in kinds or "upper" in kinds
    low = 0 if whole else (local - 1) * B

    greens, sigmas, products, columns = [], [], [], []
    for start, s_ref in zip(starts, piece_refs):
        for u in range(s_ref.shape[2] // B):
            k = source * local + start + u
            columns.append(pl.ds(pl.multiple_of((k % half) * B, B), B))
            cut = pl.ds(pl.multiple_of(k * B, B), B)
            rows = slice(u * B, (u + 1) * B)
            sr, si = s_ref[0, 0, rows], s_ref[1, 0, rows]
            sigmas.append(
                split(
                    jnp.concatenate(
                        [jnp.concatenate([sr, si], axis=1), jnp.concatenate([-si, sr], axis=1)],
                        axis=0,
                    )
                )
            )
            greens.append(lambda low, high, cut=cut: split(
                jnp.concatenate([g_ref[0, 0, low:high, cut], g_ref[1, 0, low:high, cut]], axis=1)
            ))
            if whole:
                greens[-1] = functools.partial(
                    lambda whole, low, high: rows_of(whole, low, high - low),
                    greens[-1](0, local * B),
                )
                products.append(split(times(greens[-1](0, local * B), sigmas[-1])))

    def old(kind, i):
        return ins[kind][i] if kind in ins else 0.0

    def put(ref, row, value):
        ref[0, 0, row * B : (row + 1) * B] = value[:, :B].T * scale
        ref[1, 0, row * B : (row + 1) * B] = value[:, B:].T * scale

    diag, upper = "diag" in kinds, "upper" in kinds
    for i in range(local):
        start = 0 if diag else 1
        size = int(diag) + int(upper and i < local - 1)
        if not size:
            continue
        terms = against(
            [green((i + start) * B, (i + start + size) * B) for green in greens],
            [rows_of(product, i * B, B) for product in products],
        )
        if diag:
            value = old("diag", i) + terms[:B]
            if last:
                put(outs[i * chunks // local], i % (local // chunks), value)
            else:
                outs["diag"][i] = value
        if upper and i < local - 1:
            value = old("upper", i) + terms[-B:]
            if last:
                put(outs[0], i, value)
            else:
                outs["upper"][i] = value
    if edges:
        source_high = source >= middle
        even = pan % 2 == 0

        def edge(near, column):
            return split(
                jnp.concatenate(
                    [
                        jnp.where(near, even_ref[j, 0, :, column], odd_ref[j, 0, :, column])
                        for j in range(2)
                    ],
                    axis=1,
                )
            )

        def over_terms():
            rights = []
            for number in range(len(columns)):
                if whole:
                    rights.append(rows_of(products[number], (local - 1) * B, B))
                else:
                    rights.append(split(times(greens[number](low, local * B), sigmas[number])))
            return against([edge(even, column) for column in columns], rights)

        def back_terms():
            return against(
                [green(0, B) for green in greens],
                [
                    split(times(edge(jnp.logical_not(even), column), sigma))
                    for sigma, column in zip(sigmas, columns)
                ],
            )

        if "over" in kinds:
            theirs = source_high != (pan + 1 >= middle)
            if last:
                end = outs[1]

                @pl.when(theirs)
                def _():
                    put(end, 0, old("over", 0) + over_terms())

                @pl.when(jnp.logical_not(theirs))
                def _():
                    put(end, 0, jnp.zeros((B, 2 * B), F32) + old("over", 0))

            else:
                if "over" not in ins:
                    outs["over"][0] = jnp.zeros((B, 2 * B), F32)

                @pl.when(theirs)
                def _():
                    outs["over"][0] += over_terms()

        if "back" in kinds:
            if "back" not in ins:
                outs["back"][0] = jnp.zeros((B, 2 * B), F32)

            @pl.when(source_high == (pan >= middle))
            def _():
                outs["back"][0] += back_terms()


def panel(at, green, far, pieces, carry, edges, kinds, last, chunks=1):
    rows = green.shape[2]
    local = rows // B
    devices = lax.axis_size("pan")
    counts = {"diag": local, "upper": local - 1, "over": 1, "back": 1}
    kinds = tuple(kind for kind in kinds if counts[kind])
    vmem = pl.BlockSpec(memory_space=pltpu.VMEM)
    starts, many = [], 0
    for start, piece in pieces:
        starts.append(start)
        many += piece.shape[2] // B
    operands = [at, green] + [piece for _, piece in pieces]
    if "over" in kinds or "back" in kinds:
        operands += edges
    shapes = {kind: jax.ShapeDtypeStruct((counts[kind], B, 2 * B), F32) for kind in kinds}
    aliases = {}
    first = []
    for number, kind in enumerate(kinds):
        if kind not in carry:
            first.append(kind)
            continue
        if not last:
            aliases[len(operands)] = number
        operands.append(carry[kind])
    if last:
        tall = jax.ShapeDtypeStruct((2, 1, rows, B), F32)
        shapes = {"upper": tall, "over": jax.ShapeDtypeStruct((2, 1, B, B), F32)}
        if "diag" in kinds:
            part = jax.ShapeDtypeStruct((2, 1, rows // chunks, B), F32)
            shapes = {number: part for number in range(chunks)}
    full = "diag" in kinds or "upper" in kinds
    work = 3 * 2 * (2 * B) * (2 * B) * many * (rows if full else B) * (1 + len(kinds))
    out = pl.pallas_call(
        functools.partial(panel_kernel, local, far, starts, kinds, first, last, chunks, devices, 1.0 / math.sqrt(B)),
        in_specs=[pl.BlockSpec(memory_space=pltpu.SMEM)] + [vmem] * (len(operands) - 1),
        out_specs=[vmem] * len(shapes),
        out_shape=list(shapes.values()),
        input_output_aliases=aliases,
        compiler_params=pltpu.CompilerParams(vmem_limit_bytes=VMEM_BYTES),
        cost_estimate=pl.CostEstimate(
            flops=work, bytes_accessed=8 * rows * B * many, transcendentals=0
        ),
    )(*operands)
    if last:
        return {"diag": out} if "diag" in kinds else {"upper": out[0], "over": out[1]}
    return dict(carry, **dict(zip(kinds, out)))


def scattered(fars, modes, row, size, shift_ref, at_ref, contact_ref, col_ref, row_ref, piece_refs):
    energy = at_ref[1]
    chosen = []
    for far in fars:
        apart = jnp.abs((energy ^ far) - energy)
        chosen.append([jnp.where(apart == shift_ref[m], 1.0, 0.0).astype(F32) for m in range(modes)])
    for start in range(0, size, B):
        rows = slice(row + start, row + start + B)
        outer = [col_ref[rows, m : m + 1] * row_ref[m : m + 1, rows] for m in range(modes)]
        values = [contact_ref[0, 0, rows], contact_ref[1, 0, rows]]
        for weights, ref in zip(chosen, piece_refs):
            weight = total(w * o for w, o in zip(weights, outer))
            values = [value + weight * ref[j, 0, start : start + B] for j, value in enumerate(values)]
        yield start, values


def phonon_kernel(fars, modes, row, size, *refs):
    out_ref = refs[-1]
    for start, values in scattered(fars, modes, row, size, *refs[:5], refs[5:-1]):
        for j in range(2):
            out_ref[j, 0, start : start + B] = values[j]


def phonon(shifts, at, contact, columns, lines, pieces, number, chunks):
    parts, energies, rows = contact.shape[:3]
    size = rows // chunks
    vmem = pl.BlockSpec(memory_space=pltpu.VMEM)
    smem = pl.BlockSpec(memory_space=pltpu.SMEM)
    return pl.pallas_call(
        functools.partial(
            phonon_kernel, [far for far, _ in pieces], shifts.shape[0], number * size, size
        ),
        in_specs=[smem, smem] + [vmem] * (3 + len(pieces)),
        out_specs=vmem,
        out_shape=jax.ShapeDtypeStruct((parts, energies, size, B), F32),
        compiler_params=pltpu.CompilerParams(vmem_limit_bytes=VMEM_BYTES),
        cost_estimate=pl.CostEstimate(
            flops=size * B * 20, bytes_accessed=8 * size * B * 5, transcendentals=0
        ),
    )(shifts, at, contact, columns, lines, *[piece for _, piece in pieces])


def ending_kernel(fars, modes, rows, size, scale, *refs):
    settings, refs = refs[:5], refs[5:]
    piece_refs, refs = refs[: len(fars)], refs[len(fars) :]
    row = rows - size
    done_refs, refs = refs[: row // size], refs[row // size :]
    diag_refs, refs = refs[: rows // size], refs[rows // size :]
    _, over_ref, above_ref, sigma_ref, upper_ref, diag_ref, held, tail, sems = refs
    copies = []

    def send(source, target):
        copies.append(pltpu.make_async_copy(source, target, sems.at[len(copies)]))
        copies[-1].start()

    for refs, target in ((done_refs, sigma_ref), (diag_refs, diag_ref)):
        for number, ref in enumerate(refs):
            send(ref, target.at[:, :, pl.ds(number * size, size)])
    for j in range(2):
        more = above_ref[0, :, j * B : (j + 1) * B].T * scale
        tail[j, 0] = over_ref[j, 0] + more
    send(tail, upper_ref.at[:, :, pl.ds(rows - B, B)])
    for start, values in scattered(fars, modes, row, size, *settings, piece_refs):
        for j in range(2):
            held[j, 0, start : start + B] = values[j]
        send(held.at[:, :, pl.ds(start, B)], sigma_ref.at[:, :, pl.ds(row + start, B)])
    for copy in copies:
        copy.wait()


def ending(shifts, at, contact, columns, lines, pieces, done, diag, upper, over, above):
    parts, energies, rows = contact.shape[:3]
    size = rows // (len(done) + 1)
    vmem = pl.BlockSpec(memory_space=pltpu.VMEM)
    smem = pl.BlockSpec(memory_space=pltpu.SMEM)
    hbm = pl.BlockSpec(memory_space=pl.ANY)
    operands = [shifts, at, contact, columns, lines, *[piece for _, piece in pieces], *done, *diag]
    specs = [smem, smem] + [vmem] * (len(operands) - 2) + [hbm, vmem, vmem]
    return pl.pallas_call(
        functools.partial(ending_kernel, [far for far, _ in pieces], shifts.shape[0], rows, size, 1.0 / math.sqrt(B)),
        in_specs=specs,
        out_specs=[hbm] * 3,
        out_shape=[jax.ShapeDtypeStruct(contact.shape, F32)] * 3,
        input_output_aliases={len(operands): 1},
        scratch_shapes=[
            pltpu.VMEM((parts, energies, size, B), F32),
            pltpu.VMEM((parts, energies, B, B), F32),
            pltpu.SemaphoreType.DMA((len(done) + len(diag) + 1 + size // B,)),
        ],
        compiler_params=pltpu.CompilerParams(vmem_limit_bytes=VMEM_BYTES),
        cost_estimate=pl.CostEstimate(
            flops=size * B * 20, bytes_accessed=8 * size * B * 5, transcendentals=0
        ),
    )(*operands, upper, over, above)


def cut_kernel(contact_ref, *refs):
    outs, sems = refs[:-1], refs[-1]
    copies = []
    start = 0
    for number, ref in enumerate(outs):
        size = ref.shape[2]
        at = 0 if number == len(outs) - 1 else start
        start += size
        copies.append(
            pltpu.make_async_copy(contact_ref.at[:, :, pl.ds(at, size)], ref, sems.at[number])
        )
    for copy in copies:
        copy.start()
    for copy in copies:
        copy.wait()


def cut(contact, chunks):
    parts, energies, rows = contact.shape[:3]
    part = jax.ShapeDtypeStruct((parts, energies, rows // chunks, B), F32)
    vmem = pl.BlockSpec(memory_space=pltpu.VMEM)
    return pl.pallas_call(
        cut_kernel,
        in_specs=[pl.BlockSpec(memory_space=pltpu.HBM)],
        out_specs=[vmem] * (chunks + 1),
        out_shape=[part] * chunks + [jax.ShapeDtypeStruct(contact.shape, F32)],
        scratch_shapes=[pltpu.SemaphoreType.DMA((chunks + 1,))],
        compiler_params=pltpu.CompilerParams(vmem_limit_bytes=VMEM_BYTES),
        cost_estimate=pl.CostEstimate(
            flops=0, bytes_accessed=32 * rows * B, transcendentals=0
        ),
        name="cut",
    )(contact)


def edge_rows(retarded, pan):
    rows, columns = retarded.shape[2:]
    devices = lax.axis_size("pan")
    middle = devices // 2
    up_start = (pan + 1 >= middle).astype(jnp.int32)
    down_start = (pan < middle).astype(jnp.int32)
    found, cuts = [], []
    for odd in (0, 1):
        up = pan % 2 == odd
        row = jnp.where(up, rows - B, 0)
        column = jnp.where(up, up_start, down_start) * (columns // 2)
        part = lax.dynamic_slice(retarded, (0, 0, row, column), (2, 1, B, columns // 2))
        pairs = []
        for i in range(odd, devices - 1, 2):
            pairs += [(i, i + 1), (i + 1, i)]
        cuts.append(part)
        found.append(lax.ppermute(part, "pan", pairs))
    return found, cuts


def gathered(near, chunks):
    size = chunks[0].shape[2] // B
    parts = [(i * size, chunk) for i, chunk in enumerate(chunks)]
    first = lax.axis_size("pan") // 2
    pieces = [(0, near)]
    bit = first
    while bit:
        found = []
        for far, piece in pieces:
            if bit == first:
                piece = parts
            sent = []
            for start, block in piece:
                sent.append((start, swapped(block, "pan", bit)))
            found.append((far ^ bit, sent))
        pieces += found
        bit //= 2
    return pieces


def body(retarded, contact, atom_kind, coupling, shifts):
    rows = retarded.shape[2]
    local = rows // B
    chunks = 2 if local % 2 == 0 else 1
    high = lax.axis_size("pan") // 2
    pan = lax.axis_index("pan").astype(jnp.int32)
    energy = lax.axis_index("en").astype(jnp.int32)
    at = jnp.where(jnp.arange(2, dtype=jnp.int32) == 0, pan, energy)
    atoms = rows // ORB
    kinds = lax.dynamic_slice_in_dim(atom_kind, pan * atoms, atoms, 0)
    per_atom = sum(jnp.where(kinds[:, None] == kind, coupling[kind][None, :], 0.0) for kind in range(coupling.shape[0]))
    per_row = jnp.repeat(per_atom, ORB, axis=0)
    per_line = jnp.repeat(per_atom.T, ORB, axis=1)
    edges, cuts = edge_rows(retarded, pan)
    *parts, copied = cut(contact, chunks)
    near = [(0, contact)]
    for rounds in range(ITERS):
        final = rounds == ITERS - 1
        pieces = gathered(near, parts)
        if rounds == 0:
            ready = lax.optimization_barrier((copied, per_row, per_line, *cuts))
            pieces[0] = (0, [(0, ready[0])])
            copied, per_row, per_line = ready[:3]
        groups = [(far, 0, blocks) for far, blocks in pieces[:-1]]
        groups.sort(key=lambda group: (group[0] != 0, group[0] >= high))
        if chunks > 1 and high > 1:
            far, _, blocks = groups.pop([far for far, _, _ in groups].index(high))
            groups.insert(1, (far, 0, blocks[:1]))
            groups.insert(2 if final else len(groups), (far, 1, blocks[1:]))
        sums = {}
        for far, number, blocks in groups:
            work = ("diag", "upper") if final else ("diag",)
            if final and 0 < far < high:
                if "over" not in sums:
                    sums = panel(at, retarded, 0, pieces[0][1], sums, edges, ("over", "back"), False)
                work += ("over", "back")
            sums = panel(at, retarded, far, blocks, sums, edges, work, False)
        far, blocks = pieces[-1]
        for number, block in enumerate(blocks):
            last = number == len(blocks) - 1
            new = panel(at, retarded, far, [block], sums, edges, ("diag",), last, chunks)
            sums = dict(sums, **new)
        found = spread(sums["diag"], "en")
        settings = (shifts, at, copied, per_row, per_line)
        if not final:
            parts = [phonon(*settings, own[1:], number, chunks) for number, own in enumerate(found)]
            near = [(i * (local // chunks), part) for i, part in enumerate(parts)]
    devices = lax.axis_size("pan")
    above = lax.ppermute(sums["back"], "pan", [(i + 1, i) for i in range(devices - 1)])
    for far, blocks in pieces[1:-1]:
        if far >= high:
            sums = panel(at, retarded, far, blocks, sums, edges, ("over",), False)
    far, blocks = pieces[-1]
    ends = panel(at, retarded, far, blocks, sums, edges, ("upper", "over"), True)
    done = [phonon(*settings, own[1:], number, chunks) for number, own in enumerate(found[:-1])]
    sigma, upper, diag = ending(*settings, found[-1][1:], done, sums["diag"], ends["upper"], ends["over"], above)
    return (diag, upper, sigma)


def solution(mesh):
    def step(retarded, *args):
        spread_spec = P(None, ("grp", "en"), "pan", None)
        inner = jax.shard_map(
            body,
            mesh=mesh,
            in_specs=(spread_spec, spread_spec, P(), P(), P()),
            out_specs=(spread_spec, spread_spec, spread_spec),
            check_vma=False,
        )
        return inner(retarded, *args)

    return step
```

```python
import functools
import math

import jax
import jax.numpy as jnp
from jax import lax
from jax.experimental import pallas as pl
from jax.experimental.pallas import tpu as pltpu
from jax.sharding import PartitionSpec as P


B = 128
ORB = 8
ITERS = 2
VMEM_BYTES = 28 * 2**20

F32 = jnp.float32
BF16 = jnp.bfloat16


def swapped(x, axis, bit):
    return lax.ppermute(x, axis, [(i, i ^ bit) for i in range(lax.axis_size(axis))])


def spread(chunks, axis):
    pieces = [[(0, chunk)] for chunk in chunks]
    bit = lax.axis_size(axis) // 2
    while bit:
        for own in pieces:
            found = []
            for far, piece in own:
                found.append((far ^ bit, swapped(piece, axis, bit)))
            own += found
        bit //= 2
    return pieces


def split(x):
    high = x.astype(BF16)
    return high, (x - high.astype(F32)).astype(BF16)


def dot(a, b):
    return jnp.dot(a, b, preferred_element_type=F32)


def dot_t(a, b):
    return lax.dot_general(a, b, (((1,), (1,)), ((), ())), preferred_element_type=F32)


def times(a, b):
    return dot(a[0], b[0]) + (dot(a[1], b[0]) + dot(a[0], b[1]))


def total(terms):
    return functools.reduce(lambda a, b: a + b, terms)


def rows_of(x, start, size):
    return tuple(v[start : start + size] for v in x)


def halves(x):
    return tuple(v[:, :B] for v in x), tuple(v[:, B:] for v in x)


def stacked(blocks):
    blocks = [halves(block) for block in blocks]
    return tuple(
        jnp.concatenate(
            [jnp.concatenate([block[j][part] for block in blocks], axis=1) for j in range(2)], axis=0
        )
        for part in range(2)
    )


def against(lefts, rights):
    terms = []
    for i in range(0, len(lefts), 2):
        left, right = stacked(lefts[i : i + 2]), stacked(rights[i : i + 2])
        terms += [dot_t(left[0], right[0]), dot_t(left[1], right[0]), dot_t(left[0], right[1])]
    both = total(terms)
    rows = both.shape[0] // 2
    re, im = both[:rows], both[rows:]
    return jnp.concatenate([re[:, :B] + im[:, B:], re[:, B:] - im[:, :B]], axis=1)


def edge_plan(kinds, far, blocks, local, devices):
    part = local // 2
    plan = {}
    for kind in kinds:
        for odd in range(2):
            found = []
            for place, block in enumerate(blocks):
                if (kind == "over") == (odd == 0):
                    if kind == "over":
                        column = {
                            0: ("even", block) if block < part else None,
                            devices // 2: ("late", block),
                            devices - 1: ("even", part + block),
                        }.get(far)
                    else:
                        column = {
                            0: ("even", part + block),
                            1: ("even", block - part) if block >= part else None,
                        }.get(far)
                    if column:
                        found.append((place, column[0], column[1] * B))
                elif far < devices // 2:
                    found.append((place, "odd", None))
            plan[kind, odd] = found
    return plan


def in_thirds(local, devices):
    return devices == 4 and local % 2 == 0


def panel_kernel(local, far, starts, kinds, names, first, last, chunks, devices, scale, *refs):
    refs = list(refs)
    at_ref, g_ref = refs[:2]
    piece_refs, refs = refs[2 : 2 + len(starts)], refs[2 + len(starts) :]
    edges = "over" in kinds or "back" in kinds
    edge_refs, refs = dict(zip(names, refs)), refs[len(names) :]
    ins = {}
    for kind in kinds:
        if kind not in first:
            ins[kind] = refs.pop(0)
    outs = refs if last and "diag" in kinds else dict(zip(kinds, refs))
    pan = at_ref[0]
    source = pan ^ far
    middle = devices // 2
    half = devices * local // 2
    whole = "diag" in kinds or "upper" in kinds
    low = 0 if whole else (local - 1) * B

    greens, sigmas, products, columns = [], [], [], []
    for start, s_ref in zip(starts, piece_refs):
        for u in range(s_ref.shape[2] // B):
            k = source * local + start + u
            columns.append(pl.ds(pl.multiple_of((k % half) * B, B), B))
            cut = pl.ds(pl.multiple_of(k * B, B), B)
            rows = slice(u * B, (u + 1) * B)
            sr, si = s_ref[0, 0, rows], s_ref[1, 0, rows]
            sigmas.append(
                split(
                    jnp.concatenate(
                        [jnp.concatenate([sr, si], axis=1), jnp.concatenate([-si, sr], axis=1)],
                        axis=0,
                    )
                )
            )
            greens.append(lambda low, high, cut=cut: split(
                jnp.concatenate([g_ref[0, 0, low:high, cut], g_ref[1, 0, low:high, cut]], axis=1)
            ))
            if whole:
                greens[-1] = functools.partial(
                    lambda whole, low, high: rows_of(whole, low, high - low),
                    greens[-1](0, local * B),
                )
                products.append(split(times(greens[-1](0, local * B), sigmas[-1])))

    def old(kind, i):
        return ins[kind][i] if kind in ins else 0.0

    def put(ref, row, value):
        ref[0, 0, row * B : (row + 1) * B] = value[:, :B].T * scale
        ref[1, 0, row * B : (row + 1) * B] = value[:, B:].T * scale

    diag, upper = "diag" in kinds, "upper" in kinds
    for i in range(local):
        start = 0 if diag else 1
        size = int(diag) + int(upper and i < local - 1)
        if not size:
            continue
        terms = against(
            [green((i + start) * B, (i + start + size) * B) for green in greens],
            [rows_of(product, i * B, B) for product in products],
        )
        if diag:
            value = old("diag", i) + terms[:B]
            if last:
                put(outs[i * chunks // local], i % (local // chunks), value)
            else:
                outs["diag"][i] = value
        if upper and i < local - 1:
            value = old("upper", i) + terms[-B:]
            if last:
                put(outs["upper"], i, value)
            else:
                outs["upper"][i] = value
    if not edges:
        return
    even = pan % 2 == 0

    def rows_at(ref, column):
        return split(
            jnp.concatenate([ref[0, 0, :, column], ref[1, 0, :, column]], axis=1)
        )

    def last_rows(number):
        if whole:
            return rows_of(products[number], (local - 1) * B, B)
        return split(times(greens[number](low, local * B), sigmas[number]))

    def add(kind, when, terms):
        @pl.when(when)
        def _():
            outs[kind][0] += terms()

    for kind in ("over", "back"):
        if kind in kinds:
            outs[kind][0] = ins[kind][0] if kind in ins else jnp.zeros((B, 2 * B), F32)

    if in_thirds(local, devices):
        blocks = [
            start + u for start, ref in zip(starts, piece_refs) for u in range(ref.shape[2] // B)
        ]
        plan = edge_plan([k for k in kinds if k in ("over", "back")], far, blocks, local, devices)
        for (kind, odd), found in plan.items():
            if not found:
                continue

            def terms(kind=kind, found=found):
                taken = [
                    (n, rows_at(edge_refs[name], columns[n] if at is None else slice(at, at + B)))
                    for n, name, at in found
                ]
                if kind == "over":
                    return against([edge for _, edge in taken], [last_rows(n) for n, _ in taken])
                return against(
                    [greens[n](0, B) for n, _ in taken],
                    [split(times(edge, sigmas[n])) for n, edge in taken],
                )

            add(kind, even if odd == 0 else jnp.logical_not(even), terms)
        return

    source_high = source >= middle

    def edge(near, column):
        return tuple(
            jnp.where(near, a, b)
            for a, b in zip(rows_at(edge_refs["even"], column), rows_at(edge_refs["odd"], column))
        )

    if "over" in kinds:
        add(
            "over",
            source_high != (pan + 1 >= middle),
            lambda: against(
                [edge(even, column) for column in columns],
                [last_rows(number) for number in range(len(columns))],
            ),
        )
    if "back" in kinds:
        add(
            "back",
            source_high == (pan >= middle),
            lambda: against(
                [green(0, B) for green in greens],
                [
                    split(times(edge(jnp.logical_not(even), column), sigma))
                    for sigma, column in zip(sigmas, columns)
                ],
            ),
        )


def panel(at, green, far, pieces, carry, edges, kinds, last, chunks=1):
    rows = green.shape[2]
    local = rows // B
    devices = lax.axis_size("pan")
    counts = {"diag": local, "upper": local - 1, "over": 1, "back": 1}
    kinds = tuple(kind for kind in kinds if counts[kind])
    vmem = pl.BlockSpec(memory_space=pltpu.VMEM)
    starts, many = [], 0
    for start, piece in pieces:
        starts.append(start)
        many += piece.shape[2] // B
    operands = [at, green] + [piece for _, piece in pieces]
    names = []
    if "over" in kinds or "back" in kinds:
        names = ["even", "odd"]
        if in_thirds(local, devices):
            blocks = [start + u for start, piece in pieces for u in range(piece.shape[2] // B)]
            plan = edge_plan([k for k in kinds if k in ("over", "back")], far, blocks, local, devices)
            names = sorted({name for found in plan.values() for _, name, _ in found})
        operands += [edges[name] for name in names]
    shapes = {kind: jax.ShapeDtypeStruct((counts[kind], B, 2 * B), F32) for kind in kinds}
    aliases = {}
    first = []
    for number, kind in enumerate(kinds):
        if kind not in carry:
            first.append(kind)
            continue
        if not last or kind == "over":
            aliases[len(operands)] = number
        operands.append(carry[kind])
    if last:
        tall = jax.ShapeDtypeStruct((2, 1, rows, B), F32)
        shapes["upper"] = tall
        if "diag" in kinds:
            part = jax.ShapeDtypeStruct((2, 1, rows // chunks, B), F32)
            shapes = {number: part for number in range(chunks)}
    full = "diag" in kinds or "upper" in kinds
    work = 3 * 2 * (2 * B) * (2 * B) * many * (rows if full else B) * (1 + len(kinds))
    out = pl.pallas_call(
        functools.partial(
            panel_kernel,
            local,
            far,
            starts,
            kinds,
            names,
            first,
            last,
            chunks,
            devices,
            1.0 / math.sqrt(B),
        ),
        in_specs=[pl.BlockSpec(memory_space=pltpu.SMEM)] + [vmem] * (len(operands) - 1),
        out_specs=[vmem] * len(shapes),
        out_shape=list(shapes.values()),
        input_output_aliases=aliases,
        compiler_params=pltpu.CompilerParams(vmem_limit_bytes=VMEM_BYTES),
        cost_estimate=pl.CostEstimate(
            flops=work, bytes_accessed=8 * rows * B * many, transcendentals=0
        ),
    )(*operands)
    if last and "diag" in kinds:
        return {"diag": out}
    return dict(carry, **dict(zip(shapes, out)))


def scattered(fars, modes, row, size, shift_ref, at_ref, contact_ref, col_ref, row_ref, piece_refs):
    energy = at_ref[1]
    chosen = []
    for far in fars:
        apart = jnp.abs((energy ^ far) - energy)
        chosen.append([jnp.where(apart == shift_ref[m], 1.0, 0.0).astype(F32) for m in range(modes)])
    for start in range(0, size, B):
        rows = slice(row + start, row + start + B)
        outer = [col_ref[rows, m : m + 1] * row_ref[m : m + 1, rows] for m in range(modes)]
        values = [contact_ref[0, 0, rows], contact_ref[1, 0, rows]]
        for weights, ref in zip(chosen, piece_refs):
            weight = total(w * o for w, o in zip(weights, outer))
            values = [value + weight * ref[j, 0, start : start + B] for j, value in enumerate(values)]
        yield start, values


def phonon_kernel(fars, modes, row, size, *refs):
    out_ref = refs[-1]
    for start, values in scattered(fars, modes, row, size, *refs[:5], refs[5:-1]):
        for j in range(2):
            out_ref[j, 0, start : start + B] = values[j]


def phonon(shifts, at, contact, columns, lines, pieces, number, chunks):
    parts, energies, rows = contact.shape[:3]
    size = rows // chunks
    vmem = pl.BlockSpec(memory_space=pltpu.VMEM)
    smem = pl.BlockSpec(memory_space=pltpu.SMEM)
    return pl.pallas_call(
        functools.partial(
            phonon_kernel, [far for far, _ in pieces], shifts.shape[0], number * size, size
        ),
        in_specs=[smem, smem] + [vmem] * (3 + len(pieces)),
        out_specs=vmem,
        out_shape=jax.ShapeDtypeStruct((parts, energies, size, B), F32),
        compiler_params=pltpu.CompilerParams(vmem_limit_bytes=VMEM_BYTES),
        cost_estimate=pl.CostEstimate(
            flops=size * B * 20, bytes_accessed=8 * size * B * 5, transcendentals=0
        ),
    )(shifts, at, contact, columns, lines, *[piece for _, piece in pieces])


def ending_kernel(fars, modes, rows, size, scale, *refs):
    settings, refs = refs[:5], refs[5:]
    piece_refs, refs = refs[: len(fars)], refs[len(fars) :]
    row = rows - size
    done_refs, refs = refs[: row // size], refs[row // size :]
    diag_refs, refs = refs[: rows // size], refs[rows // size :]
    _, over_ref, above_ref, sigma_ref, upper_ref, diag_ref, held, tail, sems = refs
    copies = []

    def send(source, target):
        copies.append(pltpu.make_async_copy(source, target, sems.at[len(copies)]))
        copies[-1].start()

    for refs, target in ((done_refs, sigma_ref), (diag_refs, diag_ref)):
        for number, ref in enumerate(refs):
            send(ref, target.at[:, :, pl.ds(number * size, size)])
    for j in range(2):
        part = slice(j * B, (j + 1) * B)
        tail[j, 0] = (over_ref[0, :, part] + above_ref[0, :, part]).T * scale
    send(tail, upper_ref.at[:, :, pl.ds(rows - B, B)])
    for start, values in scattered(fars, modes, row, size, *settings, piece_refs):
        for j in range(2):
            held[j, 0, start : start + B] = values[j]
        send(held.at[:, :, pl.ds(start, B)], sigma_ref.at[:, :, pl.ds(row + start, B)])
    for copy in copies:
        copy.wait()


def ending(shifts, at, contact, columns, lines, pieces, done, diag, upper, over, above):
    parts, energies, rows = contact.shape[:3]
    size = rows // (len(done) + 1)
    vmem = pl.BlockSpec(memory_space=pltpu.VMEM)
    smem = pl.BlockSpec(memory_space=pltpu.SMEM)
    hbm = pl.BlockSpec(memory_space=pl.ANY)
    operands = [shifts, at, contact, columns, lines, *[piece for _, piece in pieces], *done, *diag]
    specs = [smem, smem] + [vmem] * (len(operands) - 2) + [hbm, vmem, vmem]
    return pl.pallas_call(
        functools.partial(ending_kernel, [far for far, _ in pieces], shifts.shape[0], rows, size, 1.0 / math.sqrt(B)),
        in_specs=specs,
        out_specs=[hbm] * 3,
        out_shape=[jax.ShapeDtypeStruct(contact.shape, F32)] * 3,
        input_output_aliases={len(operands): 1},
        scratch_shapes=[
            pltpu.VMEM((parts, energies, size, B), F32),
            pltpu.VMEM((parts, energies, B, B), F32),
            pltpu.SemaphoreType.DMA((len(done) + len(diag) + 1 + size // B,)),
        ],
        compiler_params=pltpu.CompilerParams(vmem_limit_bytes=VMEM_BYTES),
        cost_estimate=pl.CostEstimate(
            flops=size * B * 20, bytes_accessed=8 * size * B * 5, transcendentals=0
        ),
    )(*operands, upper, over, above)


def cut_kernel(contact_ref, *refs):
    outs, sems = refs[:-1], refs[-1]
    copies = []
    start = 0
    for number, ref in enumerate(outs):
        size = ref.shape[2]
        at = 0 if number == len(outs) - 1 else start
        start += size
        copies.append(
            pltpu.make_async_copy(contact_ref.at[:, :, pl.ds(at, size)], ref, sems.at[number])
        )
    for copy in copies:
        copy.start()
    for copy in copies:
        copy.wait()


def cut(contact, chunks):
    parts, energies, rows = contact.shape[:3]
    part = jax.ShapeDtypeStruct((parts, energies, rows // chunks, B), F32)
    vmem = pl.BlockSpec(memory_space=pltpu.VMEM)
    return pl.pallas_call(
        cut_kernel,
        in_specs=[pl.BlockSpec(memory_space=pltpu.HBM)],
        out_specs=[vmem] * (chunks + 1),
        out_shape=[part] * chunks + [jax.ShapeDtypeStruct(contact.shape, F32)],
        scratch_shapes=[pltpu.SemaphoreType.DMA((chunks + 1,))],
        compiler_params=pltpu.CompilerParams(vmem_limit_bytes=VMEM_BYTES),
        cost_estimate=pl.CostEstimate(
            flops=0, bytes_accessed=32 * rows * B, transcendentals=0
        ),
        name="cut",
    )(contact)


def edge_rows(retarded, pan):
    rows, columns = retarded.shape[2:]
    devices = lax.axis_size("pan")
    local = rows // B
    middle = devices // 2
    thirds = in_thirds(local, devices)
    even = pan % 2 == 0

    def take(row, column, size):
        return lax.dynamic_slice(retarded, (0, 0, row, column), (2, 1, B, size))

    found, cuts = {}, []
    for odd, name in ((0, "even"), (1, "odd")):
        up = pan % 2 == odd
        row = jnp.where(up, rows - B, 0)
        if odd or not thirds:
            up_start = (pan + 1 >= middle).astype(jnp.int32)
            down_start = (pan < middle).astype(jnp.int32)
            column = jnp.where(up, up_start, down_start) * (columns // 2)
            part = take(row, column, columns // 2)
        else:
            short = jnp.where(even, pan * rows + rows // 2, (pan - 1) * rows)
            long = jnp.where(even, pan + 1, pan ^ middle) * rows
            part = jnp.concatenate([take(row, short, rows // 2), take(row, long, rows)], axis=3)
        pairs = []
        for i in range(odd, devices - 1, 2):
            pairs += [(i, i + 1), (i + 1, i)]
        cuts.append(part)
        found[name] = lax.ppermute(part, "pan", pairs)
    if thirds:
        part = take(0, (pan ^ (devices - 1)) * rows, rows)
        cuts.append(part)
        found["late"] = swapped(part, "pan", 1)
    return found, cuts


def gathered(near, chunks):
    size = chunks[0].shape[2] // B
    parts = [(i * size, chunk) for i, chunk in enumerate(chunks)]
    first = lax.axis_size("pan") // 2
    pieces = [(0, near)]
    bit = first
    while bit:
        found = []
        for far, piece in pieces:
            if bit == first:
                piece = parts
            sent = []
            for start, block in piece:
                sent.append((start, swapped(block, "pan", bit)))
            found.append((far ^ bit, sent))
        pieces += found
        bit //= 2
    return pieces


def body(retarded, contact, atom_kind, coupling, shifts):
    rows = retarded.shape[2]
    local = rows // B
    chunks = 2 if local % 2 == 0 else 1
    high = lax.axis_size("pan") // 2
    pan = lax.axis_index("pan").astype(jnp.int32)
    energy = lax.axis_index("en").astype(jnp.int32)
    at = jnp.where(jnp.arange(2, dtype=jnp.int32) == 0, pan, energy)
    atoms = rows // ORB
    kinds = lax.dynamic_slice_in_dim(atom_kind, pan * atoms, atoms, 0)
    per_atom = sum(jnp.where(kinds[:, None] == kind, coupling[kind][None, :], 0.0) for kind in range(coupling.shape[0]))
    per_row = jnp.repeat(per_atom, ORB, axis=0)
    per_line = jnp.repeat(per_atom.T, ORB, axis=1)
    edges, cuts = edge_rows(retarded, pan)
    *parts, copied = cut(contact, chunks)
    near = [(0, contact)]
    for rounds in range(ITERS):
        final = rounds == ITERS - 1
        pieces = gathered(near, parts)
        if rounds == 0:
            ready = lax.optimization_barrier((copied, per_row, per_line, *cuts))
            pieces[0] = (0, [(0, ready[0])])
            copied, per_row, per_line = ready[:3]
        groups = [(far, 0, blocks) for far, blocks in pieces[:-1]]
        groups.sort(key=lambda group: (group[0] != 0, group[0] >= high))
        if chunks > 1 and high > 1:
            far, _, blocks = groups.pop([far for far, _, _ in groups].index(high))
            groups.insert(1, (far, 0, blocks[:1]))
            groups.append((far, 1, blocks[1:]))
        sums = {}
        for far, number, blocks in groups:
            work = ("diag", "upper") if final else ("diag",)
            if final and 0 < far < high:
                if "over" not in sums:
                    sums = panel(at, retarded, 0, pieces[0][1], sums, edges, ("over", "back"), False)
                work += ("over", "back")
            sums = panel(at, retarded, far, blocks, sums, edges, work, False)
        far, blocks = pieces[-1]
        for number, block in enumerate(blocks):
            last = number == len(blocks) - 1
            new = panel(at, retarded, far, [block], sums, edges, ("diag",), last, chunks)
            sums = dict(sums, **new)
        found = spread(sums["diag"], "en")
        settings = (shifts, at, copied, per_row, per_line)
        if not final:
            parts = [phonon(*settings, own[1:], number, chunks) for number, own in enumerate(found)]
            near = [(i * (local // chunks), part) for i, part in enumerate(parts)]
    devices = lax.axis_size("pan")
    above = lax.ppermute(sums["back"], "pan", [(i + 1, i) for i in range(devices - 1)])
    far, blocks = pieces[-1]
    sums = panel(at, retarded, far, blocks, sums, edges, ("upper", "over"), True)
    for far, blocks in pieces[1:-1]:
        if far >= high:
            sums = panel(at, retarded, far, blocks, sums, edges, ("over",), False)
    done = [phonon(*settings, own[1:], number, chunks) for number, own in enumerate(found[:-1])]
    sigma, upper, diag = ending(*settings, found[-1][1:], done, sums["diag"], sums["upper"], sums["over"], above)
    return (diag, upper, sigma)


def solution(mesh):
    def step(retarded, *args):
        spread_spec = P(None, ("grp", "en"), "pan", None)
        inner = jax.shard_map(
            body,
            mesh=mesh,
            in_specs=(spread_spec, spread_spec, P(), P(), P()),
            out_specs=(spread_spec, spread_spec, spread_spec),
            check_vma=False,
        )
        return inner(retarded, *args)

    return step
```

```python
import functools
import math

import jax
import jax.numpy as jnp
from jax import lax
from jax.experimental import pallas as pl
from jax.experimental.pallas import tpu as pltpu
from jax.sharding import PartitionSpec as P


B = 128
ORB = 8
ITERS = 2
VMEM_BYTES = 28 * 2**20

F32 = jnp.float32
BF16 = jnp.bfloat16


def swapped(x, axis, bit):
    return lax.ppermute(x, axis, [(i, i ^ bit) for i in range(lax.axis_size(axis))])


def spread(chunks, axis):
    pieces = [[(0, chunk)] for chunk in chunks]
    bit = lax.axis_size(axis) // 2
    while bit:
        for own in pieces:
            found = []
            for far, piece in own:
                found.append((far ^ bit, swapped(piece, axis, bit)))
            own += found
        bit //= 2
    return pieces


def split(x):
    high = x.astype(BF16)
    return high, (x - high.astype(F32)).astype(BF16)


def dot(a, b):
    return jnp.dot(a, b, preferred_element_type=F32)


def dot_t(a, b):
    return lax.dot_general(a, b, (((1,), (1,)), ((), ())), preferred_element_type=F32)


def times(a, b):
    return dot(a[0], b[0]) + (dot(a[1], b[0]) + dot(a[0], b[1]))


def total(terms):
    return functools.reduce(lambda a, b: a + b, terms)


def rows_of(x, start, size):
    return tuple(v[start : start + size] for v in x)


def halves(x):
    return tuple(v[:, :B] for v in x), tuple(v[:, B:] for v in x)


def stacked(blocks):
    blocks = [halves(block) for block in blocks]
    return tuple(
        jnp.concatenate(
            [jnp.concatenate([block[j][part] for block in blocks], axis=1) for j in range(2)], axis=0
        )
        for part in range(2)
    )


def against(lefts, rights):
    terms = []
    for i in range(0, len(lefts), 2):
        left, right = stacked(lefts[i : i + 2]), stacked(rights[i : i + 2])
        terms += [dot_t(left[0], right[0]), dot_t(left[1], right[0]), dot_t(left[0], right[1])]
    both = total(terms)
    rows = both.shape[0] // 2
    re, im = both[:rows], both[rows:]
    return jnp.concatenate([re[:, :B] + im[:, B:], re[:, B:] - im[:, :B]], axis=1)


def edge_plan(kinds, far, blocks, local, devices):
    part = local // 2
    plan = {}
    for kind in kinds:
        for odd in range(2):
            found = []
            for place, block in enumerate(blocks):
                if (kind == "over") == (odd == 0):
                    if kind == "over":
                        column = {
                            0: ("even", block) if block < part else None,
                            devices // 2: ("late", block),
                            devices - 1: ("even", part + block),
                        }.get(far)
                    else:
                        column = {
                            0: ("even", part + block),
                            1: ("even", block - part) if block >= part else None,
                        }.get(far)
                    if column:
                        found.append((place, column[0], column[1] * B))
                elif far < devices // 2:
                    found.append((place, "odd", None))
            plan[kind, odd] = found
    return plan


def in_thirds(local, devices):
    return devices == 4 and local % 2 == 0


def panel_kernel(local, far, starts, kinds, names, first, last, chunks, devices, scale, *refs):
    refs = list(refs)
    at_ref, g_ref = refs[:2]
    piece_refs, refs = refs[2 : 2 + len(starts)], refs[2 + len(starts) :]
    edges = "over" in kinds or "back" in kinds
    edge_refs, refs = dict(zip(names, refs)), refs[len(names) :]
    ins = {}
    for kind in kinds:
        if kind not in first:
            ins[kind] = refs.pop(0)
    outs = refs if last and "diag" in kinds else dict(zip(kinds, refs))
    pan = at_ref[0]
    source = pan ^ far
    middle = devices // 2
    half = devices * local // 2
    whole = "diag" in kinds or "upper" in kinds
    low = 0 if whole else (local - 1) * B

    greens, sigmas, products, columns = [], [], [], []
    for start, s_ref in zip(starts, piece_refs):
        for u in range(s_ref.shape[2] // B):
            k = source * local + start + u
            columns.append(pl.ds(pl.multiple_of((k % half) * B, B), B))
            cut = pl.ds(pl.multiple_of(k * B, B), B)
            rows = slice(u * B, (u + 1) * B)
            sr, si = s_ref[0, 0, rows], s_ref[1, 0, rows]
            sigmas.append(
                split(
                    jnp.concatenate(
                        [jnp.concatenate([sr, si], axis=1), jnp.concatenate([-si, sr], axis=1)],
                        axis=0,
                    )
                )
            )
            greens.append(lambda low, high, cut=cut: split(
                jnp.concatenate([g_ref[0, 0, low:high, cut], g_ref[1, 0, low:high, cut]], axis=1)
            ))
            if whole:
                greens[-1] = functools.partial(
                    lambda whole, low, high: rows_of(whole, low, high - low),
                    greens[-1](0, local * B),
                )
                products.append(split(times(greens[-1](0, local * B), sigmas[-1])))

    def old(kind, i):
        return ins[kind][i] if kind in ins else 0.0

    def put(ref, row, value):
        ref[0, 0, row * B : (row + 1) * B] = value[:, :B].T * scale
        ref[1, 0, row * B : (row + 1) * B] = value[:, B:].T * scale

    diag, upper = "diag" in kinds, "upper" in kinds
    for i in range(local):
        start = 0 if diag else 1
        size = int(diag) + int(upper and i < local - 1)
        if not size:
            continue
        terms = against(
            [green((i + start) * B, (i + start + size) * B) for green in greens],
            [rows_of(product, i * B, B) for product in products],
        )
        if diag:
            value = old("diag", i) + terms[:B]
            if last:
                put(outs[i * chunks // local], i % (local // chunks), value)
            else:
                outs["diag"][i] = value
        if upper and i < local - 1:
            value = old("upper", i) + terms[-B:]
            if last:
                put(outs["upper"], i, value)
            else:
                outs["upper"][i] = value
    if not edges:
        return
    even = pan % 2 == 0

    def rows_at(ref, column):
        return split(
            jnp.concatenate([ref[0, 0, :, column], ref[1, 0, :, column]], axis=1)
        )

    def last_rows(number):
        if whole:
            return rows_of(products[number], (local - 1) * B, B)
        return split(times(greens[number](low, local * B), sigmas[number]))

    def add(kind, when, terms):
        @pl.when(when)
        def _():
            outs[kind][0] += terms()

    for kind in ("over", "back"):
        if kind in kinds:
            outs[kind][0] = ins[kind][0] if kind in ins else jnp.zeros((B, 2 * B), F32)

    if in_thirds(local, devices):
        blocks = [
            start + u for start, ref in zip(starts, piece_refs) for u in range(ref.shape[2] // B)
        ]
        plan = edge_plan([k for k in kinds if k in ("over", "back")], far, blocks, local, devices)
        for (kind, odd), found in plan.items():
            if not found:
                continue

            def terms(kind=kind, found=found):
                taken = [
                    (n, rows_at(edge_refs[name], columns[n] if at is None else slice(at, at + B)))
                    for n, name, at in found
                ]
                if kind == "over":
                    return against([edge for _, edge in taken], [last_rows(n) for n, _ in taken])
                return against(
                    [greens[n](0, B) for n, _ in taken],
                    [split(times(edge, sigmas[n])) for n, edge in taken],
                )

            add(kind, even if odd == 0 else jnp.logical_not(even), terms)
        return

    source_high = source >= middle

    def edge(near, column):
        return tuple(
            jnp.where(near, a, b)
            for a, b in zip(rows_at(edge_refs["even"], column), rows_at(edge_refs["odd"], column))
        )

    if "over" in kinds:
        add(
            "over",
            source_high != (pan + 1 >= middle),
            lambda: against(
                [edge(even, column) for column in columns],
                [last_rows(number) for number in range(len(columns))],
            ),
        )
    if "back" in kinds:
        add(
            "back",
            source_high == (pan >= middle),
            lambda: against(
                [green(0, B) for green in greens],
                [
                    split(times(edge(jnp.logical_not(even), column), sigma))
                    for sigma, column in zip(sigmas, columns)
                ],
            ),
        )


def panel(at, green, far, pieces, carry, edges, kinds, last, chunks=1):
    rows = green.shape[2]
    local = rows // B
    devices = lax.axis_size("pan")
    counts = {"diag": local, "upper": local - 1, "over": 1, "back": 1}
    kinds = tuple(kind for kind in kinds if counts[kind])
    vmem = pl.BlockSpec(memory_space=pltpu.VMEM)
    starts, many = [], 0
    for start, piece in pieces:
        starts.append(start)
        many += piece.shape[2] // B
    operands = [at, green] + [piece for _, piece in pieces]
    names = []
    if "over" in kinds or "back" in kinds:
        names = ["even", "odd"]
        if in_thirds(local, devices):
            blocks = [start + u for start, piece in pieces for u in range(piece.shape[2] // B)]
            plan = edge_plan([k for k in kinds if k in ("over", "back")], far, blocks, local, devices)
            names = sorted({name for found in plan.values() for _, name, _ in found})
        operands += [edges[name] for name in names]
    shapes = {kind: jax.ShapeDtypeStruct((counts[kind], B, 2 * B), F32) for kind in kinds}
    aliases = {}
    first = []
    for number, kind in enumerate(kinds):
        if kind not in carry:
            first.append(kind)
            continue
        if not last or kind == "over":
            aliases[len(operands)] = number
        operands.append(carry[kind])
    if last:
        tall = jax.ShapeDtypeStruct((2, 1, rows, B), F32)
        shapes["upper"] = tall
        if "diag" in kinds:
            part = jax.ShapeDtypeStruct((2, 1, rows // chunks, B), F32)
            shapes = {number: part for number in range(chunks)}
    full = "diag" in kinds or "upper" in kinds
    work = 3 * 2 * (2 * B) * (2 * B) * many * (rows if full else B) * (1 + len(kinds))
    out = pl.pallas_call(
        functools.partial(
            panel_kernel,
            local,
            far,
            starts,
            kinds,
            names,
            first,
            last,
            chunks,
            devices,
            1.0 / math.sqrt(B),
        ),
        in_specs=[pl.BlockSpec(memory_space=pltpu.SMEM)] + [vmem] * (len(operands) - 1),
        out_specs=[vmem] * len(shapes),
        out_shape=list(shapes.values()),
        input_output_aliases=aliases,
        compiler_params=pltpu.CompilerParams(vmem_limit_bytes=VMEM_BYTES),
        cost_estimate=pl.CostEstimate(
            flops=work, bytes_accessed=8 * rows * B * many, transcendentals=0
        ),
    )(*operands)
    if last and "diag" in kinds:
        return {"diag": out}
    return dict(carry, **dict(zip(shapes, out)))


def scattered(fars, modes, row, size, shift_ref, at_ref, contact_ref, col_ref, row_ref, piece_refs):
    energy = at_ref[1]
    chosen = []
    for far in fars:
        apart = jnp.abs((energy ^ far) - energy)
        chosen.append([jnp.where(apart == shift_ref[m], 1.0, 0.0).astype(F32) for m in range(modes)])
    for start in range(0, size, B):
        rows = slice(row + start, row + start + B)
        outer = [col_ref[rows, m : m + 1] * row_ref[m : m + 1, rows] for m in range(modes)]
        values = [contact_ref[0, 0, rows], contact_ref[1, 0, rows]]
        for weights, ref in zip(chosen, piece_refs):
            weight = total(w * o for w, o in zip(weights, outer))
            values = [value + weight * ref[j, 0, start : start + B] for j, value in enumerate(values)]
        yield start, values


def phonon_kernel(fars, modes, row, size, *refs):
    out_ref = refs[-1]
    for start, values in scattered(fars, modes, row, size, *refs[:5], refs[5:-1]):
        for j in range(2):
            out_ref[j, 0, start : start + B] = values[j]


def phonon(shifts, at, contact, columns, lines, pieces, number, chunks):
    parts, energies, rows = contact.shape[:3]
    size = rows // chunks
    vmem = pl.BlockSpec(memory_space=pltpu.VMEM)
    smem = pl.BlockSpec(memory_space=pltpu.SMEM)
    return pl.pallas_call(
        functools.partial(
            phonon_kernel, [far for far, _ in pieces], shifts.shape[0], number * size, size
        ),
        in_specs=[smem, smem] + [vmem] * (3 + len(pieces)),
        out_specs=vmem,
        out_shape=jax.ShapeDtypeStruct((parts, energies, size, B), F32),
        compiler_params=pltpu.CompilerParams(vmem_limit_bytes=VMEM_BYTES),
        cost_estimate=pl.CostEstimate(
            flops=size * B * 20, bytes_accessed=8 * size * B * 5, transcendentals=0
        ),
    )(shifts, at, contact, columns, lines, *[piece for _, piece in pieces])


def ending_kernel(fars, modes, rows, size, scale, *refs):
    settings, refs = refs[:5], refs[5:]
    piece_refs, refs = refs[: len(fars)], refs[len(fars) :]
    row = rows - size
    done_refs, refs = refs[: row // size], refs[row // size :]
    diag_refs, refs = refs[: rows // size], refs[rows // size :]
    _, over_ref, above_ref, sigma_ref, upper_ref, diag_ref, held, tail, sems = refs
    copies = []

    def send(source, target):
        copies.append(pltpu.make_async_copy(source, target, sems.at[len(copies)]))
        copies[-1].start()

    for refs, target in ((done_refs, sigma_ref), (diag_refs, diag_ref)):
        for number, ref in enumerate(refs):
            send(ref, target.at[:, :, pl.ds(number * size, size)])
    for j in range(2):
        part = slice(j * B, (j + 1) * B)
        tail[j, 0] = (over_ref[0, :, part] + above_ref[0, :, part]).T * scale
    send(tail, upper_ref.at[:, :, pl.ds(rows - B, B)])
    for start, values in scattered(fars, modes, row, size, *settings, piece_refs):
        for j in range(2):
            held[j, 0, start : start + B] = values[j]
        send(held.at[:, :, pl.ds(start, B)], sigma_ref.at[:, :, pl.ds(row + start, B)])
    for copy in copies:
        copy.wait()


def ending(shifts, at, contact, columns, lines, pieces, done, diag, upper, over, above):
    parts, energies, rows = contact.shape[:3]
    size = rows // (len(done) + 1)
    vmem = pl.BlockSpec(memory_space=pltpu.VMEM)
    smem = pl.BlockSpec(memory_space=pltpu.SMEM)
    hbm = pl.BlockSpec(memory_space=pl.ANY)
    operands = [shifts, at, contact, columns, lines, *[piece for _, piece in pieces], *done, *diag]
    specs = [smem, smem] + [vmem] * (len(operands) - 2) + [hbm, vmem, vmem]
    return pl.pallas_call(
        functools.partial(ending_kernel, [far for far, _ in pieces], shifts.shape[0], rows, size, 1.0 / math.sqrt(B)),
        in_specs=specs,
        out_specs=[hbm] * 3,
        out_shape=[jax.ShapeDtypeStruct(contact.shape, F32)] * 3,
        input_output_aliases={len(operands): 1},
        scratch_shapes=[
            pltpu.VMEM((parts, energies, size, B), F32),
            pltpu.VMEM((parts, energies, B, B), F32),
            pltpu.SemaphoreType.DMA((len(done) + len(diag) + 1 + size // B,)),
        ],
        compiler_params=pltpu.CompilerParams(vmem_limit_bytes=VMEM_BYTES),
        cost_estimate=pl.CostEstimate(
            flops=size * B * 20, bytes_accessed=8 * size * B * 5, transcendentals=0
        ),
    )(*operands, upper, over, above)


def cut_kernel(contact_ref, *refs):
    outs, sems = refs[:-1], refs[-1]
    copies = []
    start = 0
    for number, ref in enumerate(outs):
        size = ref.shape[2]
        at = 0 if number == len(outs) - 1 else start
        start += size
        copies.append(
            pltpu.make_async_copy(contact_ref.at[:, :, pl.ds(at, size)], ref, sems.at[number])
        )
    for copy in copies:
        copy.start()
    for copy in copies:
        copy.wait()


def cut(contact, chunks):
    parts, energies, rows = contact.shape[:3]
    part = jax.ShapeDtypeStruct((parts, energies, rows // chunks, B), F32)
    vmem = pl.BlockSpec(memory_space=pltpu.VMEM)
    return pl.pallas_call(
        cut_kernel,
        in_specs=[pl.BlockSpec(memory_space=pltpu.HBM)],
        out_specs=[vmem] * (chunks + 1),
        out_shape=[part] * chunks + [jax.ShapeDtypeStruct(contact.shape, F32)],
        scratch_shapes=[pltpu.SemaphoreType.DMA((chunks + 1,))],
        compiler_params=pltpu.CompilerParams(vmem_limit_bytes=VMEM_BYTES),
        cost_estimate=pl.CostEstimate(
            flops=0, bytes_accessed=32 * rows * B, transcendentals=0
        ),
        name="cut",
    )(contact)


def edge_rows(retarded, pan):
    rows, columns = retarded.shape[2:]
    devices = lax.axis_size("pan")
    local = rows // B
    middle = devices // 2
    thirds = in_thirds(local, devices)
    even = pan % 2 == 0

    def take(row, column, size):
        return lax.dynamic_slice(retarded, (0, 0, row, column), (2, 1, B, size))

    found, cuts = {}, []
    for odd, name in ((0, "even"), (1, "odd")):
        up = pan % 2 == odd
        row = jnp.where(up, rows - B, 0)
        if odd or not thirds:
            up_start = (pan + 1 >= middle).astype(jnp.int32)
            down_start = (pan < middle).astype(jnp.int32)
            column = jnp.where(up, up_start, down_start) * (columns // 2)
            part = take(row, column, columns // 2)
        else:
            short = jnp.where(even, pan * rows + rows // 2, (pan - 1) * rows)
            long = jnp.where(even, pan + 1, pan ^ middle) * rows
            part = jnp.concatenate([take(row, short, rows // 2), take(row, long, rows)], axis=3)
        pairs = []
        for i in range(odd, devices - 1, 2):
            pairs += [(i, i + 1), (i + 1, i)]
        cuts.append(part)
        found[name] = lax.ppermute(part, "pan", pairs)
    if thirds:
        part = take(0, (pan ^ (devices - 1)) * rows, rows)
        cuts.append(part)
        found["late"] = swapped(part, "pan", 1)
    return found, cuts


def gathered(near, chunks):
    size = chunks[0].shape[2] // B
    parts = [(i * size, chunk) for i, chunk in enumerate(chunks)]
    first = lax.axis_size("pan") // 2
    pieces = [(0, near)]
    bit = first
    while bit:
        found = []
        for far, piece in pieces:
            if bit == first:
                piece = parts
            sent = []
            for start, block in piece:
                sent.append((start, swapped(block, "pan", bit)))
            found.append((far ^ bit, sent))
        pieces += found
        bit //= 2
    return pieces


def body(retarded, contact, atom_kind, coupling, shifts):
    rows = retarded.shape[2]
    local = rows // B
    chunks = 2 if local % 2 == 0 else 1
    high = lax.axis_size("pan") // 2
    pan = lax.axis_index("pan").astype(jnp.int32)
    energy = lax.axis_index("en").astype(jnp.int32)
    at = jnp.where(jnp.arange(2, dtype=jnp.int32) == 0, pan, energy)
    atoms = rows // ORB
    kinds = lax.dynamic_slice_in_dim(atom_kind, pan * atoms, atoms, 0)
    per_atom = sum(jnp.where(kinds[:, None] == kind, coupling[kind][None, :], 0.0) for kind in range(coupling.shape[0]))
    per_row = jnp.repeat(per_atom, ORB, axis=0)
    per_line = jnp.repeat(per_atom.T, ORB, axis=1)
    edges, cuts = edge_rows(retarded, pan)
    *parts, copied = cut(contact, chunks)
    near = [(0, contact)]
    for rounds in range(ITERS):
        final = rounds == ITERS - 1
        pieces = gathered(near, parts)
        if rounds == 0:
            ready = lax.optimization_barrier((copied, per_row, per_line, *cuts))
            pieces[0] = (0, [(0, ready[0])])
            copied, per_row, per_line = ready[:3]
        groups = [(far, 0, blocks) for far, blocks in pieces[:-1]]
        groups.sort(key=lambda group: (group[0] != 0, group[0] >= high))
        if chunks > 1 and high > 1:
            far, _, blocks = groups.pop([far for far, _, _ in groups].index(high))
            groups.insert(1, (far, 0, blocks[:1]))
            groups.append((far, 1, blocks[1:]))
            for place, (near_far, _, blocks) in enumerate(groups):
                if near_far == 1 and len(blocks) > 1:
                    groups[place] = (1, 0, blocks[:1])
                    groups.append((1, 1, blocks[1:]))
                    break
        sums = {}
        for far, number, blocks in groups:
            work = ("diag", "upper") if final else ("diag",)
            if final and 0 < far < high:
                if "over" not in sums:
                    sums = panel(at, retarded, 0, pieces[0][1], sums, edges, ("over", "back"), False)
                work += ("over", "back")
            sums = panel(at, retarded, far, blocks, sums, edges, work, False)
        far, blocks = pieces[-1]
        for number, block in enumerate(blocks):
            last = number == len(blocks) - 1
            new = panel(at, retarded, far, [block], sums, edges, ("diag",), last, chunks)
            sums = dict(sums, **new)
        found = spread(sums["diag"], "en")
        settings = (shifts, at, copied, per_row, per_line)
        if not final:
            parts = [phonon(*settings, own[1:], number, chunks) for number, own in enumerate(found)]
            near = [(i * (local // chunks), part) for i, part in enumerate(parts)]
    devices = lax.axis_size("pan")
    above = lax.ppermute(sums["back"], "pan", [(i + 1, i) for i in range(devices - 1)])
    far, blocks = pieces[-1]
    sums = panel(at, retarded, far, blocks, sums, edges, ("upper", "over"), True)
    for far, blocks in pieces[1:-1]:
        if far >= high:
            sums = panel(at, retarded, far, blocks, sums, edges, ("over",), False)
    done = [phonon(*settings, own[1:], number, chunks) for number, own in enumerate(found[:-1])]
    sigma, upper, diag = ending(*settings, found[-1][1:], done, sums["diag"], sums["upper"], sums["over"], above)
    return (diag, upper, sigma)


def solution(mesh):
    def step(retarded, *args):
        spread_spec = P(None, ("grp", "en"), "pan", None)
        inner = jax.shard_map(
            body,
            mesh=mesh,
            in_specs=(spread_spec, spread_spec, P(), P(), P()),
            out_specs=(spread_spec, spread_spec, spread_spec),
            check_vma=False,
        )
        return inner(retarded, *args)

    return step
```

```python
import functools
import math

import jax
import jax.numpy as jnp
from jax import lax
from jax.experimental import pallas as pl
from jax.experimental.pallas import tpu as pltpu
from jax.sharding import PartitionSpec as P


B = 128
ORB = 8
ITERS = 2
VMEM_BYTES = 28 * 2**20

F32 = jnp.float32
BF16 = jnp.bfloat16


def swapped(x, axis, bit):
    return lax.ppermute(x, axis, [(i, i ^ bit) for i in range(lax.axis_size(axis))])


def spread(chunks, axis):
    pieces = [[(0, chunk)] for chunk in chunks]
    bit = lax.axis_size(axis) // 2
    while bit:
        for own in pieces:
            found = []
            for far, piece in own:
                found.append((far ^ bit, swapped(piece, axis, bit)))
            own += found
        bit //= 2
    return pieces


def split(x):
    high = x.astype(BF16)
    return high, (x - high.astype(F32)).astype(BF16)


def dot(a, b):
    return jnp.dot(a, b, preferred_element_type=F32)


def dot_t(a, b):
    return lax.dot_general(a, b, (((1,), (1,)), ((), ())), preferred_element_type=F32)


def times(a, b):
    return dot(a[0], b[0]) + (dot(a[1], b[0]) + dot(a[0], b[1]))


def total(terms):
    return functools.reduce(lambda a, b: a + b, terms)


def rows_of(x, start, size):
    return tuple(v[start : start + size] for v in x)


def halves(x):
    return tuple(v[:, :B] for v in x), tuple(v[:, B:] for v in x)


def stacked(blocks):
    blocks = [halves(block) for block in blocks]
    return tuple(
        jnp.concatenate(
            [jnp.concatenate([block[j][part] for block in blocks], axis=1) for j in range(2)], axis=0
        )
        for part in range(2)
    )


def against(lefts, rights):
    terms = []
    for i in range(0, len(lefts), 2):
        left, right = stacked(lefts[i : i + 2]), stacked(rights[i : i + 2])
        terms += [dot_t(left[0], right[0]), dot_t(left[1], right[0]), dot_t(left[0], right[1])]
    both = total(terms)
    rows = both.shape[0] // 2
    re, im = both[:rows], both[rows:]
    return jnp.concatenate([re[:, :B] + im[:, B:], re[:, B:] - im[:, :B]], axis=1)


def edge_plan(kinds, far, blocks, local, devices):
    part = local // 2
    plan = {}
    for kind in kinds:
        for odd in range(2):
            found = []
            for place, block in enumerate(blocks):
                if (kind == "over") == (odd == 0):
                    if kind == "over":
                        column = {
                            0: ("even", block) if block < part else None,
                            devices // 2: ("late", block),
                            devices - 1: ("even", part + block),
                        }.get(far)
                    else:
                        column = {
                            0: ("even", part + block),
                            1: ("even", block - part) if block >= part else None,
                        }.get(far)
                    if column:
                        found.append((place, column[0], column[1] * B))
                elif far < devices // 2:
                    found.append((place, "odd", None))
            plan[kind, odd] = found
    return plan


def in_thirds(local, devices):
    return devices == 4 and local % 2 == 0


def panel_kernel(local, far, starts, kinds, names, first, last, chunks, devices, scale, *refs):
    refs = list(refs)
    at_ref, g_ref = refs[:2]
    piece_refs, refs = refs[2 : 2 + len(starts)], refs[2 + len(starts) :]
    edges = "over" in kinds or "back" in kinds
    edge_refs, refs = dict(zip(names, refs)), refs[len(names) :]
    ins = {}
    for kind in kinds:
        if kind not in first:
            ins[kind] = refs.pop(0)
    outs = refs if last and "diag" in kinds else dict(zip(kinds, refs))
    pan = at_ref[0]
    source = pan ^ far
    middle = devices // 2
    half = devices * local // 2
    whole = "diag" in kinds or "upper" in kinds
    low = 0 if whole else (local - 1) * B

    greens, sigmas, products, columns = [], [], [], []
    for start, s_ref in zip(starts, piece_refs):
        for u in range(s_ref.shape[2] // B):
            k = source * local + start + u
            columns.append(pl.ds(pl.multiple_of((k % half) * B, B), B))
            cut = pl.ds(pl.multiple_of(k * B, B), B)
            rows = slice(u * B, (u + 1) * B)
            sr, si = s_ref[0, 0, rows], s_ref[1, 0, rows]
            sigmas.append(
                split(
                    jnp.concatenate(
                        [jnp.concatenate([sr, si], axis=1), jnp.concatenate([-si, sr], axis=1)],
                        axis=0,
                    )
                )
            )
            greens.append(lambda low, high, cut=cut: split(
                jnp.concatenate([g_ref[0, 0, low:high, cut], g_ref[1, 0, low:high, cut]], axis=1)
            ))
            if whole:
                greens[-1] = functools.partial(
                    lambda whole, low, high: rows_of(whole, low, high - low),
                    greens[-1](0, local * B),
                )
                products.append(split(times(greens[-1](0, local * B), sigmas[-1])))

    def old(kind, i):
        return ins[kind][i] if kind in ins else 0.0

    def put(ref, row, value):
        ref[0, 0, row * B : (row + 1) * B] = value[:, :B].T * scale
        ref[1, 0, row * B : (row + 1) * B] = value[:, B:].T * scale

    diag, upper = "diag" in kinds, "upper" in kinds
    for i in range(local):
        start = 0 if diag else 1
        size = int(diag) + int(upper and i < local - 1)
        if not size:
            continue
        terms = against(
            [green((i + start) * B, (i + start + size) * B) for green in greens],
            [rows_of(product, i * B, B) for product in products],
        )
        if diag:
            value = old("diag", i) + terms[:B]
            if last:
                put(outs[i * chunks // local], i % (local // chunks), value)
            else:
                outs["diag"][i] = value
        if upper and i < local - 1:
            value = old("upper", i) + terms[-B:]
            if last:
                put(outs["upper"], i, value)
            else:
                outs["upper"][i] = value
    if not edges:
        return
    even = pan % 2 == 0

    def rows_at(ref, column):
        return split(
            jnp.concatenate([ref[0, 0, :, column], ref[1, 0, :, column]], axis=1)
        )

    def last_rows(number):
        if whole:
            return rows_of(products[number], (local - 1) * B, B)
        return split(times(greens[number](low, local * B), sigmas[number]))

    def add(kind, when, terms):
        @pl.when(when)
        def _():
            outs[kind][0] += terms()

    for kind in ("over", "back"):
        if kind in kinds:
            outs[kind][0] = ins[kind][0] if kind in ins else jnp.zeros((B, 2 * B), F32)

    if in_thirds(local, devices):
        blocks = [
            start + u for start, ref in zip(starts, piece_refs) for u in range(ref.shape[2] // B)
        ]
        plan = edge_plan([k for k in kinds if k in ("over", "back")], far, blocks, local, devices)
        for (kind, odd), found in plan.items():
            if not found:
                continue

            def terms(kind=kind, found=found):
                taken = [
                    (n, rows_at(edge_refs[name], columns[n] if at is None else slice(at, at + B)))
                    for n, name, at in found
                ]
                if kind == "over":
                    return against([edge for _, edge in taken], [last_rows(n) for n, _ in taken])
                return against(
                    [greens[n](0, B) for n, _ in taken],
                    [split(times(edge, sigmas[n])) for n, edge in taken],
                )

            add(kind, even if odd == 0 else jnp.logical_not(even), terms)
        return

    source_high = source >= middle

    def edge(near, column):
        return tuple(
            jnp.where(near, a, b)
            for a, b in zip(rows_at(edge_refs["even"], column), rows_at(edge_refs["odd"], column))
        )

    if "over" in kinds:
        add(
            "over",
            source_high != (pan + 1 >= middle),
            lambda: against(
                [edge(even, column) for column in columns],
                [last_rows(number) for number in range(len(columns))],
            ),
        )
    if "back" in kinds:
        add(
            "back",
            source_high == (pan >= middle),
            lambda: against(
                [green(0, B) for green in greens],
                [
                    split(times(edge(jnp.logical_not(even), column), sigma))
                    for sigma, column in zip(sigmas, columns)
                ],
            ),
        )


def panel(at, green, far, pieces, carry, edges, kinds, last, chunks=1):
    rows = green.shape[2]
    local = rows // B
    devices = lax.axis_size("pan")
    counts = {"diag": local, "upper": local - 1, "over": 1, "back": 1}
    kinds = tuple(kind for kind in kinds if counts[kind])
    vmem = pl.BlockSpec(memory_space=pltpu.VMEM)
    starts, many = [], 0
    for start, piece in pieces:
        starts.append(start)
        many += piece.shape[2] // B
    operands = [at, green] + [piece for _, piece in pieces]
    names = []
    if "over" in kinds or "back" in kinds:
        names = ["even", "odd"]
        if in_thirds(local, devices):
            blocks = [start + u for start, piece in pieces for u in range(piece.shape[2] // B)]
            plan = edge_plan([k for k in kinds if k in ("over", "back")], far, blocks, local, devices)
            names = sorted({name for found in plan.values() for _, name, _ in found})
        operands += [edges[name] for name in names]
    shapes = {kind: jax.ShapeDtypeStruct((counts[kind], B, 2 * B), F32) for kind in kinds}
    aliases = {}
    first = []
    for number, kind in enumerate(kinds):
        if kind not in carry:
            first.append(kind)
            continue
        if not last or kind == "over":
            aliases[len(operands)] = number
        operands.append(carry[kind])
    if last:
        tall = jax.ShapeDtypeStruct((2, 1, rows, B), F32)
        shapes["upper"] = tall
        if "diag" in kinds:
            part = jax.ShapeDtypeStruct((2, 1, rows // chunks, B), F32)
            shapes = {number: part for number in range(chunks)}
    full = "diag" in kinds or "upper" in kinds
    work = 3 * 2 * (2 * B) * (2 * B) * many * (rows if full else B) * (1 + len(kinds))
    out = pl.pallas_call(
        functools.partial(
            panel_kernel,
            local,
            far,
            starts,
            kinds,
            names,
            first,
            last,
            chunks,
            devices,
            1.0 / math.sqrt(B),
        ),
        in_specs=[pl.BlockSpec(memory_space=pltpu.SMEM)] + [vmem] * (len(operands) - 1),
        out_specs=[vmem] * len(shapes),
        out_shape=list(shapes.values()),
        input_output_aliases=aliases,
        compiler_params=pltpu.CompilerParams(vmem_limit_bytes=VMEM_BYTES),
        cost_estimate=pl.CostEstimate(
            flops=work, bytes_accessed=8 * rows * B * many, transcendentals=0
        ),
    )(*operands)
    if last and "diag" in kinds:
        return {"diag": out}
    return dict(carry, **dict(zip(shapes, out)))


def scattered(fars, modes, row, size, shift_ref, at_ref, contact_ref, col_ref, row_ref, piece_refs):
    energy = at_ref[1]
    chosen = []
    for far in fars:
        apart = jnp.abs((energy ^ far) - energy)
        chosen.append([jnp.where(apart == shift_ref[m], 1.0, 0.0).astype(F32) for m in range(modes)])
    for start in range(0, size, B):
        rows = slice(row + start, row + start + B)
        outer = [col_ref[rows, m : m + 1] * row_ref[m : m + 1, rows] for m in range(modes)]
        values = [contact_ref[0, 0, rows], contact_ref[1, 0, rows]]
        for weights, ref in zip(chosen, piece_refs):
            weight = total(w * o for w, o in zip(weights, outer))
            values = [value + weight * ref[j, 0, start : start + B] for j, value in enumerate(values)]
        yield start, values


def phonon_kernel(fars, modes, row, size, *refs):
    out_ref = refs[-1]
    for start, values in scattered(fars, modes, row, size, *refs[:5], refs[5:-1]):
        for j in range(2):
            out_ref[j, 0, start : start + B] = values[j]


def phonon(shifts, at, contact, columns, lines, pieces, number, chunks):
    parts, energies, rows = contact.shape[:3]
    size = rows // chunks
    vmem = pl.BlockSpec(memory_space=pltpu.VMEM)
    smem = pl.BlockSpec(memory_space=pltpu.SMEM)
    return pl.pallas_call(
        functools.partial(
            phonon_kernel, [far for far, _ in pieces], shifts.shape[0], number * size, size
        ),
        in_specs=[smem, smem] + [vmem] * (3 + len(pieces)),
        out_specs=vmem,
        out_shape=jax.ShapeDtypeStruct((parts, energies, size, B), F32),
        compiler_params=pltpu.CompilerParams(vmem_limit_bytes=VMEM_BYTES),
        cost_estimate=pl.CostEstimate(
            flops=size * B * 20, bytes_accessed=8 * size * B * 5, transcendentals=0
        ),
    )(shifts, at, contact, columns, lines, *[piece for _, piece in pieces])


def ending_kernel(fars, modes, rows, size, scale, *refs):
    settings, refs = refs[:5], refs[5:]
    piece_refs, refs = refs[: len(fars)], refs[len(fars) :]
    row = rows - size
    done_refs, refs = refs[: row // size], refs[row // size :]
    diag_refs, refs = refs[: rows // size], refs[rows // size :]
    _, over_ref, above_ref, sigma_ref, upper_ref, diag_ref, held, tail, sems = refs
    copies = []

    def send(source, target):
        copies.append(pltpu.make_async_copy(source, target, sems.at[len(copies)]))
        copies[-1].start()

    for refs, target in ((done_refs, sigma_ref), (diag_refs, diag_ref)):
        for number, ref in enumerate(refs):
            send(ref, target.at[:, :, pl.ds(number * size, size)])
    for j in range(2):
        part = slice(j * B, (j + 1) * B)
        tail[j, 0] = (over_ref[0, :, part] + above_ref[0, :, part]).T * scale
    send(tail, upper_ref.at[:, :, pl.ds(rows - B, B)])
    for start, values in scattered(fars, modes, row, size, *settings, piece_refs):
        for j in range(2):
            held[j, 0, start : start + B] = values[j]
        send(held.at[:, :, pl.ds(start, B)], sigma_ref.at[:, :, pl.ds(row + start, B)])
    for copy in copies:
        copy.wait()


def ending(shifts, at, contact, columns, lines, pieces, done, diag, upper, over, above):
    parts, energies, rows = contact.shape[:3]
    size = rows // (len(done) + 1)
    vmem = pl.BlockSpec(memory_space=pltpu.VMEM)
    smem = pl.BlockSpec(memory_space=pltpu.SMEM)
    hbm = pl.BlockSpec(memory_space=pl.ANY)
    operands = [shifts, at, contact, columns, lines, *[piece for _, piece in pieces], *done, *diag]
    specs = [smem, smem] + [vmem] * (len(operands) - 2) + [hbm, vmem, vmem]
    return pl.pallas_call(
        functools.partial(ending_kernel, [far for far, _ in pieces], shifts.shape[0], rows, size, 1.0 / math.sqrt(B)),
        in_specs=specs,
        out_specs=[hbm] * 3,
        out_shape=[jax.ShapeDtypeStruct(contact.shape, F32)] * 3,
        input_output_aliases={len(operands): 1},
        scratch_shapes=[
            pltpu.VMEM((parts, energies, size, B), F32),
            pltpu.VMEM((parts, energies, B, B), F32),
            pltpu.SemaphoreType.DMA((len(done) + len(diag) + 1 + size // B,)),
        ],
        compiler_params=pltpu.CompilerParams(vmem_limit_bytes=VMEM_BYTES),
        cost_estimate=pl.CostEstimate(
            flops=size * B * 20, bytes_accessed=8 * size * B * 5, transcendentals=0
        ),
    )(*operands, upper, over, above)


def cut_kernel(contact_ref, *refs):
    outs, sems = refs[:-1], refs[-1]
    copies = []
    start = 0
    for number, ref in enumerate(outs):
        size = ref.shape[2]
        at = 0 if number == len(outs) - 1 else start
        start += size
        copies.append(
            pltpu.make_async_copy(contact_ref.at[:, :, pl.ds(at, size)], ref, sems.at[number])
        )
    for copy in copies:
        copy.start()
    for copy in copies:
        copy.wait()


def cut(contact, chunks):
    parts, energies, rows = contact.shape[:3]
    part = jax.ShapeDtypeStruct((parts, energies, rows // chunks, B), F32)
    vmem = pl.BlockSpec(memory_space=pltpu.VMEM)
    return pl.pallas_call(
        cut_kernel,
        in_specs=[pl.BlockSpec(memory_space=pltpu.HBM)],
        out_specs=[vmem] * (chunks + 1),
        out_shape=[part] * chunks + [jax.ShapeDtypeStruct(contact.shape, F32)],
        scratch_shapes=[pltpu.SemaphoreType.DMA((chunks + 1,))],
        compiler_params=pltpu.CompilerParams(vmem_limit_bytes=VMEM_BYTES),
        cost_estimate=pl.CostEstimate(
            flops=0, bytes_accessed=32 * rows * B, transcendentals=0
        ),
        name="cut",
    )(contact)


def edge_rows(retarded, pan):
    rows, columns = retarded.shape[2:]
    devices = lax.axis_size("pan")
    local = rows // B
    middle = devices // 2
    thirds = in_thirds(local, devices)
    even = pan % 2 == 0

    def take(row, column, size):
        return lax.dynamic_slice(retarded, (0, 0, row, column), (2, 1, B, size))

    found, cuts = {}, []
    for odd, name in ((0, "even"), (1, "odd")):
        up = pan % 2 == odd
        row = jnp.where(up, rows - B, 0)
        if odd or not thirds:
            up_start = (pan + 1 >= middle).astype(jnp.int32)
            down_start = (pan < middle).astype(jnp.int32)
            column = jnp.where(up, up_start, down_start) * (columns // 2)
            part = take(row, column, columns // 2)
        else:
            short = jnp.where(even, pan * rows + rows // 2, (pan - 1) * rows)
            long = jnp.where(even, pan + 1, pan ^ middle) * rows
            part = jnp.concatenate([take(row, short, rows // 2), take(row, long, rows)], axis=3)
        pairs = []
        for i in range(odd, devices - 1, 2):
            pairs += [(i, i + 1), (i + 1, i)]
        cuts.append(part)
        found[name] = lax.ppermute(part, "pan", pairs)
    if thirds:
        part = take(0, (pan ^ (devices - 1)) * rows, rows)
        cuts.append(part)
        found["late"] = swapped(part, "pan", 1)
    return found, cuts


def gathered(near, chunks):
    size = chunks[0].shape[2] // B
    parts = [(i * size, chunk) for i, chunk in enumerate(chunks)]
    first = lax.axis_size("pan") // 2
    pieces = [(0, near)]
    bit = first
    while bit:
        found = []
        for far, piece in pieces:
            if bit == first:
                piece = parts
            sent = []
            for start, block in piece:
                sent.append((start, swapped(block, "pan", bit)))
            found.append((far ^ bit, sent))
        pieces += found
        bit //= 2
    return pieces


def body(retarded, contact, atom_kind, coupling, shifts):
    rows = retarded.shape[2]
    local = rows // B
    chunks = 2 if local % 2 == 0 else 1
    high = lax.axis_size("pan") // 2
    pan = lax.axis_index("pan").astype(jnp.int32)
    energy = lax.axis_index("en").astype(jnp.int32)
    at = jnp.where(jnp.arange(2, dtype=jnp.int32) == 0, pan, energy)
    atoms = rows // ORB
    kinds = lax.dynamic_slice_in_dim(atom_kind, pan * atoms, atoms, 0)
    per_atom = sum(jnp.where(kinds[:, None] == kind, coupling[kind][None, :], 0.0) for kind in range(coupling.shape[0]))
    per_row = jnp.repeat(per_atom, ORB, axis=0)
    per_line = jnp.repeat(per_atom.T, ORB, axis=1)
    edges, cuts = edge_rows(retarded, pan)
    *parts, copied = cut(contact, chunks)
    near = [(0, contact)]
    for rounds in range(ITERS):
        final = rounds == ITERS - 1
        pieces = gathered(near, parts)
        if rounds == 0:
            ready = lax.optimization_barrier((copied, per_row, per_line, *cuts))
            pieces[0] = (0, [(0, ready[0])])
            copied, per_row, per_line = ready[:3]
        groups = [(far, 0, blocks) for far, blocks in pieces[:-1]]
        groups.sort(key=lambda group: (group[0] != 0, group[0] >= high))
        if chunks > 1 and high > 1:
            far, _, blocks = groups.pop([far for far, _, _ in groups].index(high))
            groups.insert(1, (far, 0, blocks[:1]))
            groups.append((far, 1, blocks[1:]))
            if final:
                place = [far for far, _, _ in groups].index(1)
                blocks = groups.pop(place)[2]
                for number, block in enumerate(blocks):
                    groups.insert(1 + number, (1, number, [block]))
        sums = {}
        for far, number, blocks in groups:
            work = ("diag", "upper") if final else ("diag",)
            if final and 0 < far < high:
                if "over" not in sums:
                    sums = panel(at, retarded, 0, pieces[0][1], sums, edges, ("over", "back"), False)
                work += ("over", "back")
            sums = panel(at, retarded, far, blocks, sums, edges, work, False)
        far, blocks = pieces[-1]
        for number, block in enumerate(blocks):
            last = number == len(blocks) - 1
            new = panel(at, retarded, far, [block], sums, edges, ("diag",), last, chunks)
            sums = dict(sums, **new)
        found = spread(sums["diag"], "en")
        settings = (shifts, at, copied, per_row, per_line)
        if not final:
            parts = [phonon(*settings, own[1:], number, chunks) for number, own in enumerate(found)]
            near = [(i * (local // chunks), part) for i, part in enumerate(parts)]
    devices = lax.axis_size("pan")
    above = lax.ppermute(sums["back"], "pan", [(i + 1, i) for i in range(devices - 1)])
    far, blocks = pieces[-1]
    sums = panel(at, retarded, far, blocks, sums, edges, ("upper", "over"), True)
    for far, blocks in pieces[1:-1]:
        if far >= high:
            sums = panel(at, retarded, far, blocks, sums, edges, ("over",), False)
    done = [phonon(*settings, own[1:], number, chunks) for number, own in enumerate(found[:-1])]
    sigma, upper, diag = ending(*settings, found[-1][1:], done, sums["diag"], sums["upper"], sums["over"], above)
    return (diag, upper, sigma)


def solution(mesh):
    def step(retarded, *args):
        spread_spec = P(None, ("grp", "en"), "pan", None)
        inner = jax.shard_map(
            body,
            mesh=mesh,
            in_specs=(spread_spec, spread_spec, P(), P(), P()),
            out_specs=(spread_spec, spread_spec, spread_spec),
            check_vma=False,
        )
        return inner(retarded, *args)

    return step
```

```python
import functools
import math

import jax
import jax.numpy as jnp
from jax import lax
from jax.experimental import pallas as pl
from jax.experimental.pallas import tpu as pltpu
from jax.sharding import PartitionSpec as P


B = 128
ORB = 8
ITERS = 2
VMEM_BYTES = 28 * 2**20

F32 = jnp.float32
BF16 = jnp.bfloat16


def swapped(x, axis, bit):
    return lax.ppermute(x, axis, [(i, i ^ bit) for i in range(lax.axis_size(axis))])


def spread(chunks, axis):
    pieces = [[(0, chunk)] for chunk in chunks]
    bit = lax.axis_size(axis) // 2
    while bit:
        for own in pieces:
            found = []
            for far, piece in own:
                found.append((far ^ bit, swapped(piece, axis, bit)))
            own += found
        bit //= 2
    return pieces


def split(x):
    high = x.astype(BF16)
    return high, (x - high.astype(F32)).astype(BF16)


def dot(a, b):
    return jnp.dot(a, b, preferred_element_type=F32)


def dot_t(a, b):
    return lax.dot_general(a, b, (((1,), (1,)), ((), ())), preferred_element_type=F32)


def times(a, b):
    return dot(a[0], b[0]) + (dot(a[1], b[0]) + dot(a[0], b[1]))


def total(terms):
    return functools.reduce(lambda a, b: a + b, terms)


def rows_of(x, start, size):
    return tuple(v[start : start + size] for v in x)


def halves(x):
    return tuple(v[:, :B] for v in x), tuple(v[:, B:] for v in x)


def stacked(blocks):
    blocks = [halves(block) for block in blocks]
    return tuple(
        jnp.concatenate(
            [jnp.concatenate([block[j][part] for block in blocks], axis=1) for j in range(2)], axis=0
        )
        for part in range(2)
    )


def against(lefts, rights):
    terms = []
    for i in range(0, len(lefts), 2):
        left, right = stacked(lefts[i : i + 2]), stacked(rights[i : i + 2])
        terms += [dot_t(left[0], right[0]), dot_t(left[1], right[0]), dot_t(left[0], right[1])]
    both = total(terms)
    rows = both.shape[0] // 2
    re, im = both[:rows], both[rows:]
    return jnp.concatenate([re[:, :B] + im[:, B:], re[:, B:] - im[:, :B]], axis=1)


def edge_plan(kinds, far, blocks, local, devices):
    part = local // 2
    plan = {}
    for kind in kinds:
        for odd in range(2):
            found = []
            for place, block in enumerate(blocks):
                if (kind == "over") == (odd == 0):
                    if kind == "over":
                        column = {
                            0: ("even", block) if block < part else None,
                            devices // 2: ("late", block),
                            devices - 1: ("even", part + block),
                        }.get(far)
                    else:
                        column = {
                            0: ("even", part + block),
                            1: ("even", block - part) if block >= part else None,
                        }.get(far)
                    if column:
                        found.append((place, column[0], column[1] * B))
                elif far < devices // 2:
                    found.append((place, "odd", None))
            plan[kind, odd] = found
    return plan


def in_thirds(local, devices):
    return devices == 4 and local % 2 == 0


def panel_kernel(local, far, starts, kinds, names, first, last, span, devices, scale, *refs):
    refs = list(refs)
    at_ref, g_ref = refs[:2]
    piece_refs, refs = refs[2 : 2 + len(starts)], refs[2 + len(starts) :]
    edges = "over" in kinds or "back" in kinds
    edge_refs, refs = dict(zip(names, refs)), refs[len(names) :]
    ins = {}
    for kind in kinds:
        if kind not in first:
            ins[kind] = refs.pop(0)
    outs = refs if last and "diag" in kinds else dict(zip(kinds, refs))
    pan = at_ref[0]
    source = pan ^ far
    middle = devices // 2
    half = devices * local // 2
    whole = "diag" in kinds or "upper" in kinds
    low = 0 if whole else (local - 1) * B
    top, end = (0, local) if span is None else span

    greens, sigmas, products, columns = [], [], [], []
    for start, s_ref in zip(starts, piece_refs):
        for u in range(s_ref.shape[2] // B):
            k = source * local + start + u
            columns.append(pl.ds(pl.multiple_of((k % half) * B, B), B))
            cut = pl.ds(pl.multiple_of(k * B, B), B)
            rows = slice(u * B, (u + 1) * B)
            sr, si = s_ref[0, 0, rows], s_ref[1, 0, rows]
            sigmas.append(
                split(
                    jnp.concatenate(
                        [jnp.concatenate([sr, si], axis=1), jnp.concatenate([-si, sr], axis=1)],
                        axis=0,
                    )
                )
            )
            greens.append(lambda low, high, cut=cut: split(
                jnp.concatenate([g_ref[0, 0, low:high, cut], g_ref[1, 0, low:high, cut]], axis=1)
            ))
            if whole:
                greens[-1] = functools.partial(
                    lambda whole, low, high: rows_of(whole, low - top * B, high - low),
                    greens[-1](top * B, end * B),
                )
                products.append(split(times(greens[-1](top * B, end * B), sigmas[-1])))

    def old(kind, i):
        return ins[kind][i] if kind in ins else 0.0

    def put(ref, row, value):
        ref[0, 0, row * B : (row + 1) * B] = value[:, :B].T * scale
        ref[1, 0, row * B : (row + 1) * B] = value[:, B:].T * scale

    diag, upper = "diag" in kinds, "upper" in kinds
    for i in range(top, end):
        start = 0 if diag else 1
        size = int(diag) + int(upper and i < local - 1)
        if not size:
            continue
        terms = against(
            [green((i + start) * B, (i + start + size) * B) for green in greens],
            [rows_of(product, (i - top) * B, B) for product in products],
        )
        if diag:
            value = old("diag", i) + terms[:B]
            if last:
                put(outs[0], i - top, value)
            else:
                outs["diag"][i] = value
        if upper and i < local - 1:
            value = old("upper", i) + terms[-B:]
            if last:
                put(outs["upper"], i, value)
            else:
                outs["upper"][i] = value
    if not edges:
        return
    even = pan % 2 == 0

    def rows_at(ref, column):
        return split(
            jnp.concatenate([ref[0, 0, :, column], ref[1, 0, :, column]], axis=1)
        )

    def last_rows(number):
        if whole:
            return rows_of(products[number], (local - 1) * B, B)
        return split(times(greens[number](low, local * B), sigmas[number]))

    def add(kind, when, terms):
        @pl.when(when)
        def _():
            outs[kind][0] += terms()

    for kind in ("over", "back"):
        if kind in kinds:
            outs[kind][0] = ins[kind][0] if kind in ins else jnp.zeros((B, 2 * B), F32)

    if in_thirds(local, devices):
        blocks = [
            start + u for start, ref in zip(starts, piece_refs) for u in range(ref.shape[2] // B)
        ]
        plan = edge_plan([k for k in kinds if k in ("over", "back")], far, blocks, local, devices)
        for (kind, odd), found in plan.items():
            if not found:
                continue

            def terms(kind=kind, found=found):
                taken = [
                    (n, rows_at(edge_refs[name], columns[n] if at is None else slice(at, at + B)))
                    for n, name, at in found
                ]
                if kind == "over":
                    return against([edge for _, edge in taken], [last_rows(n) for n, _ in taken])
                return against(
                    [greens[n](0, B) for n, _ in taken],
                    [split(times(edge, sigmas[n])) for n, edge in taken],
                )

            add(kind, even if odd == 0 else jnp.logical_not(even), terms)
        return

    source_high = source >= middle

    def edge(near, column):
        return tuple(
            jnp.where(near, a, b)
            for a, b in zip(rows_at(edge_refs["even"], column), rows_at(edge_refs["odd"], column))
        )

    if "over" in kinds:
        add(
            "over",
            source_high != (pan + 1 >= middle),
            lambda: against(
                [edge(even, column) for column in columns],
                [last_rows(number) for number in range(len(columns))],
            ),
        )
    if "back" in kinds:
        add(
            "back",
            source_high == (pan >= middle),
            lambda: against(
                [green(0, B) for green in greens],
                [
                    split(times(edge(jnp.logical_not(even), column), sigma))
                    for sigma, column in zip(sigmas, columns)
                ],
            ),
        )


def panel(at, green, far, pieces, carry, edges, kinds, last, span=None):
    rows = green.shape[2]
    local = rows // B
    devices = lax.axis_size("pan")
    counts = {"diag": local, "upper": local - 1, "over": 1, "back": 1}
    kinds = tuple(kind for kind in kinds if counts[kind])
    vmem = pl.BlockSpec(memory_space=pltpu.VMEM)
    starts, many = [], 0
    for start, piece in pieces:
        starts.append(start)
        many += piece.shape[2] // B
    operands = [at, green] + [piece for _, piece in pieces]
    names = []
    if "over" in kinds or "back" in kinds:
        names = ["even", "odd"]
        if in_thirds(local, devices):
            blocks = [start + u for start, piece in pieces for u in range(piece.shape[2] // B)]
            plan = edge_plan([k for k in kinds if k in ("over", "back")], far, blocks, local, devices)
            names = sorted({name for found in plan.values() for _, name, _ in found})
        operands += [edges[name] for name in names]
    shapes = {kind: jax.ShapeDtypeStruct((counts[kind], B, 2 * B), F32) for kind in kinds}
    aliases = {}
    first = []
    for number, kind in enumerate(kinds):
        if kind not in carry:
            first.append(kind)
            continue
        if not last or kind == "over":
            aliases[len(operands)] = number
        operands.append(carry[kind])
    if last:
        tall = jax.ShapeDtypeStruct((2, 1, rows, B), F32)
        shapes["upper"] = tall
        if "diag" in kinds:
            shapes = {"diag": jax.ShapeDtypeStruct((2, 1, (span[1] - span[0]) * B, B), F32)}
    full = "diag" in kinds or "upper" in kinds
    work = 3 * 2 * (2 * B) * (2 * B) * many * (rows if full else B) * (1 + len(kinds))
    out = pl.pallas_call(
        functools.partial(
            panel_kernel,
            local,
            far,
            starts,
            kinds,
            names,
            first,
            last,
            span,
            devices,
            1.0 / math.sqrt(B),
        ),
        in_specs=[pl.BlockSpec(memory_space=pltpu.SMEM)] + [vmem] * (len(operands) - 1),
        out_specs=[vmem] * len(shapes),
        out_shape=list(shapes.values()),
        input_output_aliases=aliases,
        compiler_params=pltpu.CompilerParams(vmem_limit_bytes=VMEM_BYTES),
        cost_estimate=pl.CostEstimate(
            flops=work, bytes_accessed=8 * rows * B * many, transcendentals=0
        ),
    )(*operands)
    return dict(carry, **dict(zip(shapes, out)))


def scattered(fars, modes, row, size, shift_ref, at_ref, contact_ref, col_ref, row_ref, piece_refs):
    energy = at_ref[1]
    chosen = []
    for far in fars:
        apart = jnp.abs((energy ^ far) - energy)
        chosen.append([jnp.where(apart == shift_ref[m], 1.0, 0.0).astype(F32) for m in range(modes)])
    for start in range(0, size, B):
        rows = slice(row + start, row + start + B)
        outer = [col_ref[rows, m : m + 1] * row_ref[m : m + 1, rows] for m in range(modes)]
        values = [contact_ref[0, 0, rows], contact_ref[1, 0, rows]]
        for weights, ref in zip(chosen, piece_refs):
            weight = total(w * o for w, o in zip(weights, outer))
            values = [value + weight * ref[j, 0, start : start + B] for j, value in enumerate(values)]
        yield start, values


def phonon_kernel(fars, modes, row, size, *refs):
    out_ref = refs[-1]
    for start, values in scattered(fars, modes, row, size, *refs[:5], refs[5:-1]):
        for j in range(2):
            out_ref[j, 0, start : start + B] = values[j]


def phonon(shifts, at, contact, columns, lines, pieces, number, chunks):
    parts, energies, rows = contact.shape[:3]
    size = rows // chunks
    vmem = pl.BlockSpec(memory_space=pltpu.VMEM)
    smem = pl.BlockSpec(memory_space=pltpu.SMEM)
    return pl.pallas_call(
        functools.partial(
            phonon_kernel, [far for far, _ in pieces], shifts.shape[0], number * size, size
        ),
        in_specs=[smem, smem] + [vmem] * (3 + len(pieces)),
        out_specs=vmem,
        out_shape=jax.ShapeDtypeStruct((parts, energies, size, B), F32),
        compiler_params=pltpu.CompilerParams(vmem_limit_bytes=VMEM_BYTES),
        cost_estimate=pl.CostEstimate(
            flops=size * B * 20, bytes_accessed=8 * size * B * 5, transcendentals=0
        ),
    )(shifts, at, contact, columns, lines, *[piece for _, piece in pieces])


def ending_kernel(fars, modes, rows, size, scale, *refs):
    settings, refs = refs[:5], refs[5:]
    piece_refs, refs = refs[: len(fars)], refs[len(fars) :]
    row = rows - size
    done_refs, refs = refs[: row // size], refs[row // size :]
    diag_refs, refs = refs[: rows // size], refs[rows // size :]
    _, over_ref, above_ref, sigma_ref, upper_ref, diag_ref, held, tail, sems = refs
    copies = []

    def send(source, target):
        copies.append(pltpu.make_async_copy(source, target, sems.at[len(copies)]))
        copies[-1].start()

    for refs, target in ((done_refs, sigma_ref), (diag_refs, diag_ref)):
        for number, ref in enumerate(refs):
            send(ref, target.at[:, :, pl.ds(number * size, size)])
    for j in range(2):
        part = slice(j * B, (j + 1) * B)
        tail[j, 0] = (over_ref[0, :, part] + above_ref[0, :, part]).T * scale
    send(tail, upper_ref.at[:, :, pl.ds(rows - B, B)])
    for start, values in scattered(fars, modes, row, size, *settings, piece_refs):
        for j in range(2):
            held[j, 0, start : start + B] = values[j]
        send(held.at[:, :, pl.ds(start, B)], sigma_ref.at[:, :, pl.ds(row + start, B)])
    for copy in copies:
        copy.wait()


def ending(shifts, at, contact, columns, lines, pieces, done, diag, upper, over, above):
    parts, energies, rows = contact.shape[:3]
    size = rows // (len(done) + 1)
    vmem = pl.BlockSpec(memory_space=pltpu.VMEM)
    smem = pl.BlockSpec(memory_space=pltpu.SMEM)
    hbm = pl.BlockSpec(memory_space=pl.ANY)
    operands = [shifts, at, contact, columns, lines, *[piece for _, piece in pieces], *done, *diag]
    specs = [smem, smem] + [vmem] * (len(operands) - 2) + [hbm, vmem, vmem]
    return pl.pallas_call(
        functools.partial(ending_kernel, [far for far, _ in pieces], shifts.shape[0], rows, size, 1.0 / math.sqrt(B)),
        in_specs=specs,
        out_specs=[hbm] * 3,
        out_shape=[jax.ShapeDtypeStruct(contact.shape, F32)] * 3,
        input_output_aliases={len(operands): 1},
        scratch_shapes=[
            pltpu.VMEM((parts, energies, size, B), F32),
            pltpu.VMEM((parts, energies, B, B), F32),
            pltpu.SemaphoreType.DMA((len(done) + len(diag) + 1 + size // B,)),
        ],
        compiler_params=pltpu.CompilerParams(vmem_limit_bytes=VMEM_BYTES),
        cost_estimate=pl.CostEstimate(
            flops=size * B * 20, bytes_accessed=8 * size * B * 5, transcendentals=0
        ),
    )(*operands, upper, over, above)


def cut_kernel(contact_ref, *refs):
    outs, sems = refs[:-1], refs[-1]
    copies = []
    start = 0
    for number, ref in enumerate(outs):
        size = ref.shape[2]
        at = 0 if number == len(outs) - 1 else start
        start += size
        copies.append(
            pltpu.make_async_copy(contact_ref.at[:, :, pl.ds(at, size)], ref, sems.at[number])
        )
    for copy in copies:
        copy.start()
    for copy in copies:
        copy.wait()


def cut(contact, chunks):
    parts, energies, rows = contact.shape[:3]
    part = jax.ShapeDtypeStruct((parts, energies, rows // chunks, B), F32)
    vmem = pl.BlockSpec(memory_space=pltpu.VMEM)
    return pl.pallas_call(
        cut_kernel,
        in_specs=[pl.BlockSpec(memory_space=pltpu.HBM)],
        out_specs=[vmem] * (chunks + 1),
        out_shape=[part] * chunks + [jax.ShapeDtypeStruct(contact.shape, F32)],
        scratch_shapes=[pltpu.SemaphoreType.DMA((chunks + 1,))],
        compiler_params=pltpu.CompilerParams(vmem_limit_bytes=VMEM_BYTES),
        cost_estimate=pl.CostEstimate(
            flops=0, bytes_accessed=32 * rows * B, transcendentals=0
        ),
        name="cut",
    )(contact)


def edge_rows(retarded, pan):
    rows, columns = retarded.shape[2:]
    devices = lax.axis_size("pan")
    local = rows // B
    middle = devices // 2
    thirds = in_thirds(local, devices)
    even = pan % 2 == 0

    def take(row, column, size):
        return lax.dynamic_slice(retarded, (0, 0, row, column), (2, 1, B, size))

    found, cuts = {}, []
    for odd, name in ((0, "even"), (1, "odd")):
        up = pan % 2 == odd
        row = jnp.where(up, rows - B, 0)
        if odd or not thirds:
            up_start = (pan + 1 >= middle).astype(jnp.int32)
            down_start = (pan < middle).astype(jnp.int32)
            column = jnp.where(up, up_start, down_start) * (columns // 2)
            part = take(row, column, columns // 2)
        else:
            short = jnp.where(even, pan * rows + rows // 2, (pan - 1) * rows)
            long = jnp.where(even, pan + 1, pan ^ middle) * rows
            part = jnp.concatenate([take(row, short, rows // 2), take(row, long, rows)], axis=3)
        pairs = []
        for i in range(odd, devices - 1, 2):
            pairs += [(i, i + 1), (i + 1, i)]
        cuts.append(part)
        found[name] = lax.ppermute(part, "pan", pairs)
    if thirds:
        part = take(0, (pan ^ (devices - 1)) * rows, rows)
        cuts.append(part)
        found["late"] = swapped(part, "pan", 1)
    return found, cuts


def gathered(near, chunks):
    size = chunks[0].shape[2] // B
    parts = [(i * size, chunk) for i, chunk in enumerate(chunks)]
    first = lax.axis_size("pan") // 2
    pieces = [(0, near)]
    bit = first
    while bit:
        found = []
        for far, piece in pieces:
            if bit == first:
                piece = parts
            sent = []
            for start, block in piece:
                sent.append((start, swapped(block, "pan", bit)))
            found.append((far ^ bit, sent))
        pieces += found
        bit //= 2
    return pieces


def body(retarded, contact, atom_kind, coupling, shifts):
    rows = retarded.shape[2]
    local = rows // B
    chunks = 2 if local % 2 == 0 else 1
    high = lax.axis_size("pan") // 2
    pan = lax.axis_index("pan").astype(jnp.int32)
    energy = lax.axis_index("en").astype(jnp.int32)
    at = jnp.where(jnp.arange(2, dtype=jnp.int32) == 0, pan, energy)
    atoms = rows // ORB
    kinds = lax.dynamic_slice_in_dim(atom_kind, pan * atoms, atoms, 0)
    per_atom = sum(jnp.where(kinds[:, None] == kind, coupling[kind][None, :], 0.0) for kind in range(coupling.shape[0]))
    per_row = jnp.repeat(per_atom, ORB, axis=0)
    per_line = jnp.repeat(per_atom.T, ORB, axis=1)
    edges, cuts = edge_rows(retarded, pan)
    *parts, copied = cut(contact, chunks)
    near = [(0, contact)]
    for rounds in range(ITERS):
        final = rounds == ITERS - 1
        pieces = gathered(near, parts)
        if rounds == 0:
            ready = lax.optimization_barrier((copied, per_row, per_line, *cuts))
            pieces[0] = (0, [(0, ready[0])])
            copied, per_row, per_line = ready[:3]
        groups = [(far, 0, blocks) for far, blocks in pieces[:-1]]
        groups.sort(key=lambda group: (group[0] != 0, group[0] >= high))
        if chunks > 1 and high > 1:
            far, _, blocks = groups.pop([far for far, _, _ in groups].index(high))
            groups.insert(1, (far, 0, blocks[:1]))
            groups.append((far, 1, blocks[1:]))
            for place, (near_far, _, blocks) in enumerate(groups):
                if near_far == 1 and len(blocks) > 1:
                    groups[place] = (1, 0, blocks[:1])
                    groups.append((1, 1, blocks[1:]))
                    break
        sums = {}
        for far, number, blocks in groups:
            work = ("diag", "upper") if final else ("diag",)
            if final and 0 < far < high:
                if "over" not in sums:
                    sums = panel(at, retarded, 0, pieces[0][1], sums, edges, ("over", "back"), False)
                work += ("over", "back")
            sums = panel(at, retarded, far, blocks, sums, edges, work, False)
        far, blocks = pieces[-1]
        for block in blocks[:-1]:
            sums = panel(at, retarded, far, [block], sums, edges, ("diag",), False)
        diags = []
        for number in range(chunks):
            span = (number * local // chunks, (number + 1) * local // chunks)
            made = panel(at, retarded, far, blocks[-1:], sums, edges, ("diag",), True, span)
            diags.append(made["diag"])
        found = spread(diags, "en")
        settings = (shifts, at, copied, per_row, per_line)
        if not final:
            parts = [phonon(*settings, own[1:], number, chunks) for number, own in enumerate(found)]
            near = [(i * (local // chunks), part) for i, part in enumerate(parts)]
    devices = lax.axis_size("pan")
    above = lax.ppermute(sums["back"], "pan", [(i + 1, i) for i in range(devices - 1)])
    far, blocks = pieces[-1]
    sums = panel(at, retarded, far, blocks, sums, edges, ("upper", "over"), True)
    for far, blocks in pieces[1:-1]:
        if far >= high:
            sums = panel(at, retarded, far, blocks, sums, edges, ("over",), False)
    done = [phonon(*settings, own[1:], number, chunks) for number, own in enumerate(found[:-1])]
    sigma, upper, diag = ending(*settings, found[-1][1:], done, diags, sums["upper"], sums["over"], above)
    return (diag, upper, sigma)


def solution(mesh):
    def step(retarded, *args):
        spread_spec = P(None, ("grp", "en"), "pan", None)
        inner = jax.shard_map(
            body,
            mesh=mesh,
            in_specs=(spread_spec, spread_spec, P(), P(), P()),
            out_specs=(spread_spec, spread_spec, spread_spec),
            check_vma=False,
        )
        return inner(retarded, *args)

    return step
```

```python
import functools
import math

import jax
import jax.numpy as jnp
from jax import lax
from jax.experimental import pallas as pl
from jax.experimental.pallas import tpu as pltpu
from jax.sharding import PartitionSpec as P


B = 128
ORB = 8
ITERS = 2
VMEM_BYTES = 28 * 2**20

F32 = jnp.float32
BF16 = jnp.bfloat16


def swapped(x, axis, bit):
    return lax.ppermute(x, axis, [(i, i ^ bit) for i in range(lax.axis_size(axis))])


def spread(chunks, axis):
    pieces = [[(0, chunk)] for chunk in chunks]
    bit = lax.axis_size(axis) // 2
    while bit:
        for own in pieces:
            found = []
            for far, piece in own:
                found.append((far ^ bit, swapped(piece, axis, bit)))
            own += found
        bit //= 2
    return pieces


def split(x):
    high = x.astype(BF16)
    return high, (x - high.astype(F32)).astype(BF16)


def dot(a, b):
    return jnp.dot(a, b, preferred_element_type=F32)


def dot_t(a, b):
    return lax.dot_general(a, b, (((1,), (1,)), ((), ())), preferred_element_type=F32)


def times(a, b):
    return dot(a[0], b[0]) + (dot(a[1], b[0]) + dot(a[0], b[1]))


def total(terms):
    return functools.reduce(lambda a, b: a + b, terms)


def rows_of(x, start, size):
    return tuple(v[start : start + size] for v in x)


def halves(x):
    return tuple(v[:, :B] for v in x), tuple(v[:, B:] for v in x)


def stacked(blocks):
    blocks = [halves(block) for block in blocks]
    return tuple(
        jnp.concatenate(
            [jnp.concatenate([block[j][part] for block in blocks], axis=1) for j in range(2)], axis=0
        )
        for part in range(2)
    )


def against(lefts, rights):
    terms = []
    for i in range(0, len(lefts), 2):
        left, right = stacked(lefts[i : i + 2]), stacked(rights[i : i + 2])
        terms += [dot_t(left[0], right[0]), dot_t(left[1], right[0]), dot_t(left[0], right[1])]
    both = total(terms)
    rows = both.shape[0] // 2
    re, im = both[:rows], both[rows:]
    return jnp.concatenate([re[:, :B] + im[:, B:], re[:, B:] - im[:, :B]], axis=1)


def edge_plan(kinds, far, blocks, local, devices):
    part = local // 2
    plan = {}
    for kind in kinds:
        for odd in range(2):
            found = []
            for place, block in enumerate(blocks):
                if (kind == "over") == (odd == 0):
                    if kind == "over":
                        column = {
                            0: ("even", block) if block < part else None,
                            devices // 2: ("late", block),
                            devices - 1: ("even", part + block),
                        }.get(far)
                    else:
                        column = {
                            0: ("even", part + block),
                            1: ("even", block - part) if block >= part else None,
                        }.get(far)
                    if column:
                        found.append((place, column[0], column[1] * B))
                elif far < devices // 2:
                    found.append((place, "odd", None))
            plan[kind, odd] = found
    return plan


def in_thirds(local, devices):
    return devices == 4 and local % 2 == 0


def panel_kernel(local, far, starts, kinds, names, first, last, span, devices, scale, *refs):
    refs = list(refs)
    at_ref, g_ref = refs[:2]
    piece_refs, refs = refs[2 : 2 + len(starts)], refs[2 + len(starts) :]
    edges = "over" in kinds or "back" in kinds
    edge_refs, refs = dict(zip(names, refs)), refs[len(names) :]
    ins = {}
    for kind in kinds:
        if kind not in first:
            ins[kind] = refs.pop(0)
    outs = refs if last and "diag" in kinds else dict(zip(kinds, refs))
    pan = at_ref[0]
    source = pan ^ far
    middle = devices // 2
    half = devices * local // 2
    whole = "diag" in kinds or "upper" in kinds
    low = 0 if whole else (local - 1) * B
    top, end = (0, local) if span is None else span

    greens, sigmas, products, columns = [], [], [], []
    for start, s_ref in zip(starts, piece_refs):
        for u in range(s_ref.shape[2] // B):
            k = source * local + start + u
            columns.append(pl.ds(pl.multiple_of((k % half) * B, B), B))
            cut = pl.ds(pl.multiple_of(k * B, B), B)
            rows = slice(u * B, (u + 1) * B)
            sr, si = s_ref[0, 0, rows], s_ref[1, 0, rows]
            sigmas.append(
                split(
                    jnp.concatenate(
                        [jnp.concatenate([sr, si], axis=1), jnp.concatenate([-si, sr], axis=1)],
                        axis=0,
                    )
                )
            )
            greens.append(lambda low, high, cut=cut: split(
                jnp.concatenate([g_ref[0, 0, low:high, cut], g_ref[1, 0, low:high, cut]], axis=1)
            ))
            if whole:
                greens[-1] = functools.partial(
                    lambda whole, low, high: rows_of(whole, low - top * B, high - low),
                    greens[-1](top * B, end * B),
                )
                products.append(split(times(greens[-1](top * B, end * B), sigmas[-1])))

    def old(kind, i):
        return ins[kind][i] if kind in ins else 0.0

    def put(ref, row, value):
        ref[0, 0, row * B : (row + 1) * B] = value[:, :B].T * scale
        ref[1, 0, row * B : (row + 1) * B] = value[:, B:].T * scale

    diag, upper = "diag" in kinds, "upper" in kinds
    for i in range(top, end):
        start = 0 if diag else 1
        size = int(diag) + int(upper and i < local - 1)
        if not size:
            continue
        terms = against(
            [green((i + start) * B, (i + start + size) * B) for green in greens],
            [rows_of(product, (i - top) * B, B) for product in products],
        )
        if diag:
            value = old("diag", i) + terms[:B]
            if last:
                put(outs[0], i - top, value)
            else:
                outs["diag"][i] = value
        if upper and i < local - 1:
            value = old("upper", i) + terms[-B:]
            if last:
                put(outs["upper"], i, value)
            else:
                outs["upper"][i] = value
    if not edges:
        return
    even = pan % 2 == 0

    def rows_at(ref, column):
        return split(
            jnp.concatenate([ref[0, 0, :, column], ref[1, 0, :, column]], axis=1)
        )

    def last_rows(number):
        if whole:
            return rows_of(products[number], (local - 1) * B, B)
        return split(times(greens[number](low, local * B), sigmas[number]))

    def add(kind, when, terms):
        @pl.when(when)
        def _():
            outs[kind][0] += terms()

    for kind in ("over", "back"):
        if kind in kinds:
            outs[kind][0] = ins[kind][0] if kind in ins else jnp.zeros((B, 2 * B), F32)

    if in_thirds(local, devices):
        blocks = [
            start + u for start, ref in zip(starts, piece_refs) for u in range(ref.shape[2] // B)
        ]
        plan = edge_plan([k for k in kinds if k in ("over", "back")], far, blocks, local, devices)
        for (kind, odd), found in plan.items():
            if not found:
                continue

            def terms(kind=kind, found=found):
                taken = [
                    (n, rows_at(edge_refs[name], columns[n] if at is None else slice(at, at + B)))
                    for n, name, at in found
                ]
                if kind == "over":
                    return against([edge for _, edge in taken], [last_rows(n) for n, _ in taken])
                return against(
                    [greens[n](0, B) for n, _ in taken],
                    [split(times(edge, sigmas[n])) for n, edge in taken],
                )

            add(kind, even if odd == 0 else jnp.logical_not(even), terms)
        return

    source_high = source >= middle

    def edge(near, column):
        return tuple(
            jnp.where(near, a, b)
            for a, b in zip(rows_at(edge_refs["even"], column), rows_at(edge_refs["odd"], column))
        )

    if "over" in kinds:
        add(
            "over",
            source_high != (pan + 1 >= middle),
            lambda: against(
                [edge(even, column) for column in columns],
                [last_rows(number) for number in range(len(columns))],
            ),
        )
    if "back" in kinds:
        add(
            "back",
            source_high == (pan >= middle),
            lambda: against(
                [green(0, B) for green in greens],
                [
                    split(times(edge(jnp.logical_not(even), column), sigma))
                    for sigma, column in zip(sigmas, columns)
                ],
            ),
        )


def panel(at, green, far, pieces, carry, edges, kinds, last, span=None):
    rows = green.shape[2]
    local = rows // B
    devices = lax.axis_size("pan")
    counts = {"diag": local, "upper": local - 1, "over": 1, "back": 1}
    kinds = tuple(kind for kind in kinds if counts[kind])
    vmem = pl.BlockSpec(memory_space=pltpu.VMEM)
    starts, many = [], 0
    for start, piece in pieces:
        starts.append(start)
        many += piece.shape[2] // B
    operands = [at, green] + [piece for _, piece in pieces]
    names = []
    if "over" in kinds or "back" in kinds:
        names = ["even", "odd"]
        if in_thirds(local, devices):
            blocks = [start + u for start, piece in pieces for u in range(piece.shape[2] // B)]
            plan = edge_plan([k for k in kinds if k in ("over", "back")], far, blocks, local, devices)
            names = sorted({name for found in plan.values() for _, name, _ in found})
        operands += [edges[name] for name in names]
    shapes = {kind: jax.ShapeDtypeStruct((counts[kind], B, 2 * B), F32) for kind in kinds}
    aliases = {}
    first = []
    for number, kind in enumerate(kinds):
        if kind not in carry:
            first.append(kind)
            continue
        if not last or kind == "over":
            aliases[len(operands)] = number
        operands.append(carry[kind])
    if last:
        tall = jax.ShapeDtypeStruct((2, 1, rows, B), F32)
        shapes["upper"] = tall
        if "diag" in kinds:
            shapes = {"diag": jax.ShapeDtypeStruct((2, 1, (span[1] - span[0]) * B, B), F32)}
    full = "diag" in kinds or "upper" in kinds
    work = 3 * 2 * (2 * B) * (2 * B) * many * (rows if full else B) * (1 + len(kinds))
    out = pl.pallas_call(
        functools.partial(
            panel_kernel,
            local,
            far,
            starts,
            kinds,
            names,
            first,
            last,
            span,
            devices,
            1.0 / math.sqrt(B),
        ),
        in_specs=[pl.BlockSpec(memory_space=pltpu.SMEM)] + [vmem] * (len(operands) - 1),
        out_specs=[vmem] * len(shapes),
        out_shape=list(shapes.values()),
        input_output_aliases=aliases,
        compiler_params=pltpu.CompilerParams(vmem_limit_bytes=VMEM_BYTES),
        cost_estimate=pl.CostEstimate(
            flops=work, bytes_accessed=8 * rows * B * many, transcendentals=0
        ),
    )(*operands)
    return dict(carry, **dict(zip(shapes, out)))


def scattered(fars, modes, row, size, shift_ref, at_ref, contact_ref, col_ref, row_ref, piece_refs):
    energy = at_ref[1]
    chosen = []
    for far in fars:
        apart = jnp.abs((energy ^ far) - energy)
        chosen.append([jnp.where(apart == shift_ref[m], 1.0, 0.0).astype(F32) for m in range(modes)])
    for start in range(0, size, B):
        rows = slice(row + start, row + start + B)
        outer = [col_ref[rows, m : m + 1] * row_ref[m : m + 1, rows] for m in range(modes)]
        values = [contact_ref[0, 0, rows], contact_ref[1, 0, rows]]
        for weights, ref in zip(chosen, piece_refs):
            weight = total(w * o for w, o in zip(weights, outer))
            values = [value + weight * ref[j, 0, start : start + B] for j, value in enumerate(values)]
        yield start, values


def phonon_kernel(fars, modes, row, size, *refs):
    out_ref = refs[-1]
    for start, values in scattered(fars, modes, row, size, *refs[:5], refs[5:-1]):
        for j in range(2):
            out_ref[j, 0, start : start + B] = values[j]


def phonon(shifts, at, contact, columns, lines, pieces, number, chunks):
    parts, energies, rows = contact.shape[:3]
    size = rows // chunks
    vmem = pl.BlockSpec(memory_space=pltpu.VMEM)
    smem = pl.BlockSpec(memory_space=pltpu.SMEM)
    return pl.pallas_call(
        functools.partial(
            phonon_kernel, [far for far, _ in pieces], shifts.shape[0], number * size, size
        ),
        in_specs=[smem, smem] + [vmem] * (3 + len(pieces)),
        out_specs=vmem,
        out_shape=jax.ShapeDtypeStruct((parts, energies, size, B), F32),
        compiler_params=pltpu.CompilerParams(vmem_limit_bytes=VMEM_BYTES),
        cost_estimate=pl.CostEstimate(
            flops=size * B * 20, bytes_accessed=8 * size * B * 5, transcendentals=0
        ),
    )(shifts, at, contact, columns, lines, *[piece for _, piece in pieces])


def ending_kernel(fars, modes, rows, size, scale, *refs):
    settings, refs = refs[:5], refs[5:]
    piece_refs, refs = refs[: len(fars)], refs[len(fars) :]
    row = rows - size
    done_refs, refs = refs[: row // size], refs[row // size :]
    diag_refs, refs = refs[: rows // size], refs[rows // size :]
    _, over_ref, above_ref, sigma_ref, upper_ref, diag_ref, held, tail, sems = refs
    copies = []

    def send(source, target):
        copies.append(pltpu.make_async_copy(source, target, sems.at[len(copies)]))
        copies[-1].start()

    for refs, target in ((done_refs, sigma_ref), (diag_refs, diag_ref)):
        for number, ref in enumerate(refs):
            send(ref, target.at[:, :, pl.ds(number * size, size)])
    for j in range(2):
        part = slice(j * B, (j + 1) * B)
        tail[j, 0] = (over_ref[0, :, part] + above_ref[0, :, part]).T * scale
    send(tail, upper_ref.at[:, :, pl.ds(rows - B, B)])
    for start, values in scattered(fars, modes, row, size, *settings, piece_refs):
        for j in range(2):
            held[j, 0, start : start + B] = values[j]
        send(held.at[:, :, pl.ds(start, B)], sigma_ref.at[:, :, pl.ds(row + start, B)])
    for copy in copies:
        copy.wait()


def ending(shifts, at, contact, columns, lines, pieces, done, diag, upper, over, above):
    parts, energies, rows = contact.shape[:3]
    size = rows // (len(done) + 1)
    vmem = pl.BlockSpec(memory_space=pltpu.VMEM)
    smem = pl.BlockSpec(memory_space=pltpu.SMEM)
    hbm = pl.BlockSpec(memory_space=pl.ANY)
    operands = [shifts, at, contact, columns, lines, *[piece for _, piece in pieces], *done, *diag]
    specs = [smem, smem] + [vmem] * (len(operands) - 2) + [hbm, vmem, vmem]
    return pl.pallas_call(
        functools.partial(ending_kernel, [far for far, _ in pieces], shifts.shape[0], rows, size, 1.0 / math.sqrt(B)),
        in_specs=specs,
        out_specs=[hbm] * 3,
        out_shape=[jax.ShapeDtypeStruct(contact.shape, F32)] * 3,
        input_output_aliases={len(operands): 1},
        scratch_shapes=[
            pltpu.VMEM((parts, energies, size, B), F32),
            pltpu.VMEM((parts, energies, B, B), F32),
            pltpu.SemaphoreType.DMA((len(done) + len(diag) + 1 + size // B,)),
        ],
        compiler_params=pltpu.CompilerParams(vmem_limit_bytes=VMEM_BYTES),
        cost_estimate=pl.CostEstimate(
            flops=size * B * 20, bytes_accessed=8 * size * B * 5, transcendentals=0
        ),
    )(*operands, upper, over, above)


def cut_kernel(contact_ref, *refs):
    outs, sems = refs[:-1], refs[-1]
    copies = []
    start = 0
    for number, ref in enumerate(outs):
        size = ref.shape[2]
        at = 0 if number == len(outs) - 1 else start
        start += size
        copies.append(
            pltpu.make_async_copy(contact_ref.at[:, :, pl.ds(at, size)], ref, sems.at[number])
        )
    for copy in copies:
        copy.start()
    for copy in copies:
        copy.wait()


def cut(contact, chunks):
    parts, energies, rows = contact.shape[:3]
    part = jax.ShapeDtypeStruct((parts, energies, rows // chunks, B), F32)
    vmem = pl.BlockSpec(memory_space=pltpu.VMEM)
    return pl.pallas_call(
        cut_kernel,
        in_specs=[pl.BlockSpec(memory_space=pltpu.HBM)],
        out_specs=[vmem] * (chunks + 1),
        out_shape=[part] * chunks + [jax.ShapeDtypeStruct(contact.shape, F32)],
        scratch_shapes=[pltpu.SemaphoreType.DMA((chunks + 1,))],
        compiler_params=pltpu.CompilerParams(vmem_limit_bytes=VMEM_BYTES),
        cost_estimate=pl.CostEstimate(
            flops=0, bytes_accessed=32 * rows * B, transcendentals=0
        ),
        name="cut",
    )(contact)


def edge_rows(retarded, pan):
    rows, columns = retarded.shape[2:]
    devices = lax.axis_size("pan")
    local = rows // B
    middle = devices // 2
    thirds = in_thirds(local, devices)
    even = pan % 2 == 0

    def take(row, column, size):
        return lax.dynamic_slice(retarded, (0, 0, row, column), (2, 1, B, size))

    found, cuts = {}, []
    for odd, name in ((0, "even"), (1, "odd")):
        up = pan % 2 == odd
        row = jnp.where(up, rows - B, 0)
        if odd or not thirds:
            up_start = (pan + 1 >= middle).astype(jnp.int32)
            down_start = (pan < middle).astype(jnp.int32)
            column = jnp.where(up, up_start, down_start) * (columns // 2)
            part = take(row, column, columns // 2)
        else:
            short = jnp.where(even, pan * rows + rows // 2, (pan - 1) * rows)
            long = jnp.where(even, pan + 1, pan ^ middle) * rows
            part = jnp.concatenate([take(row, short, rows // 2), take(row, long, rows)], axis=3)
        pairs = []
        for i in range(odd, devices - 1, 2):
            pairs += [(i, i + 1), (i + 1, i)]
        cuts.append(part)
        found[name] = lax.ppermute(part, "pan", pairs)
    if thirds:
        part = take(0, (pan ^ (devices - 1)) * rows, rows)
        cuts.append(part)
        found["late"] = swapped(part, "pan", 1)
    return found, cuts


def gathered(near, chunks):
    size = chunks[0].shape[2] // B
    parts = [(i * size, chunk) for i, chunk in enumerate(chunks)]
    first = lax.axis_size("pan") // 2
    pieces = [(0, near)]
    bit = first
    while bit:
        found = []
        for far, piece in pieces:
            if bit == first:
                piece = parts
            sent = []
            for start, block in piece:
                sent.append((start, swapped(block, "pan", bit)))
            found.append((far ^ bit, sent))
        pieces += found
        bit //= 2
    return pieces


def body(retarded, contact, atom_kind, coupling, shifts):
    rows = retarded.shape[2]
    local = rows // B
    chunks = 2 if local % 2 == 0 else 1
    high = lax.axis_size("pan") // 2
    pan = lax.axis_index("pan").astype(jnp.int32)
    energy = lax.axis_index("en").astype(jnp.int32)
    at = jnp.where(jnp.arange(2, dtype=jnp.int32) == 0, pan, energy)
    atoms = rows // ORB
    kinds = lax.dynamic_slice_in_dim(atom_kind, pan * atoms, atoms, 0)
    per_atom = sum(jnp.where(kinds[:, None] == kind, coupling[kind][None, :], 0.0) for kind in range(coupling.shape[0]))
    per_row = jnp.repeat(per_atom, ORB, axis=0)
    per_line = jnp.repeat(per_atom.T, ORB, axis=1)
    edges, cuts = edge_rows(retarded, pan)
    *parts, copied = cut(contact, chunks)
    near = [(0, contact)]
    for rounds in range(ITERS):
        final = rounds == ITERS - 1
        pieces = gathered(near, parts)
        if rounds == 0:
            ready = lax.optimization_barrier((copied, per_row, per_line, *cuts))
            pieces[0] = (0, [(0, ready[0])])
            copied, per_row, per_line = ready[:3]
        groups = [(far, 0, blocks) for far, blocks in pieces[:-1]]
        groups.sort(key=lambda group: (group[0] != 0, group[0] >= high))
        if chunks > 1 and high > 1:
            far, _, blocks = groups.pop([far for far, _, _ in groups].index(high))
            groups.insert(1, (far, 0, blocks[:1]))
            groups.append((far, 1, blocks[1:]))
            for place, (near_far, _, blocks) in enumerate(groups):
                if near_far == 1 and len(blocks) > 1:
                    groups[place] = (1, 0, blocks[:1])
                    groups.append((1, 1, blocks[1:]))
                    break
        sums = {}
        for far, number, blocks in groups:
            work = ("diag", "upper") if final else ("diag",)
            if final and 0 < far < high:
                if "over" not in sums:
                    sums = panel(at, retarded, 0, pieces[0][1], sums, edges, ("over", "back"), False)
                work += ("over", "back")
            sums = panel(at, retarded, far, blocks, sums, edges, work, False)
        far, blocks = pieces[-1]
        for block in blocks[:-1]:
            work = ("diag", "upper", "over") if final else ("diag",)
            sums = panel(at, retarded, far, [block], sums, edges, work, False)
        diags = []
        for number in range(chunks):
            span = (number * local // chunks, (number + 1) * local // chunks)
            made = panel(at, retarded, far, blocks[-1:], sums, edges, ("diag",), True, span)
            diags.append(made["diag"])
        found = spread(diags, "en")
        settings = (shifts, at, copied, per_row, per_line)
        if not final:
            parts = [phonon(*settings, own[1:], number, chunks) for number, own in enumerate(found)]
            near = [(i * (local // chunks), part) for i, part in enumerate(parts)]
    devices = lax.axis_size("pan")
    above = lax.ppermute(sums["back"], "pan", [(i + 1, i) for i in range(devices - 1)])
    far, blocks = pieces[-1]
    sums = panel(at, retarded, far, blocks[-1:], sums, edges, ("upper", "over"), True)
    for far, blocks in pieces[1:-1]:
        if far >= high:
            sums = panel(at, retarded, far, blocks, sums, edges, ("over",), False)
    done = [phonon(*settings, own[1:], number, chunks) for number, own in enumerate(found[:-1])]
    sigma, upper, diag = ending(*settings, found[-1][1:], done, diags, sums["upper"], sums["over"], above)
    return (diag, upper, sigma)


def solution(mesh):
    def step(retarded, *args):
        spread_spec = P(None, ("grp", "en"), "pan", None)
        inner = jax.shard_map(
            body,
            mesh=mesh,
            in_specs=(spread_spec, spread_spec, P(), P(), P()),
            out_specs=(spread_spec, spread_spec, spread_spec),
            check_vma=False,
        )
        return inner(retarded, *args)

    return step
```

```python
import functools
import math

import jax
import jax.numpy as jnp
from jax import lax
from jax.experimental import pallas as pl
from jax.experimental.pallas import tpu as pltpu
from jax.sharding import PartitionSpec as P


B = 128
ORB = 8
ITERS = 2
VMEM_BYTES = 28 * 2**20

F32 = jnp.float32
BF16 = jnp.bfloat16


def swapped(x, axis, bit):
    return lax.ppermute(x, axis, [(i, i ^ bit) for i in range(lax.axis_size(axis))])


def spread(chunks, axis):
    pieces = [[(0, chunk)] for chunk in chunks]
    bit = lax.axis_size(axis) // 2
    while bit:
        for own in pieces:
            found = []
            for far, piece in own:
                found.append((far ^ bit, swapped(piece, axis, bit)))
            own += found
        bit //= 2
    return pieces


def split(x):
    high = x.astype(BF16)
    return high, (x - high.astype(F32)).astype(BF16)


def dot(a, b):
    return jnp.dot(a, b, preferred_element_type=F32)


def dot_t(a, b):
    return lax.dot_general(a, b, (((1,), (1,)), ((), ())), preferred_element_type=F32)


def times(a, b):
    return dot(a[0], b[0]) + (dot(a[1], b[0]) + dot(a[0], b[1]))


def total(terms):
    return functools.reduce(lambda a, b: a + b, terms)


def rows_of(x, start, size):
    return tuple(v[start : start + size] for v in x)


def halves(x):
    return tuple(v[:, :B] for v in x), tuple(v[:, B:] for v in x)


def stacked(blocks):
    blocks = [halves(block) for block in blocks]
    return tuple(
        jnp.concatenate(
            [jnp.concatenate([block[j][part] for block in blocks], axis=1) for j in range(2)], axis=0
        )
        for part in range(2)
    )


def against(lefts, rights):
    terms = []
    for i in range(0, len(lefts), 2):
        left, right = stacked(lefts[i : i + 2]), stacked(rights[i : i + 2])
        terms += [dot_t(left[0], right[0]), dot_t(left[1], right[0]), dot_t(left[0], right[1])]
    both = total(terms)
    rows = both.shape[0] // 2
    re, im = both[:rows], both[rows:]
    return jnp.concatenate([re[:, :B] + im[:, B:], re[:, B:] - im[:, :B]], axis=1)


def edge_plan(kinds, far, blocks, local, devices):
    part = local // 2
    plan = {}
    for kind in kinds:
        for odd in range(2):
            found = []
            for place, block in enumerate(blocks):
                if (kind == "over") == (odd == 0):
                    if kind == "over":
                        column = {
                            0: ("even", block) if block < part else None,
                            devices // 2: ("late", block),
                            devices - 1: ("even", part + block),
                        }.get(far)
                    else:
                        column = {
                            0: ("even", part + block),
                            1: ("even", block - part) if block >= part else None,
                        }.get(far)
                    if column:
                        found.append((place, column[0], column[1] * B))
                elif far < devices // 2:
                    found.append((place, "odd", None))
            plan[kind, odd] = found
    return plan


def in_thirds(local, devices):
    return devices == 4 and local % 2 == 0


def panel_kernel(local, far, starts, kinds, names, first, last, span, devices, scale, *refs):
    refs = list(refs)
    at_ref, g_ref = refs[:2]
    piece_refs, refs = refs[2 : 2 + len(starts)], refs[2 + len(starts) :]
    edges = "over" in kinds or "back" in kinds
    edge_refs, refs = dict(zip(names, refs)), refs[len(names) :]
    ins = {}
    for kind in kinds:
        if kind not in first:
            ins[kind] = refs.pop(0)
    outs = refs if last and "diag" in kinds else dict(zip(kinds, refs))
    pan = at_ref[0]
    source = pan ^ far
    middle = devices // 2
    half = devices * local // 2
    whole = "diag" in kinds or "upper" in kinds
    low = 0 if whole else (local - 1) * B
    top, end = (0, local) if span is None else span

    greens, sigmas, products, columns = [], [], [], []
    for (start, piece_far), s_ref in zip(starts, piece_refs):
        for u in range(s_ref.shape[2] // B):
            k = (pan ^ piece_far) * local + start + u
            columns.append(pl.ds(pl.multiple_of((k % half) * B, B), B))
            cut = pl.ds(pl.multiple_of(k * B, B), B)
            rows = slice(u * B, (u + 1) * B)
            sr, si = s_ref[0, 0, rows], s_ref[1, 0, rows]
            sigmas.append(
                split(
                    jnp.concatenate(
                        [jnp.concatenate([sr, si], axis=1), jnp.concatenate([-si, sr], axis=1)],
                        axis=0,
                    )
                )
            )
            greens.append(lambda low, high, cut=cut: split(
                jnp.concatenate([g_ref[0, 0, low:high, cut], g_ref[1, 0, low:high, cut]], axis=1)
            ))
            if whole:
                greens[-1] = functools.partial(
                    lambda whole, low, high: rows_of(whole, low - top * B, high - low),
                    greens[-1](top * B, end * B),
                )
                products.append(split(times(greens[-1](top * B, end * B), sigmas[-1])))

    def old(kind, i):
        return ins[kind][i] if kind in ins else 0.0

    def put(ref, row, value):
        ref[0, 0, row * B : (row + 1) * B] = value[:, :B].T * scale
        ref[1, 0, row * B : (row + 1) * B] = value[:, B:].T * scale

    diag, upper = "diag" in kinds, "upper" in kinds
    for i in range(top, end):
        start = 0 if diag else 1
        size = int(diag) + int(upper and i < local - 1)
        if not size:
            continue
        terms = against(
            [green((i + start) * B, (i + start + size) * B) for green in greens],
            [rows_of(product, (i - top) * B, B) for product in products],
        )
        if diag:
            value = old("diag", i) + terms[:B]
            if last:
                put(outs[0], i - top, value)
            else:
                outs["diag"][i] = value
        if upper and i < local - 1:
            value = old("upper", i) + terms[-B:]
            if last:
                put(outs["upper"], i, value)
            else:
                outs["upper"][i] = value
    if not edges:
        return
    even = pan % 2 == 0

    def rows_at(ref, column):
        return split(
            jnp.concatenate([ref[0, 0, :, column], ref[1, 0, :, column]], axis=1)
        )

    def last_rows(number):
        if whole:
            return rows_of(products[number], (local - 1) * B, B)
        return split(times(greens[number](low, local * B), sigmas[number]))

    def add(kind, when, terms):
        @pl.when(when)
        def _():
            outs[kind][0] += terms()

    for kind in ("over", "back"):
        if kind in kinds:
            outs[kind][0] = ins[kind][0] if kind in ins else jnp.zeros((B, 2 * B), F32)

    if in_thirds(local, devices):
        blocks = [
            start + u for (start, _), ref in zip(starts, piece_refs) for u in range(ref.shape[2] // B)
        ]
        plan = edge_plan([k for k in kinds if k in ("over", "back")], far, blocks, local, devices)
        for (kind, odd), found in plan.items():
            if not found:
                continue

            def terms(kind=kind, found=found):
                taken = [
                    (n, rows_at(edge_refs[name], columns[n] if at is None else slice(at, at + B)))
                    for n, name, at in found
                ]
                if kind == "over":
                    return against([edge for _, edge in taken], [last_rows(n) for n, _ in taken])
                return against(
                    [greens[n](0, B) for n, _ in taken],
                    [split(times(edge, sigmas[n])) for n, edge in taken],
                )

            add(kind, even if odd == 0 else jnp.logical_not(even), terms)
        return

    source_high = source >= middle

    def edge(near, column):
        return tuple(
            jnp.where(near, a, b)
            for a, b in zip(rows_at(edge_refs["even"], column), rows_at(edge_refs["odd"], column))
        )

    if "over" in kinds:
        add(
            "over",
            source_high != (pan + 1 >= middle),
            lambda: against(
                [edge(even, column) for column in columns],
                [last_rows(number) for number in range(len(columns))],
            ),
        )
    if "back" in kinds:
        add(
            "back",
            source_high == (pan >= middle),
            lambda: against(
                [green(0, B) for green in greens],
                [
                    split(times(edge(jnp.logical_not(even), column), sigma))
                    for sigma, column in zip(sigmas, columns)
                ],
            ),
        )


def panel(at, green, far, pieces, carry, edges, kinds, last, span=None):
    rows = green.shape[2]
    local = rows // B
    devices = lax.axis_size("pan")
    counts = {"diag": local, "upper": local - 1, "over": 1, "back": 1}
    kinds = tuple(kind for kind in kinds if counts[kind])
    vmem = pl.BlockSpec(memory_space=pltpu.VMEM)
    starts, many = [], 0
    for start, piece, *other in pieces:
        starts.append((start, other[0] if other else far))
        many += piece.shape[2] // B
    operands = [at, green] + [piece for _, piece, *_ in pieces]
    names = []
    if "over" in kinds or "back" in kinds:
        names = ["even", "odd"]
        if in_thirds(local, devices):
            blocks = [start + u for start, piece in pieces for u in range(piece.shape[2] // B)]
            plan = edge_plan([k for k in kinds if k in ("over", "back")], far, blocks, local, devices)
            names = sorted({name for found in plan.values() for _, name, _ in found})
        operands += [edges[name] for name in names]
    shapes = {kind: jax.ShapeDtypeStruct((counts[kind], B, 2 * B), F32) for kind in kinds}
    aliases = {}
    first = []
    for number, kind in enumerate(kinds):
        if kind not in carry:
            first.append(kind)
            continue
        if not last or kind == "over":
            aliases[len(operands)] = number
        operands.append(carry[kind])
    if last:
        tall = jax.ShapeDtypeStruct((2, 1, rows, B), F32)
        shapes["upper"] = tall
        if "diag" in kinds:
            shapes = {"diag": jax.ShapeDtypeStruct((2, 1, (span[1] - span[0]) * B, B), F32)}
    full = "diag" in kinds or "upper" in kinds
    work = 3 * 2 * (2 * B) * (2 * B) * many * (rows if full else B) * (1 + len(kinds))
    out = pl.pallas_call(
        functools.partial(
            panel_kernel,
            local,
            far,
            starts,
            kinds,
            names,
            first,
            last,
            span,
            devices,
            1.0 / math.sqrt(B),
        ),
        in_specs=[pl.BlockSpec(memory_space=pltpu.SMEM)] + [vmem] * (len(operands) - 1),
        out_specs=[vmem] * len(shapes),
        out_shape=list(shapes.values()),
        input_output_aliases=aliases,
        compiler_params=pltpu.CompilerParams(vmem_limit_bytes=VMEM_BYTES),
        cost_estimate=pl.CostEstimate(
            flops=work, bytes_accessed=8 * rows * B * many, transcendentals=0
        ),
    )(*operands)
    return dict(carry, **dict(zip(shapes, out)))


def scattered(fars, modes, row, size, shift_ref, at_ref, contact_ref, col_ref, row_ref, piece_refs):
    energy = at_ref[1]
    chosen = []
    for far in fars:
        apart = jnp.abs((energy ^ far) - energy)
        chosen.append([jnp.where(apart == shift_ref[m], 1.0, 0.0).astype(F32) for m in range(modes)])
    for start in range(0, size, B):
        rows = slice(row + start, row + start + B)
        outer = [col_ref[rows, m : m + 1] * row_ref[m : m + 1, rows] for m in range(modes)]
        values = [contact_ref[0, 0, rows], contact_ref[1, 0, rows]]
        for weights, ref in zip(chosen, piece_refs):
            weight = total(w * o for w, o in zip(weights, outer))
            values = [value + weight * ref[j, 0, start : start + B] for j, value in enumerate(values)]
        yield start, values


def phonon_kernel(fars, modes, row, size, *refs):
    out_ref = refs[-1]
    for start, values in scattered(fars, modes, row, size, *refs[:5], refs[5:-1]):
        for j in range(2):
            out_ref[j, 0, start : start + B] = values[j]


def phonon(shifts, at, contact, columns, lines, pieces, number, chunks):
    parts, energies, rows = contact.shape[:3]
    size = rows // chunks
    vmem = pl.BlockSpec(memory_space=pltpu.VMEM)
    smem = pl.BlockSpec(memory_space=pltpu.SMEM)
    return pl.pallas_call(
        functools.partial(
            phonon_kernel, [far for far, _ in pieces], shifts.shape[0], number * size, size
        ),
        in_specs=[smem, smem] + [vmem] * (3 + len(pieces)),
        out_specs=vmem,
        out_shape=jax.ShapeDtypeStruct((parts, energies, size, B), F32),
        compiler_params=pltpu.CompilerParams(vmem_limit_bytes=VMEM_BYTES),
        cost_estimate=pl.CostEstimate(
            flops=size * B * 20, bytes_accessed=8 * size * B * 5, transcendentals=0
        ),
    )(shifts, at, contact, columns, lines, *[piece for _, piece in pieces])


def ending_kernel(fars, modes, rows, size, scale, *refs):
    settings, refs = refs[:5], refs[5:]
    piece_refs, refs = refs[: len(fars)], refs[len(fars) :]
    row = rows - size
    done_refs, refs = refs[: row // size], refs[row // size :]
    diag_refs, refs = refs[: rows // size], refs[rows // size :]
    _, over_ref, above_ref, sigma_ref, upper_ref, diag_ref, held, tail, sems = refs
    copies = []

    def send(source, target):
        copies.append(pltpu.make_async_copy(source, target, sems.at[len(copies)]))
        copies[-1].start()

    for refs, target in ((done_refs, sigma_ref), (diag_refs, diag_ref)):
        for number, ref in enumerate(refs):
            send(ref, target.at[:, :, pl.ds(number * size, size)])
    for j in range(2):
        part = slice(j * B, (j + 1) * B)
        tail[j, 0] = (over_ref[0, :, part] + above_ref[0, :, part]).T * scale
    send(tail, upper_ref.at[:, :, pl.ds(rows - B, B)])
    for start, values in scattered(fars, modes, row, size, *settings, piece_refs):
        for j in range(2):
            held[j, 0, start : start + B] = values[j]
        send(held.at[:, :, pl.ds(start, B)], sigma_ref.at[:, :, pl.ds(row + start, B)])
    for copy in copies:
        copy.wait()


def ending(shifts, at, contact, columns, lines, pieces, done, diag, upper, over, above):
    parts, energies, rows = contact.shape[:3]
    size = rows // (len(done) + 1)
    vmem = pl.BlockSpec(memory_space=pltpu.VMEM)
    smem = pl.BlockSpec(memory_space=pltpu.SMEM)
    hbm = pl.BlockSpec(memory_space=pl.ANY)
    operands = [shifts, at, contact, columns, lines, *[piece for _, piece in pieces], *done, *diag]
    specs = [smem, smem] + [vmem] * (len(operands) - 2) + [hbm, vmem, vmem]
    return pl.pallas_call(
        functools.partial(ending_kernel, [far for far, _ in pieces], shifts.shape[0], rows, size, 1.0 / math.sqrt(B)),
        in_specs=specs,
        out_specs=[hbm] * 3,
        out_shape=[jax.ShapeDtypeStruct(contact.shape, F32)] * 3,
        input_output_aliases={len(operands): 1},
        scratch_shapes=[
            pltpu.VMEM((parts, energies, size, B), F32),
            pltpu.VMEM((parts, energies, B, B), F32),
            pltpu.SemaphoreType.DMA((len(done) + len(diag) + 1 + size // B,)),
        ],
        compiler_params=pltpu.CompilerParams(vmem_limit_bytes=VMEM_BYTES),
        cost_estimate=pl.CostEstimate(
            flops=size * B * 20, bytes_accessed=8 * size * B * 5, transcendentals=0
        ),
    )(*operands, upper, over, above)


def cut_kernel(contact_ref, *refs):
    outs, sems = refs[:-1], refs[-1]
    copies = []
    start = 0
    for number, ref in enumerate(outs):
        size = ref.shape[2]
        at = 0 if number == len(outs) - 1 else start
        start += size
        copies.append(
            pltpu.make_async_copy(contact_ref.at[:, :, pl.ds(at, size)], ref, sems.at[number])
        )
    for copy in copies:
        copy.start()
    for copy in copies:
        copy.wait()


def cut(contact, chunks):
    parts, energies, rows = contact.shape[:3]
    part = jax.ShapeDtypeStruct((parts, energies, rows // chunks, B), F32)
    vmem = pl.BlockSpec(memory_space=pltpu.VMEM)
    return pl.pallas_call(
        cut_kernel,
        in_specs=[pl.BlockSpec(memory_space=pltpu.HBM)],
        out_specs=[vmem] * (chunks + 1),
        out_shape=[part] * chunks + [jax.ShapeDtypeStruct(contact.shape, F32)],
        scratch_shapes=[pltpu.SemaphoreType.DMA((chunks + 1,))],
        compiler_params=pltpu.CompilerParams(vmem_limit_bytes=VMEM_BYTES),
        cost_estimate=pl.CostEstimate(
            flops=0, bytes_accessed=32 * rows * B, transcendentals=0
        ),
        name="cut",
    )(contact)


def edge_rows(retarded, pan):
    rows, columns = retarded.shape[2:]
    devices = lax.axis_size("pan")
    local = rows // B
    middle = devices // 2
    thirds = in_thirds(local, devices)
    even = pan % 2 == 0

    def take(row, column, size):
        return lax.dynamic_slice(retarded, (0, 0, row, column), (2, 1, B, size))

    found, cuts = {}, []
    for odd, name in ((0, "even"), (1, "odd")):
        up = pan % 2 == odd
        row = jnp.where(up, rows - B, 0)
        if odd or not thirds:
            up_start = (pan + 1 >= middle).astype(jnp.int32)
            down_start = (pan < middle).astype(jnp.int32)
            column = jnp.where(up, up_start, down_start) * (columns // 2)
            part = take(row, column, columns // 2)
        else:
            short = jnp.where(even, pan * rows + rows // 2, (pan - 1) * rows)
            long = jnp.where(even, pan + 1, pan ^ middle) * rows
            part = jnp.concatenate([take(row, short, rows // 2), take(row, long, rows)], axis=3)
        pairs = []
        for i in range(odd, devices - 1, 2):
            pairs += [(i, i + 1), (i + 1, i)]
        cuts.append(part)
        found[name] = lax.ppermute(part, "pan", pairs)
    if thirds:
        part = take(0, (pan ^ (devices - 1)) * rows, rows)
        cuts.append(part)
        found["late"] = swapped(part, "pan", 1)
    return found, cuts


def gathered(near, chunks):
    size = chunks[0].shape[2] // B
    parts = [(i * size, chunk) for i, chunk in enumerate(chunks)]
    first = lax.axis_size("pan") // 2
    pieces = [(0, near)]
    bit = first
    while bit:
        found = []
        for far, piece in pieces:
            if bit == first:
                piece = parts
            sent = []
            for start, block in piece:
                sent.append((start, swapped(block, "pan", bit)))
            found.append((far ^ bit, sent))
        pieces += found
        bit //= 2
    return pieces


def body(retarded, contact, atom_kind, coupling, shifts):
    rows = retarded.shape[2]
    local = rows // B
    chunks = 2 if local % 2 == 0 else 1
    high = lax.axis_size("pan") // 2
    pan = lax.axis_index("pan").astype(jnp.int32)
    energy = lax.axis_index("en").astype(jnp.int32)
    at = jnp.where(jnp.arange(2, dtype=jnp.int32) == 0, pan, energy)
    atoms = rows // ORB
    kinds = lax.dynamic_slice_in_dim(atom_kind, pan * atoms, atoms, 0)
    per_atom = sum(jnp.where(kinds[:, None] == kind, coupling[kind][None, :], 0.0) for kind in range(coupling.shape[0]))
    per_row = jnp.repeat(per_atom, ORB, axis=0)
    per_line = jnp.repeat(per_atom.T, ORB, axis=1)
    edges, cuts = edge_rows(retarded, pan)
    *parts, copied = cut(contact, chunks)
    near = [(0, contact)]
    for rounds in range(ITERS):
        final = rounds == ITERS - 1
        pieces = gathered(near, parts)
        if rounds == 0:
            ready = lax.optimization_barrier((copied, per_row, per_line, *cuts))
            pieces[0] = (0, [(0, ready[0])])
            copied, per_row, per_line = ready[:3]
        groups = [(far, 0, blocks) for far, blocks in pieces[:-1]]
        groups.sort(key=lambda group: (group[0] != 0, group[0] >= high))
        if chunks > 1 and high > 1:
            far, _, blocks = groups.pop([far for far, _, _ in groups].index(high))
            groups.insert(1, (far, 0, blocks[:1]))
            groups.append((far, 1, blocks[1:]))
            for place, (near_far, _, blocks) in enumerate(groups):
                if near_far == 1 and len(blocks) > 1:
                    groups[place] = (1, 0, blocks[:1])
                    groups.append((1, 1, blocks[1:]))
                    break
        joined = []
        if not final and chunks > 1 and high > 1:
            far, _, blocks = groups.pop()
            joined = [(start, block, far) for start, block in blocks]
        sums = {}
        for far, number, blocks in groups:
            work = ("diag", "upper") if final else ("diag",)
            if final and 0 < far < high:
                if "over" not in sums:
                    sums = panel(at, retarded, 0, pieces[0][1], sums, edges, ("over", "back"), False)
                work += ("over", "back")
            sums = panel(at, retarded, far, blocks, sums, edges, work, False)
        far, blocks = pieces[-1]
        for block in blocks[:-1]:
            work = ("diag", "upper", "over") if final else ("diag",)
            sums = panel(at, retarded, far, [block, *joined], sums, edges, work, False)
            joined = []
        diags = []
        for number in range(chunks):
            span = (number * local // chunks, (number + 1) * local // chunks)
            made = panel(at, retarded, far, blocks[-1:], sums, edges, ("diag",), True, span)
            diags.append(made["diag"])
        found = spread(diags, "en")
        settings = (shifts, at, copied, per_row, per_line)
        if not final:
            parts = [phonon(*settings, own[1:], number, chunks) for number, own in enumerate(found)]
            near = [(i * (local // chunks), part) for i, part in enumerate(parts)]
    devices = lax.axis_size("pan")
    above = lax.ppermute(sums["back"], "pan", [(i + 1, i) for i in range(devices - 1)])
    far, blocks = pieces[-1]
    sums = panel(at, retarded, far, blocks[-1:], sums, edges, ("upper", "over"), True)
    for far, blocks in pieces[1:-1]:
        if far >= high:
            sums = panel(at, retarded, far, blocks, sums, edges, ("over",), False)
    done = [phonon(*settings, own[1:], number, chunks) for number, own in enumerate(found[:-1])]
    sigma, upper, diag = ending(*settings, found[-1][1:], done, diags, sums["upper"], sums["over"], above)
    return (diag, upper, sigma)


def solution(mesh):
    def step(retarded, *args):
        spread_spec = P(None, ("grp", "en"), "pan", None)
        inner = jax.shard_map(
            body,
            mesh=mesh,
            in_specs=(spread_spec, spread_spec, P(), P(), P()),
            out_specs=(spread_spec, spread_spec, spread_spec),
            check_vma=False,
        )
        return inner(retarded, *args)

    return step
```
